32 devices in a mesh: grp: 4 (over x, core), tile: 8 (over z, y).
Axes of the slice: x: 2, y: 2, z: 4, core: 2. Of those that a mesh axis runs over, the one named last changes fastest.
Arguments:
- start_field: float32 [512, 128, 512], P('grp', 'tile'), may hold values from -4 to 4
- class_ids: int32 [128, 512], P('tile'), may hold values from 0 to 7
- run_levels: int32 [512, 8], replicated, may hold values from 0 to 7
- steepness: float32 [512], replicated, may hold values from 0.1 to 1
- step_pick: int32 [512], replicated, may hold values from 1 to 4
- input_layer: float32 [69, 2048], replicated, may hold values from -2 to 2
- output_layer: bfloat16 [2048, 65536], P(None, ('grp', 'tile')), may hold values from -0.125 to 0.125
- output_bias: float32 [65536], P(('grp', 'tile')), may hold values from -1.5 to 1.5
Outputs:
- misfit: bfloat16 [512, 65536], P(None, ('grp', 'tile'))
- output_next: bfloat16 [2048, 65536], P(None, ('grp', 'tile'))
- bias_next: float32 [65536], P(('grp', 'tile'))
- input_next: float32 [69, 2048], replicated
The draws below stay inside these ranges and needn't reach their ends.
All inputs are finite; a program needn't handle non-finite values.
Results may differ from the reference program's by a relative error of at most 0.0029.
The reference program's roundings to bfloat16 on the way (of `hidden` and `slope`) count: a program that leaves them out, or rounds other values in their place, can miss the bound.
Values sent between devices are 32-bit elements; how exact they have to be, the bound alone decides.
No kernel may reach another device: no remote copies, remote signals or barrier semaphores. Data moves between devices by JAX's collectives and lax.ppermute only.
A program may use at most 128 MiB of HBM per device.

```python
import math
import jax
import jax.numpy as jnp
from jax import lax

GY = 512
STEPS = 4
HID = 2048
NCLASS = 8
LEVELS = 8
RUNS = 512
GX = 128
CELLS = 65536
CS = 2048
FEAT = 69
N_GRP = 4
N_TILE = 8
DEVICES = 32


def set_ends(result, stream_key, smallest, largest):
    dims = result.shape
    place = [jax.random.randint(jax.random.fold_in(stream_key, axis), (), 0, dims[axis]) for axis in range(len(dims))]
    result = result.at[tuple(place)].set(smallest)
    longest = dims.index(max(dims))
    place[longest] = (place[longest] + 1) % dims[longest]
    return result.at[tuple(place)].set(largest)


def levels(key, extent, pieces, low, largest):
    level, own = 1.0, jax.random.fold_in(key, 6)
    for axis_at, shards_of in pieces:
        heights = jnp.exp(jax.random.uniform(jax.random.fold_in(own, axis_at), (shards_of,), jnp.float32, low / len(pieces), largest / len(pieces)))
        level = level * jnp.repeat(heights, extent[axis_at] // shards_of).reshape([-1 if axis == axis_at else 1 for axis in range(len(extent))])
    return level


def noise(key, dims, deviation, most, cuts=(), held_as=jnp.bfloat16):
    factor_of = levels(key, dims, cuts, -0.22, 0.18) if cuts else 1.0
    values = jax.random.normal(key, dims, jnp.float32) * deviation * factor_of
    return jnp.minimum(jnp.maximum(values, -most), most).astype(held_as)


def setup_inputs(seed: int = 0) -> dict:
    key_list = jax.random.split(jax.random.key(seed), 9)
    start_field = noise(key_list[0], (RUNS, GX, GY), 1.0, 4.0, ((0, 4), (1, 8)), jnp.float32)
    class_ids = set_ends(jax.random.randint(key_list[1], (GX, GY), 0, NCLASS), jax.random.fold_in(key_list[1], 1), 0, NCLASS - 1).astype(jnp.int32)
    run_levels = set_ends(jax.random.randint(key_list[2], (RUNS, NCLASS), 0, LEVELS), jax.random.fold_in(key_list[2], 1), 0, LEVELS - 1).astype(jnp.int32)
    steepness = jnp.clip(jnp.exp(jax.random.uniform(key_list[3], (RUNS,), jnp.float32, math.log(0.1), math.log(1.0))), 0.1, 1.0)
    step_pick = set_ends(jax.random.randint(key_list[4], (RUNS,), 1, STEPS + 1), jax.random.fold_in(key_list[4], 1), 1, STEPS).astype(jnp.int32)
    input_layer = noise(key_list[5], (FEAT, HID), (NCLASS + 2) ** -0.5, 2.0, (), jnp.float32)
    output_layer = noise(key_list[6], (HID, CELLS), HID ** -0.5, 0.125, ((1, 32),))
    output_bias = noise(key_list[7], (CELLS,), 0.3, 1.5, ((0, 32),), jnp.float32)
    return dict(start_field=start_field, class_ids=class_ids, run_levels=run_levels, steepness=steepness, step_pick=step_pick, input_layer=input_layer, output_layer=output_layer, output_bias=output_bias)


def coefficients(run_levels, class_ids):
    table = 0.03 * jnp.exp(run_levels.astype(jnp.float32) * jnp.log(jnp.float32(1.35)))
    kappa = jnp.zeros((run_levels.shape[0],) + class_ids.shape, jnp.float32)
    for klass in range(run_levels.shape[1]):
        picked = jnp.where(class_ids == klass, 1.0, 0.0).astype(jnp.float32)
        kappa = kappa + picked[None] * table[:, klass][:, None, None]
    return kappa


def advance(field, kappa, steep):
    ratio = field * field
    spread = kappa * (1.0 + steep * ratio) / (1.0 + ratio)
    fpad = jnp.pad(field, ((0, 0), (0, 0), (1, 1)))
    spad = jnp.pad(spread, ((0, 0), (0, 0), (1, 1)))
    centre = field[:, 1:-1]
    middle = spread[:, 1:-1]
    total = centre + 0.5 * (middle + spread[:, :-2]) * (field[:, :-2] - centre)
    total = total + 0.5 * (middle + spread[:, 2:]) * (field[:, 2:] - centre)
    total = total + 0.5 * (middle + spad[:, 1:-1, :-2]) * (fpad[:, 1:-1, :-2] - centre)
    total = total + 0.5 * (middle + spad[:, 1:-1, 2:]) * (fpad[:, 1:-1, 2:] - centre)
    return total


def features(run_levels, step_pick, steepness):
    count = run_levels.shape[0]
    onehot = (run_levels[:, :, None] == jnp.arange(LEVELS, dtype=jnp.int32)[None, None, :]).astype(jnp.float32)
    onehot = onehot.reshape(count, -1)
    moment = (step_pick[:, None] == jnp.arange(1, STEPS + 1, dtype=jnp.int32)[None, :]).astype(jnp.float32)
    return jnp.concatenate([onehot, moment, steepness[:, None]], axis=1)


def dsilu(pre):
    logistic = jax.nn.sigmoid(pre)
    return logistic * (1.0 + pre * (1.0 - logistic))


def reference(start_field, class_ids, run_levels, steepness, step_pick, input_layer, output_layer, output_bias):
    kappa = coefficients(run_levels, class_ids)
    kappa_pad = jnp.pad(kappa, ((0, 0), (1, 1), (0, 0)))
    steep = steepness[:, None, None]
    field = start_field
    snapshot = jnp.zeros_like(start_field)
    for step in range(STEPS):
        wide = jnp.pad(field, ((0, 0), (1, 1), (0, 0)))
        field = advance(wide, kappa_pad, steep)
        snapshot = jnp.where(step_pick[:, None, None] == step + 1, field, snapshot)
    target = snapshot.reshape(RUNS, N_TILE, N_GRP, CS).transpose(2, 1, 0, 3).reshape(DEVICES, RUNS, CS)
    feats = features(run_levels, step_pick, steepness)
    pre = jnp.dot(feats, input_layer, precision=lax.Precision.HIGHEST)
    hidden = jax.nn.silu(pre).astype(jnp.bfloat16)
    weights = output_layer.reshape(HID, DEVICES, CS).transpose(1, 0, 2)
    biases = output_bias.reshape(DEVICES, CS)

    def learn_block(back, blocks):
        weight, bias, goal = blocks
        error = jnp.dot(hidden, weight, preferred_element_type=jnp.float32) + bias[None, :] - goal
        slope = (error * (2.0 / RUNS)).astype(jnp.bfloat16)
        grad = lax.dot_general(hidden, slope, (((0,), (0,)), ((), ())), preferred_element_type=jnp.float32)
        new_weight = (weight.astype(jnp.float32) - 0.5 * grad).astype(jnp.bfloat16)
        new_bias = bias - 0.5 * jnp.sum(slope.astype(jnp.float32), axis=0)
        back = back + lax.dot_general(slope, weight, (((1,), (1,)), ((), ())), preferred_element_type=jnp.float32)
        return back, (error.astype(jnp.bfloat16), new_weight, new_bias)

    back, outputs = lax.scan(learn_block, jnp.zeros((RUNS, HID), jnp.float32), (weights, biases, target))
    errors, new_weights, new_biases = outputs
    misfit = errors.transpose(1, 0, 2).reshape(RUNS, CELLS)
    output_next = new_weights.transpose(1, 0, 2).reshape(HID, CELLS)
    bias_next = new_biases.reshape(CELLS)
    slope_in = back * dsilu(pre)
    grad_in = lax.dot_general(feats, slope_in, (((0,), (0,)), ((), ())), precision=lax.Precision.HIGHEST)
    input_next = input_layer - 2.0 * grad_in
    return misfit, output_next, bias_next, input_next
```

```python
import functools

import jax
import jax.numpy as jnp
from jax import lax
from jax.experimental import pallas as pl
from jax.experimental.pallas import tpu as pltpu
from jax.sharding import PartitionSpec as P


STEPS = 4
LEVELS = 8
LANES = 128
SUB = 8
CHUNKS = 2
F32 = jnp.float32
BF16 = jnp.bfloat16
SPACE = pl.BlockSpec(memory_space=pltpu.VMEM)
ANY = pl.BlockSpec(memory_space=pl.ANY)


def cost(flops, nbytes, transcendentals=0):
    return pl.CostEstimate(
        flops=int(flops), bytes_accessed=int(nbytes), transcendentals=int(transcendentals)
    )


def spans(cols, chunks):
    width = cols // chunks
    out = []
    for c in range(chunks):
        low = max(c * width - SUB, 0)
        high = min((c + 1) * width + SUB, cols)
        sent = 0 if c == 0 else c * width + SUB
        out.append((low, high, sent))
    return out


def pack_kernel(parts, field_ref, ids_ref, *outs):
    rows, cols = ids_ref.shape
    for side in range(2):
        for r in range(STEPS):
            row = r if side == 0 else rows - STEPS + r
            for j in range(cols // LANES):
                tile = jnp.transpose(field_ref[:, row, j * LANES : (j + 1) * LANES])
                for c, (_, high, sent) in enumerate(parts):
                    first, last = max(sent, j * LANES), min(high, (j + 1) * LANES)
                    if first < last:
                        at = r * (high - sent) + first - sent
                        outs[2 * c + side][at : at + last - first, :] = tile[
                            first - j * LANES : last - j * LANES, :
                        ]
                at = STEPS * (parts[0][1] - parts[0][2]) + r * (cols // LANES) + j
                outs[side][at : at + 1, :] = ids_ref[
                    row : row + 1, j * LANES : (j + 1) * LANES
                ].astype(F32)


def pack_edges(start_field, ids, parts):
    runs, rows, cols = start_field.shape
    shapes = []
    for c, (_, high, sent) in enumerate(parts):
        extra = STEPS * cols // LANES if c == 0 else 0
        shapes += [jax.ShapeDtypeStruct((STEPS * (high - sent) + extra, runs), F32)] * 2
    return pl.pallas_call(
        functools.partial(pack_kernel, parts),
        in_specs=[SPACE, SPACE],
        out_specs=[SPACE] * len(shapes),
        out_shape=shapes,
        cost_estimate=cost(0, 6 * runs * rows * cols),
        name="pack_edges",
    )(start_field, ids)


def diffuse_kernel(chunk, chunks, ends_ref, field_ref, ids_ref, runs_ref, *refs):
    edges, (out_ref, raw_ref, u0_ref, u1_ref, d_ref, a_ref, b_ref, fx_ref, v_ref, sem) = (
        refs[:-10],
        refs[-10:],
    )
    cols = ids_ref.shape[2]
    rows = field_ref.shape[1]
    total = rows + 2 * STEPS
    parts = spans(cols, chunks)
    low, high, sent = parts[chunk]
    width = high - low
    own = cols // chunks
    tile0, tile1 = low // LANES, -(-high // LANES)
    copy = pltpu.make_async_copy(field_ref.at[:, :, tile0 * LANES : tile1 * LANES], raw_ref, sem)
    copy.start()

    level, pick, steep = runs_ref[0:LEVELS], runs_ref[LEVELS : LEVELS + 1], runs_ref[LEVELS + 1 : LEVELS + 2]
    table = 0.03 * jnp.exp(level * jnp.log(F32(1.35)))
    both = jnp.concatenate([table * (0.5 * steep), table * (0.5 * (1.0 - steep))], axis=1)
    pieces = []
    for _ in range(3):
        piece = both.astype(BF16).astype(F32)
        pieces.append(piece)
        both = both - piece
    pieces.append(jnp.zeros_like(both))
    tables = jnp.concatenate(pieces, axis=0).astype(BF16)
    klass = lax.broadcasted_iota(jnp.int32, (4 * LEVELS, LANES), 0) % LEVELS
    pick8 = jnp.broadcast_to(pick, (SUB, LANES))
    has_top, has_bottom = ends_ref[0], ends_ref[1]
    zeros = jnp.zeros((SUB, LANES), F32)

    def inside(r):
        return jnp.where(r < STEPS, has_top, jnp.where(r >= total - STEPS, has_bottom, 1.0))

    def coefficients(r, carry):
        valid = inside(r)
        ids = ids_ref[r]
        for j in range(tile0, tile1):
            here = jnp.broadcast_to(ids[:, j * LANES : (j + 1) * LANES], klass.shape)
            onehot = jnp.where(here == klass, valid, 0.0)
            ab = lax.dot_general(
                onehot.astype(BF16), tables, (((0,), (0,)), ((), ())), preferred_element_type=F32
            )
            first, last = max(low, j * LANES), min(high, (j + 1) * LANES)
            at, of = slice(first - low, last - low), slice(first - j * LANES, last - j * LANES)
            a_ref[r, at, :] = ab[of, :LANES]
            b_ref[r, at, :] = ab[of, LANES:]
        for ref in (u0_ref, u1_ref, d_ref):
            ref[r, 0:SUB, :] = zeros
            ref[r, SUB + width : 2 * SUB + width, :] = zeros
        return carry

    lax.fori_loop(0, total, coefficients, 0, unroll=4)

    for side in range(2):
        here = edges[side]
        for r in range(STEPS):
            row = r if side == 0 else total - STEPS + r
            n = high - sent
            at = SUB + sent - low
            u0_ref[row, at : at + n, :] = here[r * n : (r + 1) * n, :]
            if chunk:
                prior = edges[2 + side]
                n0 = parts[chunk - 1][1] - parts[chunk - 1][2]
                m = sent - low
                u0_ref[row, SUB : SUB + m, :] = prior[(r + 1) * n0 - m : (r + 1) * n0, :]
    copy.wait()
    for i in range(rows):
        for j in range(tile0, tile1):
            tile = jnp.transpose(raw_ref[:, i, (j - tile0) * LANES : (j - tile0 + 1) * LANES])
            first, last = max(low, j * LANES), min(high, (j + 1) * LANES)
            at = SUB + first - low
            u0_ref[STEPS + i, at : at + last - first, :] = tile[first - j * LANES : last - j * LANES, :]

    blocks = range(width // SUB)
    for step in range(1, STEPS + 1):
        src, dst = (u0_ref, u1_ref) if step % 2 else (u1_ref, u0_ref)

        def conduct(r, k, u, src=src):
            at = slice(k * SUB, (k + 1) * SUB)
            d = a_ref[r, at, :] + b_ref[r, at, :] * (1.0 / (1.0 + u * u))
            d_ref[r, SUB + k * SUB : 2 * SUB + k * SUB, :] = d
            return d

        top = step - 1
        for k in blocks:
            at = slice(SUB + k * SUB, 2 * SUB + k * SUB)
            u, un = src[top, at, :], src[top + 1, at, :]
            d, dn = conduct(top, k, u), conduct(top + 1, k, un)
            v_ref[k * SUB : (k + 1) * SUB, :] = (d + dn) * (un - u)

        def advance(r, carry, src=src, dst=dst, step=step, conduct=conduct):
            for k in range(-1, width // SUB):
                p = SUB + k * SUB
                flux = (d_ref[r, p : p + SUB, :] + d_ref[r, p + 1 : p + 1 + SUB, :]) * (
                    src[r, p + 1 : p + 1 + SUB, :] - src[r, p : p + SUB, :]
                )
                fx_ref[p : p + SUB, :] = flux
            active = pick8 >= jnp.where(inside(r) > 0.0, F32(step), F32(2 * STEPS))
            for k in blocks:
                p = SUB + k * SUB
                at = slice(k * SUB, (k + 1) * SUB)
                u, un = src[r, p : p + SUB, :], src[r + 1, p : p + SUB, :]
                d = d_ref[r, p : p + SUB, :]
                dn = conduct(r + 1, k, un)
                down = (d + dn) * (un - u)
                across = fx_ref[p : p + SUB, :] - fx_ref[p - 1 : p - 1 + SUB, :]
                new = u + across + (down - v_ref[at, :])
                v_ref[at, :] = down
                dst[r, p : p + SUB, :] = jnp.where(active, new, u)
            return carry

        lax.fori_loop(step, total - step, advance, 0)

    result = u0_ref if STEPS % 2 == 0 else u1_ref
    per_block = rows // out_ref.shape[0]
    for i in range(rows):
        for j in range(own // LANES):
            p = SUB + chunk * own + j * LANES - low
            at = (i % per_block) * own + j * LANES
            out_ref[i // per_block, :, at : at + LANES] = jnp.transpose(
                result[STEPS + i, p : p + LANES, :]
            )


def diffuse(chunk, chunks, start_field, edges, ids_wide, run_rows, ends, blocks):
    runs, rows, cols = start_field.shape
    total = rows + 2 * STEPS
    low, high, _ = spans(cols, chunks)[chunk]
    width = high - low
    tiles = -(-high // LANES) - low // LANES
    own = cols // chunks
    edges = list(edges[chunk]) + (list(edges[chunk - 1]) if chunk else [])
    state = pltpu.VMEM((total, width + 2 * SUB, runs), F32)
    return pl.pallas_call(
        functools.partial(diffuse_kernel, chunk, chunks),
        in_specs=[pl.BlockSpec(memory_space=pltpu.SMEM), ANY, SPACE, SPACE] + [SPACE] * len(edges),
        out_specs=SPACE,
        out_shape=jax.ShapeDtypeStruct((blocks, runs, rows * own // blocks), F32),
        scratch_shapes=[
            pltpu.VMEM((runs, rows, tiles * LANES), F32),
            state,
            state,
            state,
            pltpu.VMEM((total, width, runs), F32),
            pltpu.VMEM((total, width, runs), F32),
            pltpu.VMEM((width + 2 * SUB, runs), F32),
            pltpu.VMEM((width, runs), F32),
            pltpu.SemaphoreType.DMA,
        ],
        cost_estimate=cost(100 * runs * total * width, 12 * runs * total * width),
        name="diffuse",
    )(ends, start_field, ids_wide, run_rows, *edges)


PITCH = 80


def hidden_kernel(
    runs_ref, layer_ref, hidden_ref, hidden_t_ref, gain_t_ref, project_ref, f_ref, ft_ref, rest_ref, stack_ref
):
    depth, runs = ft_ref.shape
    n_feat, block = layer_ref.shape
    n_exact = n_feat - 1
    steep = runs_ref[LEVELS + 1 : LEVELS + 2]
    rest = steep - steep.astype(BF16).astype(F32)

    @pl.when(pl.program_id(0) == 0)
    def _():
        held = runs_ref[...]
        row = lax.broadcasted_iota(jnp.int32, (depth, held.shape[0]), 0)
        col = lax.broadcasted_iota(jnp.int32, (depth, held.shape[0]), 1)

        def place(row):
            return jnp.where(row < 3 * PITCH, row % PITCH, PITCH)

        n_level = LEVELS * LEVELS
        at = place(row)
        source = jnp.where(
            at < n_level,
            at // LEVELS,
            jnp.where(at < n_exact, LEVELS, jnp.where(at == n_exact, LEVELS + 1, -1)),
        )
        spread = jnp.where(col == source, 1.0, 0.0).astype(BF16)
        value = jnp.dot(spread, held.astype(BF16), preferred_element_type=F32)
        at = place(lax.broadcasted_iota(jnp.int32, (depth, runs), 0))
        wanted = jnp.where(at < n_level, at % LEVELS, at - n_level + 1).astype(F32)
        feats = jnp.where(at < n_exact, jnp.where(value == wanted, 1.0, 0.0), value)
        ft_ref[...] = feats.astype(BF16)
        f_ref[...] = jnp.transpose(feats).astype(BF16)
        line = lax.broadcasted_iota(jnp.int32, (LANES, runs), 0)
        wide_rest = jnp.broadcast_to(rest, (LANES, runs))
        project = jnp.where(
            line < n_feat, feats[:LANES], jnp.where(line == n_feat, wide_rest, 0.0)
        )
        project_ref[...] = jnp.transpose(project).astype(BF16)
        rest_ref[...] = jnp.transpose(wide_rest)
        stack_ref[...] = jnp.zeros(stack_ref.shape, F32)

    layer = layer_ref[...]
    left = layer
    for piece in range(3):
        part = left.astype(BF16).astype(F32)
        stack_ref[piece * PITCH : piece * PITCH + n_feat, :] = part
        left = left - part
    stack = stack_ref[...]
    column = jnp.concatenate([rest_ref[...]] * (block // LANES), axis=1)
    pre = jnp.dot(f_ref[...], stack.astype(BF16), preferred_element_type=F32)
    pre = pre + column * layer[n_exact:n_feat, :]
    hidden_ref[...] = (pre * jax.nn.sigmoid(pre)).astype(BF16)
    stack_t = jnp.transpose(stack)
    last = sum(stack_t[:, p * PITCH + n_exact : p * PITCH + n_feat] for p in range(3))
    pre = jnp.dot(stack_t.astype(BF16), ft_ref[...], preferred_element_type=F32)
    pre = pre + last * rest
    logistic = jax.nn.sigmoid(pre)
    hidden_t_ref[...] = (pre * logistic).astype(BF16)
    gain_t_ref[...] = logistic * (1.0 + pre * (1.0 - logistic))


def hidden_units(run_rows, layer, block=512):
    held, runs = run_rows.shape
    n_feat, hid = layer.shape
    depth = -(-3 * PITCH // LANES) * LANES
    return pl.pallas_call(
        hidden_kernel,
        grid=(hid // block,),
        in_specs=[
            pl.BlockSpec((held, runs), lambda i: (0, 0)),
            pl.BlockSpec((n_feat, block), lambda i: (0, i)),
        ],
        out_specs=[
            pl.BlockSpec((runs, block), lambda i: (0, i)),
            pl.BlockSpec((block, runs), lambda i: (i, 0)),
            pl.BlockSpec((block, runs), lambda i: (i, 0)),
            pl.BlockSpec((runs, LANES), lambda i: (0, 0)),
        ],
        out_shape=[
            jax.ShapeDtypeStruct((runs, hid), BF16),
            jax.ShapeDtypeStruct((hid, runs), BF16),
            jax.ShapeDtypeStruct((hid, runs), F32),
            jax.ShapeDtypeStruct((runs, LANES), BF16),
        ],
        scratch_shapes=[
            pltpu.VMEM((runs, depth), BF16),
            pltpu.VMEM((depth, runs), BF16),
            pltpu.VMEM((runs, LANES), F32),
            pltpu.VMEM((depth, block), F32),
        ],
        cost_estimate=cost(4 * runs * hid * depth, 10 * runs * hid, 4 * runs * hid),
        name="hidden_units",
    )(run_rows, layer)


def predict_kernel(hidden_ref, weight_ref, bias_ref, out_ref):
    out_ref[...] = (
        jnp.dot(hidden_ref[...], weight_ref[...], preferred_element_type=F32) + bias_ref[...]
    )


def predict(hidden, weight, bias, block=512):
    runs, hid = hidden.shape
    cells = weight.shape[1]
    return pl.pallas_call(
        predict_kernel,
        grid=(cells // block,),
        in_specs=[
            pl.BlockSpec((runs, hid), lambda i: (0, 0)),
            pl.BlockSpec((hid, block), lambda i: (0, i)),
            pl.BlockSpec((1, block), lambda i: (0, i)),
        ],
        out_specs=pl.BlockSpec((runs, block), lambda i: (0, i)),
        out_shape=jax.ShapeDtypeStruct((runs, cells), F32),
        cost_estimate=cost(2 * runs * hid * cells, 2 * hid * cells + 4 * runs * cells),
        name="predict",
    )(hidden, weight, bias)


def learn_kernel(last, has_before, scale, *refs):
    guess_ref, target_ref, weight_ref, bias_ref, gain_ref, feats_ref = refs[:6]
    rest = refs[6:]
    if has_before:
        acc_in_ref = rest[3]
        rest = rest[4:]
    misfit_ref, slope_ref, bias_out_ref, acc_ref, back_ref = rest
    sources, per_source, own = target_ref.shape
    step = pl.program_id(0)
    total = jnp.zeros((1, own), F32)
    for s in range(sources):
        at = slice(s * per_source, (s + 1) * per_source)
        error = guess_ref[at, :] - target_ref[s]
        misfit_ref[at, :] = error.astype(BF16)
        slope = (error * scale).astype(BF16)
        slope_ref[at, :] = slope
        total = total + jnp.sum(slope.astype(F32), axis=0, keepdims=True)
    bias_out_ref[...] = bias_ref[...] - 0.5 * total
    back = lax.dot_general(
        weight_ref[...], slope_ref[...], (((1,), (1,)), ((), ())), preferred_element_type=F32
    )

    @pl.when(step == 0)
    def _():
        back_ref[...] = back

    @pl.when(step > 0)
    def _():
        back_ref[...] += back

    @pl.when(step == pl.num_programs(0) - 1)
    def _():
        full = back_ref[...] * gain_ref[...]
        high = full.astype(BF16)
        low = (full - high.astype(F32)).astype(BF16)
        feats = feats_ref[...]
        acc = jnp.dot(high, feats, preferred_element_type=F32)
        acc = acc + jnp.dot(low, feats, preferred_element_type=F32)
        if has_before:
            acc = acc + acc_in_ref[...]
        if last:
            acc_ref[...] = jnp.transpose(acc)[: acc_ref.shape[0], :]
        else:
            acc_ref[...] = acc


def learn_chunk(chunk, chunks, cols, guess, target, weight, bias, gain_t, feats, before, kept, scale):
    hid, cells = weight.shape
    sources, per_source, mine = target.shape
    runs = sources * per_source
    own = cols // chunks
    last, has_before = chunk == chunks - 1, before is not None
    strip = lambda i: (0, i * chunks + chunk)
    in_specs = [
        pl.BlockSpec((runs, own), strip),
        pl.BlockSpec((sources, per_source, own), lambda i: (0, 0, i)),
        pl.BlockSpec((hid, own), strip),
        pl.BlockSpec((1, own), strip),
        SPACE,
        SPACE,
    ]
    args = [guess, target, weight, bias, gain_t, feats]
    aliases = {}
    if has_before:
        in_specs += [ANY, ANY, ANY, SPACE]
        args += list(before)
        aliases = {6: 0, 7: 1, 8: 2}
    acc_shape = (kept, hid) if last else (hid, LANES)
    return pl.pallas_call(
        functools.partial(learn_kernel, last, has_before, scale),
        grid=(mine // own,),
        in_specs=in_specs,
        out_specs=[
            pl.BlockSpec((runs, own), strip),
            pl.BlockSpec((runs, own), strip),
            pl.BlockSpec((1, own), strip),
            pl.BlockSpec(acc_shape, lambda i: (0, 0)),
        ],
        out_shape=[
            jax.ShapeDtypeStruct((runs, cells), BF16),
            jax.ShapeDtypeStruct((runs, cells), BF16),
            jax.ShapeDtypeStruct((1, cells), F32),
            jax.ShapeDtypeStruct(acc_shape, F32),
        ],
        scratch_shapes=[pltpu.VMEM((hid, runs), F32)],
        input_output_aliases=aliases,
        cost_estimate=cost(2 * runs * hid * (mine + 2 * LANES), 2 * hid * mine + 12 * runs * mine),
        name="learn",
    )(*args)


def update_kernel(hidden_t_ref, slope_ref, weight_ref, out_ref):
    grad = jnp.dot(hidden_t_ref[...], slope_ref[...], preferred_element_type=F32)
    out_ref[...] = (weight_ref[...].astype(F32) - 0.5 * grad).astype(BF16)


def update(hidden_t, slope, weight, block=256):
    hid, cells = weight.shape
    runs = slope.shape[0]
    return pl.pallas_call(
        update_kernel,
        grid=(hid // block,),
        in_specs=[
            pl.BlockSpec((block, runs), lambda i: (i, 0)),
            pl.BlockSpec((runs, cells), lambda i: (0, 0)),
            pl.BlockSpec((block, cells), lambda i: (i, 0)),
        ],
        out_specs=pl.BlockSpec((block, cells), lambda i: (i, 0)),
        out_shape=jax.ShapeDtypeStruct((hid, cells), BF16),
        cost_estimate=cost(2 * runs * hid * cells, 4 * hid * cells + 4 * runs * cells),
        name="update",
    )(hidden_t, slope, weight)


def halve(x, axis, bit):
    size = lax.axis_size(axis)
    upper = (lax.axis_index(axis) & bit) != 0
    half = x.shape[0] // 2
    kept = lax.dynamic_slice_in_dim(x, jnp.where(upper, half, 0), half, 0)
    sent = lax.dynamic_slice_in_dim(x, jnp.where(upper, 0, half), half, 0)
    return kept + lax.ppermute(sent, axis, [(i, i ^ bit) for i in range(size)])


def rejoin(x, axis, bit):
    size = lax.axis_size(axis)
    upper = (lax.axis_index(axis) & bit) != 0
    other = lax.ppermute(x, axis, [(i, i ^ bit) for i in range(size)])
    return jnp.where(
        upper, jnp.concatenate([other, x], axis=0), jnp.concatenate([x, other], axis=0)
    )


def sum_over_devices(x):
    grp, tile = lax.axis_size("grp"), lax.axis_size("tile")
    bits = [1 << b for b in range(grp.bit_length() - 1)]
    for bit in bits:
        x = halve(x, "grp", bit)
    n = x.shape[0] // tile
    x = lax.all_to_all(x.reshape(tile, n, LANES), "tile", 0, 0, tiled=True)
    x = jnp.sum(x.reshape(tile, n, LANES), axis=0)
    x = lax.all_to_all(jnp.broadcast_to(x[None], (tile, n, LANES)), "tile", 0, 0, tiled=True)
    x = x.reshape(tile * n, LANES)
    for bit in bits[::-1]:
        x = rejoin(x, "grp", bit)
    return x


def on_device(
    start_field, class_ids, run_levels, steepness, step_pick, input_layer, output_layer, output_bias
):
    local_runs, _, cols = start_field.shape
    n_grp, n_tile = lax.axis_size("grp"), lax.axis_size("tile")
    tile = lax.axis_index("tile")
    first_run = lax.axis_index("grp") * local_runs
    chunks = CHUNKS
    parts = spans(cols, chunks)
    runs_total, classes = run_levels.shape
    n_feat, hid = input_layer.shape

    up = [(i, i + 1) for i in range(n_tile - 1)]
    down = [(j, i) for i, j in up]
    packed = pack_edges(start_field, class_ids, parts)
    edges = []
    for c in range(chunks):
        top, bottom = packed[2 * c], packed[2 * c + 1]
        above = lax.ppermute(bottom, "tile", up)
        below = lax.ppermute(top, "tile", down)
        edges.append((above, below))

    run_rows = jnp.concatenate(
        [
            run_levels.T.astype(F32),
            step_pick[None, :].astype(F32),
            steepness[None, :],
            jnp.zeros((2 * LEVELS - classes - 2, runs_total), F32),
        ],
        axis=0,
    )
    run_rows_here = lax.dynamic_slice_in_dim(run_rows, first_run, local_runs, 1)
    ends = jnp.stack([(tile > 0).astype(F32), (tile < n_tile - 1).astype(F32)])
    brought = STEPS * (parts[0][1] - parts[0][2])
    ids_wide = jnp.concatenate(
        [
            edges[0][0][brought:].reshape(STEPS, cols).astype(jnp.int32),
            class_ids,
            edges[0][1][brought:].reshape(STEPS, cols).astype(jnp.int32),
        ],
        axis=0,
    )[:, None, :]

    hidden, hidden_t, gain_t, project = hidden_units(run_rows, input_layer)
    bias_row = output_bias[None, :]
    guess = predict(hidden, output_layer, bias_row)
    kept = -(-(n_feat + 1) // SUB) * SUB

    state = None
    scale = 2.0 / runs_total
    for c in range(chunks):
        snap = diffuse(c, chunks, start_field, edges, ids_wide, run_rows_here, ends, n_grp)
        target = lax.all_to_all(snap, "grp", split_axis=0, concat_axis=0, tiled=True)
        state = learn_chunk(
            c, chunks, cols, guess, target, output_layer, bias_row, gain_t, project, state, kept, scale
        )
    misfit, slope, bias_next, partial = state
    output_next = update(hidden_t, slope, output_layer)
    flat = partial.reshape(-1, LANES)
    unit = SUB * n_grp * n_tile
    padded = -(-flat.shape[0] // unit) * unit
    flat = jnp.pad(flat, ((0, padded - flat.shape[0]), (0, 0)))
    total = sum_over_devices(flat)[: kept * hid // LANES].reshape(kept, hid)
    grad_in = jnp.concatenate(
        [total[: n_feat - 1], total[n_feat - 1 : n_feat] + total[n_feat : n_feat + 1]], axis=0
    )
    input_next = input_layer - 2.0 * grad_in
    return misfit, output_next, bias_next.reshape(-1), input_next


def solution(mesh):
    in_specs = (
        P("grp", "tile", None),
        P("tile", None),
        P(),
        P(),
        P(),
        P(),
        P(None, ("grp", "tile")),
        P(("grp", "tile")),
    )
    out_specs = (P(None, ("grp", "tile")), P(None, ("grp", "tile")), P(("grp", "tile")), P())

    return jax.shard_map(
        on_device, mesh=mesh, in_specs=in_specs, out_specs=out_specs, check_vma=False
    )
```

```python
import functools

import jax
import jax.numpy as jnp
from jax import lax
from jax.experimental import pallas as pl
from jax.experimental.pallas import tpu as pltpu
from jax.sharding import PartitionSpec as P


STEPS = 4
LEVELS = 8
LANES = 128
SUB = 8
CHUNKS = 2
F32 = jnp.float32
BF16 = jnp.bfloat16
SPACE = pl.BlockSpec(memory_space=pltpu.VMEM)
ANY = pl.BlockSpec(memory_space=pl.ANY)
SCALARS = pl.BlockSpec(memory_space=pltpu.SMEM)


def cost(flops, nbytes, transcendentals=0):
    return pl.CostEstimate(
        flops=int(flops), bytes_accessed=int(nbytes), transcendentals=int(transcendentals)
    )


def spans(cols, chunks):
    width = cols // chunks
    out = []
    for c in range(chunks):
        low = max(c * width - SUB, 0)
        high = min((c + 1) * width + SUB, cols)
        sent = 0 if c == 0 else c * width + SUB
        out.append((low, high, sent))
    return out


def pack_kernel(parts, field_ref, ids_ref, *outs):
    rows, cols = ids_ref.shape
    for side in range(2):
        for r in range(STEPS):
            row = r if side == 0 else rows - STEPS + r
            for j in range(cols // LANES):
                tile = jnp.transpose(field_ref[:, row, j * LANES : (j + 1) * LANES])
                for c, (_, high, sent) in enumerate(parts):
                    first, last = max(sent, j * LANES), min(high, (j + 1) * LANES)
                    if first < last:
                        at = r * (high - sent) + first - sent
                        outs[2 * c + side][at : at + last - first, :] = tile[
                            first - j * LANES : last - j * LANES, :
                        ]
                at = STEPS * (parts[0][1] - parts[0][2]) + r * (cols // LANES) + j
                outs[side][at : at + 1, :] = ids_ref[
                    row : row + 1, j * LANES : (j + 1) * LANES
                ].astype(F32)


def pack_edges(start_field, ids, parts):
    runs, rows, cols = start_field.shape
    shapes = []
    for c, (_, high, sent) in enumerate(parts):
        extra = STEPS * cols // LANES if c == 0 else 0
        shapes += [jax.ShapeDtypeStruct((STEPS * (high - sent) + extra, runs), F32)] * 2
    return pl.pallas_call(
        functools.partial(pack_kernel, parts),
        in_specs=[SPACE, SPACE],
        out_specs=[SPACE] * len(shapes),
        out_shape=shapes,
        cost_estimate=cost(0, 6 * runs * rows * cols),
        name="pack_edges",
    )(start_field, ids)


def diffuse_kernel(chunk, chunks, ends_ref, grp_ref, field_ref, ids_ref, runs_ref, *refs):
    edges, outs = refs[: 2 + 2 * (chunk > 0)], refs[2 + 2 * (chunk > 0) : -9]
    raw_ref, u0_ref, u1_ref, d_ref, a_ref, b_ref, fx_ref, v_ref, sem = refs[-9:]
    cols = ids_ref.shape[2]
    rows = field_ref.shape[1]
    total = rows + 2 * STEPS
    parts = spans(cols, chunks)
    low, high, sent = parts[chunk]
    width = high - low
    own = cols // chunks
    tile0, tile1 = low // LANES, -(-high // LANES)
    copy = pltpu.make_async_copy(field_ref.at[:, :, tile0 * LANES : tile1 * LANES], raw_ref, sem)
    copy.start()

    level, pick, steep = runs_ref[0:LEVELS], runs_ref[LEVELS : LEVELS + 1], runs_ref[LEVELS + 1 : LEVELS + 2]
    table = 0.03 * jnp.exp(level * jnp.log(F32(1.35)))
    both = jnp.concatenate([table * (0.5 * steep), table * (0.5 * (1.0 - steep))], axis=1)
    pieces = []
    for _ in range(3):
        piece = both.astype(BF16).astype(F32)
        pieces.append(piece)
        both = both - piece
    pieces.append(jnp.zeros_like(both))
    tables = jnp.concatenate(pieces, axis=0).astype(BF16)
    klass = lax.broadcasted_iota(jnp.int32, (4 * LEVELS, LANES), 0) % LEVELS
    pick8 = jnp.broadcast_to(pick, (SUB, LANES))
    has_top, has_bottom = ends_ref[0], ends_ref[1]
    zeros = jnp.zeros((SUB, LANES), F32)

    def inside(r):
        return jnp.where(r < STEPS, has_top, jnp.where(r >= total - STEPS, has_bottom, 1.0))

    def coefficients(r, carry):
        valid = inside(r)
        ids = ids_ref[r]
        for j in range(tile0, tile1):
            here = jnp.broadcast_to(ids[:, j * LANES : (j + 1) * LANES], klass.shape)
            onehot = jnp.where(here == klass, valid, 0.0)
            ab = lax.dot_general(
                onehot.astype(BF16), tables, (((0,), (0,)), ((), ())), preferred_element_type=F32
            )
            first, last = max(low, j * LANES), min(high, (j + 1) * LANES)
            at, of = slice(first - low, last - low), slice(first - j * LANES, last - j * LANES)
            a_ref[r, at, :] = ab[of, :LANES]
            b_ref[r, at, :] = ab[of, LANES:]
        for ref in (u0_ref, u1_ref, d_ref):
            ref[r, 0:SUB, :] = zeros
            ref[r, SUB + width : 2 * SUB + width, :] = zeros
        return carry

    lax.fori_loop(0, total, coefficients, 0, unroll=4)

    for side in range(2):
        here = edges[side]
        for r in range(STEPS):
            row = r if side == 0 else total - STEPS + r
            n = high - sent
            at = SUB + sent - low
            u0_ref[row, at : at + n, :] = here[r * n : (r + 1) * n, :]
            if chunk:
                prior = edges[2 + side]
                n0 = parts[chunk - 1][1] - parts[chunk - 1][2]
                m = sent - low
                u0_ref[row, SUB : SUB + m, :] = prior[(r + 1) * n0 - m : (r + 1) * n0, :]
    copy.wait()
    for i in range(rows):
        for j in range(tile0, tile1):
            tile = jnp.transpose(raw_ref[:, i, (j - tile0) * LANES : (j - tile0 + 1) * LANES])
            first, last = max(low, j * LANES), min(high, (j + 1) * LANES)
            at = SUB + first - low
            u0_ref[STEPS + i, at : at + last - first, :] = tile[first - j * LANES : last - j * LANES, :]

    blocks = range(width // SUB)
    for step in range(1, STEPS + 1):
        src, dst = (u0_ref, u1_ref) if step % 2 else (u1_ref, u0_ref)

        def conduct(r, k, u, src=src):
            at = slice(k * SUB, (k + 1) * SUB)
            d = a_ref[r, at, :] + b_ref[r, at, :] * (1.0 / (1.0 + u * u))
            d_ref[r, SUB + k * SUB : 2 * SUB + k * SUB, :] = d
            return d

        top = step - 1
        for k in blocks:
            at = slice(SUB + k * SUB, 2 * SUB + k * SUB)
            u, un = src[top, at, :], src[top + 1, at, :]
            d, dn = conduct(top, k, u), conduct(top + 1, k, un)
            v_ref[k * SUB : (k + 1) * SUB, :] = (d + dn) * (un - u)

        def advance(r, carry, src=src, dst=dst, step=step, conduct=conduct):
            for k in range(-1, width // SUB):
                p = SUB + k * SUB
                flux = (d_ref[r, p : p + SUB, :] + d_ref[r, p + 1 : p + 1 + SUB, :]) * (
                    src[r, p + 1 : p + 1 + SUB, :] - src[r, p : p + SUB, :]
                )
                fx_ref[p : p + SUB, :] = flux
            active = pick8 >= jnp.where(inside(r) > 0.0, F32(step), F32(2 * STEPS))
            for k in blocks:
                p = SUB + k * SUB
                at = slice(k * SUB, (k + 1) * SUB)
                u, un = src[r, p : p + SUB, :], src[r + 1, p : p + SUB, :]
                d = d_ref[r, p : p + SUB, :]
                dn = conduct(r + 1, k, un)
                down = (d + dn) * (un - u)
                across = fx_ref[p : p + SUB, :] - fx_ref[p - 1 : p - 1 + SUB, :]
                new = u + across + (down - v_ref[at, :])
                v_ref[at, :] = down
                dst[r, p : p + SUB, :] = jnp.where(active, new, u)
            return carry

        lax.fori_loop(step, total - step, advance, 0)

    result = u0_ref if STEPS % 2 == 0 else u1_ref
    per_block = rows // len(outs)
    for offset, out_ref in enumerate(outs):
        row = STEPS + (grp_ref[0] ^ offset) * per_block
        for i in range(per_block):
            for j in range(own // LANES):
                p = SUB + chunk * own + j * LANES - low
                at = i * own + j * LANES
                out_ref[:, at : at + LANES] = jnp.transpose(result[row + i, p : p + LANES, :])


def diffuse(chunk, chunks, start_field, edges, ids_wide, run_rows, ends, grp, blocks):
    runs, rows, cols = start_field.shape
    total = rows + 2 * STEPS
    low, high, _ = spans(cols, chunks)[chunk]
    width = high - low
    tiles = -(-high // LANES) - low // LANES
    own = cols // chunks
    edges = list(edges[chunk]) + (list(edges[chunk - 1]) if chunk else [])
    state = pltpu.VMEM((total, width + 2 * SUB, runs), F32)
    return pl.pallas_call(
        functools.partial(diffuse_kernel, chunk, chunks),
        in_specs=[SCALARS, SCALARS, ANY, SPACE, SPACE] + [SPACE] * len(edges),
        out_specs=[SPACE] * blocks,
        out_shape=[jax.ShapeDtypeStruct((runs, rows * own // blocks), F32)] * blocks,
        scratch_shapes=[
            pltpu.VMEM((runs, rows, tiles * LANES), F32),
            state,
            state,
            state,
            pltpu.VMEM((total, width, runs), F32),
            pltpu.VMEM((total, width, runs), F32),
            pltpu.VMEM((width + 2 * SUB, runs), F32),
            pltpu.VMEM((width, runs), F32),
            pltpu.SemaphoreType.DMA,
        ],
        cost_estimate=cost(100 * runs * total * width, 12 * runs * total * width),
        name="diffuse",
    )(ends, grp, start_field, ids_wide, run_rows, *edges)


PITCH = 80


def hidden_kernel(
    runs_ref, layer_ref, hidden_ref, hidden_t_ref, gain_t_ref, project_ref, f_ref, ft_ref, rest_ref, stack_ref
):
    depth, runs = ft_ref.shape
    n_feat, block = layer_ref.shape
    n_exact = n_feat - 1
    steep = runs_ref[LEVELS + 1 : LEVELS + 2]
    rest = steep - steep.astype(BF16).astype(F32)

    @pl.when(pl.program_id(0) == 0)
    def _():
        held = runs_ref[...]
        row = lax.broadcasted_iota(jnp.int32, (depth, held.shape[0]), 0)
        col = lax.broadcasted_iota(jnp.int32, (depth, held.shape[0]), 1)

        def place(row):
            return jnp.where(row < 3 * PITCH, row % PITCH, PITCH)

        n_level = LEVELS * LEVELS
        at = place(row)
        source = jnp.where(
            at < n_level,
            at // LEVELS,
            jnp.where(at < n_exact, LEVELS, jnp.where(at == n_exact, LEVELS + 1, -1)),
        )
        spread = jnp.where(col == source, 1.0, 0.0).astype(BF16)
        value = jnp.dot(spread, held.astype(BF16), preferred_element_type=F32)
        at = place(lax.broadcasted_iota(jnp.int32, (depth, runs), 0))
        wanted = jnp.where(at < n_level, at % LEVELS, at - n_level + 1).astype(F32)
        feats = jnp.where(at < n_exact, jnp.where(value == wanted, 1.0, 0.0), value)
        ft_ref[...] = feats.astype(BF16)
        f_ref[...] = jnp.transpose(feats).astype(BF16)
        line = lax.broadcasted_iota(jnp.int32, (LANES, runs), 0)
        wide_rest = jnp.broadcast_to(rest, (LANES, runs))
        project = jnp.where(
            line < n_feat, feats[:LANES], jnp.where(line == n_feat, wide_rest, 0.0)
        )
        project_ref[...] = jnp.transpose(project).astype(BF16)
        rest_ref[...] = jnp.transpose(wide_rest)
        stack_ref[...] = jnp.zeros(stack_ref.shape, F32)

    layer = layer_ref[...]
    left = layer
    for piece in range(3):
        part = left.astype(BF16).astype(F32)
        stack_ref[piece * PITCH : piece * PITCH + n_feat, :] = part
        left = left - part
    stack = stack_ref[...]
    column = jnp.concatenate([rest_ref[...]] * (block // LANES), axis=1)
    pre = jnp.dot(f_ref[...], stack.astype(BF16), preferred_element_type=F32)
    pre = pre + column * layer[n_exact:n_feat, :]
    hidden_ref[...] = (pre * jax.nn.sigmoid(pre)).astype(BF16)
    stack_t = jnp.transpose(stack)
    last = sum(stack_t[:, p * PITCH + n_exact : p * PITCH + n_feat] for p in range(3))
    pre = jnp.dot(stack_t.astype(BF16), ft_ref[...], preferred_element_type=F32)
    pre = pre + last * rest
    logistic = jax.nn.sigmoid(pre)
    hidden_t_ref[...] = (pre * logistic).astype(BF16)
    gain_t_ref[...] = logistic * (1.0 + pre * (1.0 - logistic))


def hidden_units(run_rows, layer, block=512):
    held, runs = run_rows.shape
    n_feat, hid = layer.shape
    depth = -(-3 * PITCH // LANES) * LANES
    return pl.pallas_call(
        hidden_kernel,
        grid=(hid // block,),
        in_specs=[
            pl.BlockSpec((held, runs), lambda i: (0, 0)),
            pl.BlockSpec((n_feat, block), lambda i: (0, i)),
        ],
        out_specs=[
            pl.BlockSpec((runs, block), lambda i: (0, i)),
            pl.BlockSpec((block, runs), lambda i: (i, 0)),
            pl.BlockSpec((block, runs), lambda i: (i, 0)),
            pl.BlockSpec((runs, LANES), lambda i: (0, 0)),
        ],
        out_shape=[
            jax.ShapeDtypeStruct((runs, hid), BF16),
            jax.ShapeDtypeStruct((hid, runs), BF16),
            jax.ShapeDtypeStruct((hid, runs), F32),
            jax.ShapeDtypeStruct((runs, LANES), BF16),
        ],
        scratch_shapes=[
            pltpu.VMEM((runs, depth), BF16),
            pltpu.VMEM((depth, runs), BF16),
            pltpu.VMEM((runs, LANES), F32),
            pltpu.VMEM((depth, block), F32),
        ],
        cost_estimate=cost(4 * runs * hid * depth, 10 * runs * hid, 4 * runs * hid),
        name="hidden_units",
    )(run_rows, layer)


def predict_kernel(hidden_ref, weight_ref, bias_ref, out_ref):
    out_ref[...] = (
        jnp.dot(hidden_ref[...], weight_ref[...], preferred_element_type=F32) + bias_ref[...]
    )


def predict(hidden, weight, bias, block=512):
    runs, hid = hidden.shape
    cells = weight.shape[1]
    return pl.pallas_call(
        predict_kernel,
        grid=(cells // block,),
        in_specs=[
            pl.BlockSpec((runs, hid), lambda i: (0, 0)),
            pl.BlockSpec((hid, block), lambda i: (0, i)),
            pl.BlockSpec((1, block), lambda i: (0, i)),
        ],
        out_specs=pl.BlockSpec((runs, block), lambda i: (0, i)),
        out_shape=jax.ShapeDtypeStruct((runs, cells), F32),
        cost_estimate=cost(2 * runs * hid * cells, 2 * hid * cells + 4 * runs * cells),
        name="predict",
    )(hidden, weight, bias)


def learn_kernel(last, has_before, scale, sources, *refs):
    grp_ref, guess_ref = refs[:2]
    targets, refs = refs[2 : 2 + sources], refs[2 + sources :]
    weight_ref, bias_ref, gain_any, feats_ref = refs[:4]
    refs = refs[4:]
    if not last:
        hidden_t_ref, refs = refs[0], refs[1:]
    if has_before:
        acc_in_ref, refs = refs[2], refs[3:]
    misfit_ref, bias_out_ref, acc_ref, extra_ref = refs[:4]
    back_ref, gain_ref, sem = refs[4:7]
    slope_ref = extra_ref if last else refs[7]
    step, steps = pl.program_id(0), pl.num_programs(0)
    load = pltpu.make_async_copy(gain_any, gain_ref, sem)

    @pl.when(step == 0)
    def _():
        load.start()

    per_source, own = targets[0].shape
    total = jnp.zeros((1, own), F32)
    for offset, target_ref in enumerate(targets):
        at = pl.ds(pl.multiple_of((grp_ref[0] ^ offset) * per_source, per_source), per_source)
        error = guess_ref[at, :] - target_ref[...]
        misfit_ref[at, :] = error.astype(BF16)
        slope = (error * scale).astype(BF16)
        slope_ref[at, :] = slope
        total = total + jnp.sum(slope.astype(F32), axis=0, keepdims=True)
    bias_out_ref[...] = bias_ref[...] - 0.5 * total
    back = lax.dot_general(
        weight_ref[...], slope_ref[...], (((1,), (1,)), ((), ())), preferred_element_type=F32
    )

    @pl.when(step == 0)
    def _():
        back_ref[...] = back

    @pl.when(step > 0)
    def _():
        back_ref[...] += back

    if not last:
        grad = jnp.dot(hidden_t_ref[...], slope_ref[...], preferred_element_type=F32)
        extra_ref[...] = (weight_ref[...].astype(F32) - 0.5 * grad).astype(BF16)

    @pl.when(step == steps - 1)
    def _():
        load.wait()
        full = back_ref[...] * gain_ref[...]
        high = full.astype(BF16)
        low = (full - high.astype(F32)).astype(BF16)
        feats = feats_ref[...]
        acc = jnp.dot(high, feats, preferred_element_type=F32)
        acc = acc + jnp.dot(low, feats, preferred_element_type=F32)
        if has_before:
            acc = acc + acc_in_ref[...]
        if last:
            acc_ref[...] = jnp.transpose(acc)[: acc_ref.shape[0], :]
        else:
            acc_ref[...] = acc


def learn(chunk, chunks, cols, grp, guess, targets, weight, bias, gain_t, feats, hidden_t, before, kept, scale):
    hid, cells = weight.shape
    sources = len(targets)
    per_source, mine = targets[0].shape
    runs = sources * per_source
    own = cols // chunks
    last, has_before = chunk == chunks - 1, before is not None
    strip = lambda i: (0, i * chunks + chunk)
    in_specs = [SCALARS, pl.BlockSpec((runs, own), strip)]
    in_specs += [pl.BlockSpec((per_source, own), lambda i: (0, i))] * sources
    in_specs += [pl.BlockSpec((hid, own), strip), pl.BlockSpec((1, own), strip), ANY, SPACE]
    args = [grp, guess, *targets, weight, bias, gain_t, feats]
    if not last:
        in_specs.append(SPACE)
        args.append(hidden_t)
    aliases = {}
    if has_before:
        aliases = {len(args): 0, len(args) + 1: 1}
        in_specs += [ANY, ANY, SPACE]
        args += list(before[:3])
        if not last:
            aliases[len(args)] = 3
            in_specs.append(ANY)
            args.append(before[3])
    acc_shape = (kept, hid) if last else (hid, LANES)
    extra = (runs, own, runs) if last else (hid, own, hid)
    scratch = [
        pltpu.VMEM((hid, runs), F32),
        pltpu.VMEM((hid, runs), F32),
        pltpu.SemaphoreType.DMA,
    ]
    if not last:
        scratch.append(pltpu.VMEM((runs, own), BF16))
    products = 1 if last else 2
    return pl.pallas_call(
        functools.partial(learn_kernel, last, has_before, scale, sources),
        grid=(mine // own,),
        in_specs=in_specs,
        out_specs=[
            pl.BlockSpec((runs, own), strip),
            pl.BlockSpec((1, own), strip),
            pl.BlockSpec(acc_shape, lambda i: (0, 0)),
            pl.BlockSpec((extra[0], own), (lambda i: (0, i)) if last else strip),
        ],
        out_shape=[
            jax.ShapeDtypeStruct((runs, cells), BF16),
            jax.ShapeDtypeStruct((1, cells), F32),
            jax.ShapeDtypeStruct(acc_shape, F32),
            jax.ShapeDtypeStruct((runs, mine) if last else (hid, cells), BF16),
        ],
        scratch_shapes=scratch,
        input_output_aliases=aliases,
        cost_estimate=cost(
            2 * runs * hid * (products * mine + 2 * LANES), 2 * hid * mine * products + 12 * runs * mine
        ),
        name="learn",
    )(*args)


def update_kernel(hidden_t_ref, slope_ref, weight_ref, _, out_ref):
    grad = jnp.dot(hidden_t_ref[...], slope_ref[...], preferred_element_type=F32)
    out_ref[...] = (weight_ref[...].astype(F32) - 0.5 * grad).astype(BF16)


def update(chunks, cols, hidden_t, slope, weight, so_far):
    hid, cells = weight.shape
    runs, mine = slope.shape
    own = cols // chunks
    strip = lambda i: (0, i * chunks + chunks - 1)
    return pl.pallas_call(
        update_kernel,
        grid=(mine // own,),
        in_specs=[
            pl.BlockSpec((hid, runs), lambda i: (0, 0)),
            pl.BlockSpec((runs, own), lambda i: (0, i)),
            pl.BlockSpec((hid, own), strip),
            ANY,
        ],
        out_specs=pl.BlockSpec((hid, own), strip),
        out_shape=jax.ShapeDtypeStruct((hid, cells), BF16),
        input_output_aliases={3: 0},
        cost_estimate=cost(2 * runs * hid * mine, 4 * hid * mine + 4 * runs * mine),
        name="update",
    )(hidden_t, slope, weight, so_far)


def halve(x, axis, bit):
    size = lax.axis_size(axis)
    upper = (lax.axis_index(axis) & bit) != 0
    half = x.shape[0] // 2
    kept = lax.dynamic_slice_in_dim(x, jnp.where(upper, half, 0), half, 0)
    sent = lax.dynamic_slice_in_dim(x, jnp.where(upper, 0, half), half, 0)
    return kept + lax.ppermute(sent, axis, [(i, i ^ bit) for i in range(size)])


def rejoin(x, axis, bit):
    size = lax.axis_size(axis)
    upper = (lax.axis_index(axis) & bit) != 0
    other = lax.ppermute(x, axis, [(i, i ^ bit) for i in range(size)])
    return jnp.where(
        upper, jnp.concatenate([other, x], axis=0), jnp.concatenate([x, other], axis=0)
    )


def sum_over_devices(x):
    grp, tile = lax.axis_size("grp"), lax.axis_size("tile")
    bits = [1 << b for b in range(grp.bit_length() - 1)]
    for bit in bits:
        x = halve(x, "grp", bit)
    n = x.shape[0] // tile
    x = lax.all_to_all(x.reshape(tile, n, LANES), "tile", 0, 0, tiled=True)
    x = jnp.sum(x.reshape(tile, n, LANES), axis=0)
    x = lax.all_to_all(jnp.broadcast_to(x[None], (tile, n, LANES)), "tile", 0, 0, tiled=True)
    x = x.reshape(tile * n, LANES)
    for bit in bits[::-1]:
        x = rejoin(x, "grp", bit)
    return x


def on_device(
    start_field, class_ids, run_levels, steepness, step_pick, input_layer, output_layer, output_bias
):
    local_runs, _, cols = start_field.shape
    n_grp, n_tile = lax.axis_size("grp"), lax.axis_size("tile")
    tile = lax.axis_index("tile")
    first_run = lax.axis_index("grp") * local_runs
    chunks = CHUNKS
    parts = spans(cols, chunks)
    runs_total, classes = run_levels.shape
    n_feat, hid = input_layer.shape

    up = [(i, i + 1) for i in range(n_tile - 1)]
    down = [(j, i) for i, j in up]
    packed = pack_edges(start_field, class_ids, parts)
    edges = []
    for c in range(chunks):
        top, bottom = packed[2 * c], packed[2 * c + 1]
        above = lax.ppermute(bottom, "tile", up)
        below = lax.ppermute(top, "tile", down)
        edges.append((above, below))

    run_rows = jnp.concatenate(
        [
            run_levels.T.astype(F32),
            step_pick[None, :].astype(F32),
            steepness[None, :],
            jnp.zeros((2 * LEVELS - classes - 2, runs_total), F32),
        ],
        axis=0,
    )
    run_rows_here = lax.dynamic_slice_in_dim(run_rows, first_run, local_runs, 1)
    ends = jnp.stack([(tile > 0).astype(F32), (tile < n_tile - 1).astype(F32)])
    brought = STEPS * (parts[0][1] - parts[0][2])
    ids_wide = jnp.concatenate(
        [
            edges[0][0][brought:].reshape(STEPS, cols).astype(jnp.int32),
            class_ids,
            edges[0][1][brought:].reshape(STEPS, cols).astype(jnp.int32),
        ],
        axis=0,
    )[:, None, :]

    hidden, hidden_t, gain_t, project = hidden_units(run_rows, input_layer)
    bias_row = output_bias[None, :]
    guess = predict(hidden, output_layer, bias_row)
    kept = -(-(n_feat + 1) // SUB) * SUB

    state = None
    scale = 2.0 / runs_total
    grp = lax.axis_index("grp").astype(jnp.int32)[None]
    for c in range(chunks):
        snaps = diffuse(c, chunks, start_field, edges, ids_wide, run_rows_here, ends, grp, n_grp)
        targets = [snaps[0]]
        for offset in range(1, n_grp):
            pairs = [(i, i ^ offset) for i in range(n_grp)]
            targets.append(lax.ppermute(snaps[offset], "grp", pairs))
        before = state
        state = learn(
            c, chunks, cols, grp, guess, targets, output_layer, bias_row,
            gain_t, project, hidden_t, before, kept, scale,
        )
    misfit, bias_next, partial, slope = state
    output_next = update(chunks, cols, hidden_t, slope, output_layer, before[3])
    flat = partial.reshape(-1, LANES)
    unit = SUB * n_grp * n_tile
    padded = -(-flat.shape[0] // unit) * unit
    flat = jnp.pad(flat, ((0, padded - flat.shape[0]), (0, 0)))
    total = sum_over_devices(flat)[: kept * hid // LANES].reshape(kept, hid)
    grad_in = jnp.concatenate(
        [total[: n_feat - 1], total[n_feat - 1 : n_feat] + total[n_feat : n_feat + 1]], axis=0
    )
    input_next = input_layer - 2.0 * grad_in
    return misfit, output_next, bias_next.reshape(-1), input_next


def solution(mesh):
    in_specs = (
        P("grp", "tile", None),
        P("tile", None),
        P(),
        P(),
        P(),
        P(),
        P(None, ("grp", "tile")),
        P(("grp", "tile")),
    )
    out_specs = (P(None, ("grp", "tile")), P(None, ("grp", "tile")), P(("grp", "tile")), P())

    return jax.shard_map(
        on_device, mesh=mesh, in_specs=in_specs, out_specs=out_specs, check_vma=False
    )
```

```python
import functools

import jax
import jax.numpy as jnp
from jax import lax
from jax.experimental import pallas as pl
from jax.experimental.pallas import tpu as pltpu
from jax.sharding import PartitionSpec as P


STEPS = 4
LEVELS = 8
LANES = 128
SUB = 8
BLOCK = 256
CHUNKS = 2
UPDATES = 2
F32 = jnp.float32
BF16 = jnp.bfloat16
SPACE = pl.BlockSpec(memory_space=pltpu.VMEM)
ANY = pl.BlockSpec(memory_space=pl.ANY)
SCALARS = pl.BlockSpec(memory_space=pltpu.SMEM)


def cost(flops, nbytes, transcendentals=0):
    return pl.CostEstimate(
        flops=int(flops), bytes_accessed=int(nbytes), transcendentals=int(transcendentals)
    )


def spans(cols, chunks):
    width = cols // chunks
    out = []
    for c in range(chunks):
        low = max(c * width - SUB, 0)
        high = min((c + 1) * width + SUB, cols)
        sent = 0 if c == 0 else c * width + SUB
        out.append((low, high, sent))
    return out


def pack_kernel(parts, field_ref, ids_ref, *outs):
    rows, cols = ids_ref.shape
    for j in range(cols // LANES):

        @pl.when(pl.program_id(0) == j)
        def _(j=j):
            for side in range(2):
                for r in range(STEPS):
                    row = r if side == 0 else rows - STEPS + r
                    tile = jnp.transpose(field_ref[:, row, :])
                    for c, (_, high, sent) in enumerate(parts):
                        first, last = max(sent, j * LANES), min(high, (j + 1) * LANES)
                        if first < last:
                            at = r * (high - sent) + first - sent
                            outs[2 * c + side][at : at + last - first, :] = tile[
                                first - j * LANES : last - j * LANES, :
                            ]
                    at = STEPS * (parts[0][1] - parts[0][2]) + r * (cols // LANES) + j
                    outs[side][at : at + 1, :] = ids_ref[
                        row : row + 1, j * LANES : (j + 1) * LANES
                    ].astype(F32)


def pack_edges(start_field, ids, parts):
    runs, rows, cols = start_field.shape
    shapes = []
    for c, (_, high, sent) in enumerate(parts):
        extra = STEPS * cols // LANES if c == 0 else 0
        shapes += [jax.ShapeDtypeStruct((STEPS * (high - sent) + extra, runs), F32)] * 2
    return pl.pallas_call(
        functools.partial(pack_kernel, parts),
        grid=(cols // LANES,),
        in_specs=[
            pl.BlockSpec((runs, rows, LANES), lambda j: (0, 0, j)),
            pl.BlockSpec((rows, cols), lambda j: (0, 0)),
        ],
        out_specs=[pl.BlockSpec(x.shape, lambda j: (0, 0)) for x in shapes],
        out_shape=shapes,
        cost_estimate=cost(0, 6 * runs * rows * cols),
        name="pack_edges",
    )(start_field, ids)


def diffuse_kernel(chunk, chunks, ends_ref, grp_ref, field_ref, ids_ref, runs_ref, *refs):
    edges, outs = refs[: 2 + 2 * (chunk > 0)], refs[2 + 2 * (chunk > 0) : -9]
    raw_ref, u0_ref, u1_ref, d_ref, a_ref, b_ref, fx_ref, v_ref, sem = refs[-9:]
    cols = ids_ref.shape[2]
    rows = field_ref.shape[1]
    total = rows + 2 * STEPS
    parts = spans(cols, chunks)
    low, high, sent = parts[chunk]
    width = high - low
    own = cols // chunks
    tile0, tile1 = low // LANES, -(-high // LANES)
    copy = pltpu.make_async_copy(field_ref.at[:, :, tile0 * LANES : tile1 * LANES], raw_ref, sem)
    copy.start()

    level, pick, steep = runs_ref[0:LEVELS], runs_ref[LEVELS : LEVELS + 1], runs_ref[LEVELS + 1 : LEVELS + 2]
    table = 0.03 * jnp.exp(level * jnp.log(F32(1.35)))
    both = jnp.concatenate([table * (0.5 * steep), table * (0.5 * (1.0 - steep))], axis=1)
    pieces = []
    for _ in range(3):
        piece = both.astype(BF16).astype(F32)
        pieces.append(piece)
        both = both - piece
    pieces.append(jnp.zeros_like(both))
    tables = jnp.concatenate(pieces, axis=0).astype(BF16)
    klass = lax.broadcasted_iota(jnp.int32, (4 * LEVELS, LANES), 0) % LEVELS
    pick8 = jnp.broadcast_to(pick, (SUB, LANES))
    has_top, has_bottom = ends_ref[0], ends_ref[1]
    zeros = jnp.zeros((SUB, LANES), F32)

    def inside(r):
        return jnp.where(r < STEPS, has_top, jnp.where(r >= total - STEPS, has_bottom, 1.0))

    def coefficients(r, carry):
        valid = inside(r)
        ids = ids_ref[r]
        for j in range(tile0, tile1):
            here = jnp.broadcast_to(ids[:, j * LANES : (j + 1) * LANES], klass.shape)
            onehot = jnp.where(here == klass, valid, 0.0)
            ab = lax.dot_general(
                onehot.astype(BF16), tables, (((0,), (0,)), ((), ())), preferred_element_type=F32
            )
            first, last = max(low, j * LANES), min(high, (j + 1) * LANES)
            at, of = slice(first - low, last - low), slice(first - j * LANES, last - j * LANES)
            a_ref[r, at, :] = ab[of, :LANES]
            b_ref[r, at, :] = ab[of, LANES:]
        for ref in (u0_ref, u1_ref, d_ref):
            ref[r, 0:SUB, :] = zeros
            ref[r, SUB + width : 2 * SUB + width, :] = zeros
        return carry

    lax.fori_loop(0, total, coefficients, 0, unroll=4)

    for side in range(2):
        here = edges[side]
        for r in range(STEPS):
            row = r if side == 0 else total - STEPS + r
            n = high - sent
            at = SUB + sent - low
            u0_ref[row, at : at + n, :] = here[r * n : (r + 1) * n, :]
            if chunk:
                prior = edges[2 + side]
                n0 = parts[chunk - 1][1] - parts[chunk - 1][2]
                m = sent - low
                u0_ref[row, SUB : SUB + m, :] = prior[(r + 1) * n0 - m : (r + 1) * n0, :]
    copy.wait()
    for i in range(rows):
        for j in range(tile0, tile1):
            tile = jnp.transpose(raw_ref[:, i, (j - tile0) * LANES : (j - tile0 + 1) * LANES])
            first, last = max(low, j * LANES), min(high, (j + 1) * LANES)
            at = SUB + first - low
            u0_ref[STEPS + i, at : at + last - first, :] = tile[first - j * LANES : last - j * LANES, :]

    blocks = range(width // SUB)
    for step in range(1, STEPS + 1):
        src, dst = (u0_ref, u1_ref) if step % 2 else (u1_ref, u0_ref)

        def conduct(r, k, u, src=src):
            at = slice(k * SUB, (k + 1) * SUB)
            d = a_ref[r, at, :] + b_ref[r, at, :] * (1.0 / (1.0 + u * u))
            d_ref[r, SUB + k * SUB : 2 * SUB + k * SUB, :] = d
            return d

        top = step - 1
        for k in blocks:
            at = slice(SUB + k * SUB, 2 * SUB + k * SUB)
            u, un = src[top, at, :], src[top + 1, at, :]
            d, dn = conduct(top, k, u), conduct(top + 1, k, un)
            v_ref[k * SUB : (k + 1) * SUB, :] = (d + dn) * (un - u)

        def advance(r, carry, src=src, dst=dst, step=step, conduct=conduct):
            active = pick8 >= jnp.where(inside(r) > 0.0, F32(step), F32(2 * STEPS))
            for k in range(-1, width // SUB):
                p = SUB + k * SUB
                u, d = src[r, p : p + SUB, :], d_ref[r, p : p + SUB, :]
                flux = (d + d_ref[r, p + 1 : p + 1 + SUB, :]) * (src[r, p + 1 : p + 1 + SUB, :] - u)
                fx_ref[p : p + SUB, :] = flux
                if k < 0:
                    continue
                at = slice(k * SUB, (k + 1) * SUB)
                un = src[r + 1, p : p + SUB, :]
                dn = conduct(r + 1, k, un)
                down = (d + dn) * (un - u)
                across = flux - fx_ref[p - 1 : p - 1 + SUB, :]
                new = u + across + (down - v_ref[at, :])
                v_ref[at, :] = down
                dst[r, p : p + SUB, :] = jnp.where(active, new, u)
            return carry

        lax.fori_loop(step, total - step, advance, 0)

    result = u0_ref if STEPS % 2 == 0 else u1_ref
    per_block = rows // len(outs)
    for offset, out_ref in enumerate(outs):
        row = STEPS + (grp_ref[0] ^ offset) * per_block
        for i in range(per_block):
            for j in range(own // LANES):
                p = SUB + chunk * own + j * LANES - low
                at = i * own + j * LANES
                out_ref[:, at : at + LANES] = jnp.transpose(result[row + i, p : p + LANES, :])


def diffuse(chunk, chunks, start_field, edges, ids_wide, run_rows, ends, grp, blocks):
    runs, rows, cols = start_field.shape
    total = rows + 2 * STEPS
    low, high, _ = spans(cols, chunks)[chunk]
    width = high - low
    tiles = -(-high // LANES) - low // LANES
    own = cols // chunks
    edges = list(edges[chunk]) + (list(edges[chunk - 1]) if chunk else [])
    state = pltpu.VMEM((total, width + 2 * SUB, runs), F32)
    return pl.pallas_call(
        functools.partial(diffuse_kernel, chunk, chunks),
        in_specs=[SCALARS, SCALARS, ANY, SPACE, SPACE] + [SPACE] * len(edges),
        out_specs=[SPACE] * blocks,
        out_shape=[jax.ShapeDtypeStruct((runs, rows * own // blocks), F32)] * blocks,
        scratch_shapes=[
            pltpu.VMEM((runs, rows, tiles * LANES), F32),
            state,
            state,
            state,
            pltpu.VMEM((total, width, runs), F32),
            pltpu.VMEM((total, width, runs), F32),
            pltpu.VMEM((width + 2 * SUB, runs), F32),
            pltpu.VMEM((width, runs), F32),
            pltpu.SemaphoreType.DMA,
        ],
        cost_estimate=cost(100 * runs * total * width, 12 * runs * total * width),
        name="diffuse",
    )(ends, grp, start_field, ids_wide, run_rows, *edges)


PITCH = 80


def hidden_kernel(
    runs_ref, layer_ref, hidden_ref, hidden_t_ref, gain_t_ref, project_ref, f_ref, ft_ref, rest_ref, stack_ref
):
    depth, runs = ft_ref.shape
    n_feat, block = layer_ref.shape
    n_exact = n_feat - 1
    steep = runs_ref[LEVELS + 1 : LEVELS + 2]
    rest = steep - steep.astype(BF16).astype(F32)

    @pl.when(pl.program_id(0) == 0)
    def _():
        held = runs_ref[...]
        row = lax.broadcasted_iota(jnp.int32, (depth, held.shape[0]), 0)
        col = lax.broadcasted_iota(jnp.int32, (depth, held.shape[0]), 1)

        def place(row):
            return jnp.where(row < 3 * PITCH, row % PITCH, PITCH)

        n_level = LEVELS * LEVELS
        at = place(row)
        source = jnp.where(
            at < n_level,
            at // LEVELS,
            jnp.where(at < n_exact, LEVELS, jnp.where(at == n_exact, LEVELS + 1, -1)),
        )
        spread = jnp.where(col == source, 1.0, 0.0).astype(BF16)
        value = jnp.dot(spread, held.astype(BF16), preferred_element_type=F32)
        at = place(lax.broadcasted_iota(jnp.int32, (depth, runs), 0))
        wanted = jnp.where(at < n_level, at % LEVELS, at - n_level + 1).astype(F32)
        feats = jnp.where(at < n_exact, jnp.where(value == wanted, 1.0, 0.0), value)
        ft_ref[...] = feats.astype(BF16)
        f_ref[...] = jnp.transpose(feats).astype(BF16)
        line = lax.broadcasted_iota(jnp.int32, (LANES, runs), 0)
        wide_rest = jnp.broadcast_to(rest, (LANES, runs))
        project = jnp.where(
            line < n_feat, feats[:LANES], jnp.where(line == n_feat, wide_rest, 0.0)
        )
        project_ref[...] = jnp.transpose(project).astype(BF16)
        rest_ref[...] = jnp.transpose(wide_rest)
        stack_ref[...] = jnp.zeros(stack_ref.shape, F32)

    layer = layer_ref[...]
    left = layer
    for piece in range(3):
        part = left.astype(BF16).astype(F32)
        stack_ref[piece * PITCH : piece * PITCH + n_feat, :] = part
        left = left - part
    stack = stack_ref[...]
    column = jnp.concatenate([rest_ref[...]] * (block // LANES), axis=1)
    pre = jnp.dot(f_ref[...], stack.astype(BF16), preferred_element_type=F32)
    pre = pre + column * layer[n_exact:n_feat, :]
    hidden_ref[...] = (pre * jax.nn.sigmoid(pre)).astype(BF16)
    stack_t = jnp.transpose(stack)
    last = sum(stack_t[:, p * PITCH + n_exact : p * PITCH + n_feat] for p in range(3))
    pre = jnp.dot(stack_t.astype(BF16), ft_ref[...], preferred_element_type=F32)
    pre = pre + last * rest
    logistic = jax.nn.sigmoid(pre)
    hidden_t_ref[...] = (pre * logistic).astype(BF16)
    gain_t_ref[...] = logistic * (1.0 + pre * (1.0 - logistic))


def hidden_units(run_rows, layer, block=512):
    held, runs = run_rows.shape
    n_feat, hid = layer.shape
    depth = -(-3 * PITCH // LANES) * LANES
    return pl.pallas_call(
        hidden_kernel,
        grid=(hid // block,),
        in_specs=[
            pl.BlockSpec((held, runs), lambda i: (0, 0)),
            pl.BlockSpec((n_feat, block), lambda i: (0, i)),
        ],
        out_specs=[
            pl.BlockSpec((runs, block), lambda i: (0, i)),
            pl.BlockSpec((block, runs), lambda i: (i, 0)),
            pl.BlockSpec((block, runs), lambda i: (i, 0)),
            pl.BlockSpec((runs, LANES), lambda i: (0, 0)),
        ],
        out_shape=[
            jax.ShapeDtypeStruct((runs, hid), BF16),
            jax.ShapeDtypeStruct((hid, runs), BF16),
            jax.ShapeDtypeStruct((hid, runs), F32),
            jax.ShapeDtypeStruct((runs, LANES), BF16),
        ],
        scratch_shapes=[
            pltpu.VMEM((runs, depth), BF16),
            pltpu.VMEM((depth, runs), BF16),
            pltpu.VMEM((runs, LANES), F32),
            pltpu.VMEM((depth, block), F32),
        ],
        cost_estimate=cost(4 * runs * hid * depth, 10 * runs * hid, 4 * runs * hid),
        name="hidden_units",
    )(run_rows, layer)


def predict_kernel(hidden_ref, weight_ref, bias_ref, out_ref):
    out_ref[...] = (
        jnp.dot(hidden_ref[...], weight_ref[...], preferred_element_type=F32) + bias_ref[...]
    )


def predict(hidden, weight, bias, block=512):
    runs, hid = hidden.shape
    cells = weight.shape[1]
    return pl.pallas_call(
        predict_kernel,
        grid=(cells // block,),
        in_specs=[
            pl.BlockSpec((runs, hid), lambda i: (0, 0)),
            pl.BlockSpec((hid, block), lambda i: (0, i)),
            pl.BlockSpec((1, block), lambda i: (0, i)),
        ],
        out_specs=pl.BlockSpec((runs, block), lambda i: (0, i)),
        out_shape=jax.ShapeDtypeStruct((runs, cells), F32),
        cost_estimate=cost(2 * runs * hid * cells, 2 * hid * cells + 4 * runs * cells),
        name="predict",
    )(hidden, weight, bias)


def learn_kernel(last, has_before, scale, sources, *refs):
    grp_ref, guess_ref = refs[:2]
    targets, refs = refs[2 : 2 + sources], refs[2 + sources :]
    weight_ref, bias_ref, gain_any, feats_ref = refs[:4]
    refs = refs[4:]
    if not last:
        hidden_t_ref, refs = refs[0], refs[1:]
    if has_before:
        acc_in_any, refs = refs[2], refs[3 + (not last) :]
    misfit_ref, bias_out_ref, acc_ref, extra_ref = refs[:4]
    back_ref, gain_ref, sem, acc_in_ref = refs[4:8]
    slope_ref = extra_ref if last else refs[8]
    step, steps = pl.program_id(0), pl.num_programs(0)
    load = pltpu.make_async_copy(gain_any, gain_ref, sem.at[0])
    if has_before:
        load_acc = pltpu.make_async_copy(acc_in_any, acc_in_ref, sem.at[1])

    @pl.when(step == 0)
    def _():
        load.start()
        if has_before:
            load_acc.start()
        back_ref[...] = jnp.zeros(back_ref.shape, F32)

    per_source, own = targets[0].shape
    total = jnp.zeros((1, own), F32)
    for offset, target_ref in enumerate(targets):
        at = pl.ds(pl.multiple_of((grp_ref[0] ^ offset) * per_source, per_source), per_source)
        error = guess_ref[at, :] - target_ref[...]
        misfit_ref[at, :] = error.astype(BF16)
        slope = (error * scale).astype(BF16)
        slope_ref[at, :] = slope
        total = total + jnp.sum(slope.astype(F32), axis=0, keepdims=True)
    bias_out_ref[...] = bias_ref[...] - 0.5 * total
    slope = slope_ref[...]
    for h in range(0, weight_ref.shape[0], BLOCK):
        at = slice(h, h + BLOCK)
        weight = weight_ref[at, :]
        back_ref[at, :] += lax.dot_general(
            weight, slope, (((1,), (1,)), ((), ())), preferred_element_type=F32
        )
        if not last:
            grad = jnp.dot(hidden_t_ref[at, :], slope, preferred_element_type=F32)
            extra_ref[at, :] = (weight.astype(F32) - 0.5 * grad).astype(BF16)

    @pl.when(step == steps - 1)
    def _():
        load.wait()
        if has_before:
            load_acc.wait()
        feats = feats_ref[...]
        for h in range(0, back_ref.shape[0], BLOCK):
            at = slice(h, h + BLOCK)
            full = back_ref[at, :] * gain_ref[at, :]
            high = full.astype(BF16)
            low = (full - high.astype(F32)).astype(BF16)
            acc = jnp.dot(high, feats, preferred_element_type=F32)
            acc = acc + jnp.dot(low, feats, preferred_element_type=F32)
            if has_before:
                acc = acc + acc_in_ref[at, :]
            if last:
                for t in range(0, BLOCK, LANES):
                    turned = jnp.transpose(acc[t : t + LANES, :])
                    acc_ref[(h + t) // LANES] = turned[: acc_ref.shape[1], :]
            else:
                acc_ref[at, :] = acc


def learn(chunk, chunks, cols, grp, guess, targets, weight, bias, gain_t, feats, hidden_t, before, kept, scale):
    hid, cells = weight.shape
    sources = len(targets)
    per_source, mine = targets[0].shape
    runs = sources * per_source
    own = cols // chunks
    last, has_before = chunk == chunks - 1, before is not None
    strip = lambda i: (0, i * chunks + chunk)
    in_specs = [SCALARS, pl.BlockSpec((runs, own), strip)]
    in_specs += [pl.BlockSpec((per_source, own), lambda i: (0, i))] * sources
    in_specs += [pl.BlockSpec((hid, own), strip), pl.BlockSpec((1, own), strip), ANY, SPACE]
    args = [grp, guess, *targets, weight, bias, gain_t, feats]
    if not last:
        in_specs.append(SPACE)
        args.append(hidden_t)
    aliases = {}
    if has_before:
        aliases = {len(args): 0, len(args) + 1: 1}
        in_specs += [ANY, ANY, ANY]
        args += list(before[:3])
        if not last:
            aliases[len(args)] = 3
            in_specs.append(ANY)
            args.append(before[3])
    acc_shape = (hid // LANES, kept, LANES) if last else (hid, LANES)
    extra = (runs, own, runs) if last else (hid, own, hid)
    scratch = [
        pltpu.VMEM((hid, runs), F32),
        pltpu.VMEM((hid, runs), F32),
        pltpu.SemaphoreType.DMA((2,)),
        pltpu.VMEM((hid, LANES), F32),
    ]
    if not last:
        scratch.append(pltpu.VMEM((runs, own), BF16))
    products = 1 if last else 2
    return pl.pallas_call(
        functools.partial(learn_kernel, last, has_before, scale, sources),
        grid=(mine // own,),
        in_specs=in_specs,
        out_specs=[
            pl.BlockSpec((runs, own), strip),
            pl.BlockSpec((1, own), strip),
            pl.BlockSpec(acc_shape, lambda i: (0,) * len(acc_shape)),
            pl.BlockSpec((extra[0], own), (lambda i: (0, i)) if last else strip),
        ],
        out_shape=[
            jax.ShapeDtypeStruct((runs, cells), BF16),
            jax.ShapeDtypeStruct((1, cells), F32),
            jax.ShapeDtypeStruct(acc_shape, F32),
            jax.ShapeDtypeStruct((runs, mine) if last else (hid, cells), BF16),
        ],
        scratch_shapes=scratch,
        input_output_aliases=aliases,
        cost_estimate=cost(
            2 * runs * hid * (products * mine + 2 * LANES), 2 * hid * mine * products + 12 * runs * mine
        ),
        name="learn",
    )(*args)


def update_kernel(hidden_t_ref, slope_ref, weight_ref, _, out_ref):
    slope = slope_ref[...]
    for h in range(0, weight_ref.shape[0], BLOCK):
        at = slice(h, h + BLOCK)
        grad = jnp.dot(hidden_t_ref[at, :], slope, preferred_element_type=F32)
        out_ref[at, :] = (weight_ref[at, :].astype(F32) - 0.5 * grad).astype(BF16)


def update(first, count, chunks, cols, hidden_t, slope, weight, so_far):
    hid, cells = weight.shape
    runs, _ = slope.shape
    own = cols // chunks
    strip = lambda i: (0, (first + i) * chunks + chunks - 1)
    return pl.pallas_call(
        update_kernel,
        grid=(count,),
        in_specs=[
            pl.BlockSpec((hid, runs), lambda i: (0, 0)),
            pl.BlockSpec((runs, own), lambda i: (0, first + i)),
            pl.BlockSpec((hid, own), strip),
            ANY,
        ],
        out_specs=pl.BlockSpec((hid, own), strip),
        out_shape=jax.ShapeDtypeStruct((hid, cells), BF16),
        input_output_aliases={3: 0},
        cost_estimate=cost(2 * runs * hid * own * count, (4 * hid + 4 * runs) * own * count),
        name="update",
    )(hidden_t, slope, weight, so_far)


def finish_kernel(total_ref, layer_ref, out_ref):
    n_feat = layer_ref.shape[0]
    line = lax.broadcasted_iota(jnp.int32, (n_feat, LANES), 0)
    for t in range(total_ref.shape[0]):
        at = slice(t * LANES, (t + 1) * LANES)
        rest = jnp.broadcast_to(total_ref[t, n_feat : n_feat + 1, :], (n_feat, LANES))
        grad = total_ref[t, :n_feat, :] + jnp.where(line == n_feat - 1, rest, 0.0)
        out_ref[:, at] = layer_ref[:, at] - 2.0 * grad


def finish(total, layer):
    return pl.pallas_call(
        finish_kernel,
        in_specs=[SPACE, SPACE],
        out_specs=SPACE,
        out_shape=jax.ShapeDtypeStruct(layer.shape, F32),
        cost_estimate=cost(3 * layer.size, 12 * layer.size),
        name="finish",
    )(total, layer)


def bits_of(size):
    return [1 << b for b in range(size.bit_length() - 1)]


def halve(x, axis, bit):
    size = lax.axis_size(axis)
    upper = (lax.axis_index(axis) & bit) != 0
    half = x.shape[0] // 2
    kept = lax.dynamic_slice_in_dim(x, jnp.where(upper, half, 0), half, 0)
    sent = lax.dynamic_slice_in_dim(x, jnp.where(upper, 0, half), half, 0)
    return kept + lax.ppermute(sent, axis, [(i, i ^ bit) for i in range(size)])


def rejoin(x, axis, bit):
    size = lax.axis_size(axis)
    upper = (lax.axis_index(axis) & bit) != 0
    other = lax.ppermute(x, axis, [(i, i ^ bit) for i in range(size)])
    return jnp.where(
        upper, jnp.concatenate([other, x], axis=0), jnp.concatenate([x, other], axis=0)
    )


def sum_over_devices(x):
    grp, tile = lax.axis_size("grp"), lax.axis_size("tile")
    for bit in bits_of(grp):
        x = halve(x, "grp", bit)
    for bit in bits_of(tile):
        x = x + lax.ppermute(x, "tile", [(i, i ^ bit) for i in range(tile)])
    for bit in bits_of(grp)[::-1]:
        x = rejoin(x, "grp", bit)
    return x


def on_device(
    start_field, class_ids, run_levels, steepness, step_pick, input_layer, output_layer, output_bias
):
    local_runs, rows, cols = start_field.shape
    n_grp, n_tile = lax.axis_size("grp"), lax.axis_size("tile")
    tile = lax.axis_index("tile")
    first_run = lax.axis_index("grp") * local_runs
    chunks = CHUNKS
    parts = spans(cols, chunks)
    runs_total, classes = run_levels.shape
    n_feat, _ = input_layer.shape

    up = [(i, i + 1) for i in range(n_tile - 1)]
    down = [(j, i) for i, j in up]
    packed = pack_edges(start_field, class_ids, parts)
    edges = []
    for c in range(chunks):
        top, bottom = packed[2 * c], packed[2 * c + 1]
        above = lax.ppermute(bottom, "tile", up)
        below = lax.ppermute(top, "tile", down)
        edges.append((above, below))

    run_rows = jnp.concatenate(
        [
            run_levels.T.astype(F32),
            step_pick[None, :].astype(F32),
            steepness[None, :],
            jnp.zeros((2 * LEVELS - classes - 2, runs_total), F32),
        ],
        axis=0,
    )
    run_rows_here = lax.dynamic_slice_in_dim(run_rows, first_run, local_runs, 1)
    ends = jnp.stack([(tile > 0).astype(F32), (tile < n_tile - 1).astype(F32)])
    brought = STEPS * (parts[0][1] - parts[0][2])
    ids_wide = jnp.concatenate(
        [
            edges[0][0][brought:].reshape(STEPS, cols).astype(jnp.int32),
            class_ids,
            edges[0][1][brought:].reshape(STEPS, cols).astype(jnp.int32),
        ],
        axis=0,
    )[:, None, :]

    hidden, hidden_t, gain_t, project = hidden_units(run_rows, input_layer)
    bias_row = output_bias[None, :]
    guess = predict(hidden, output_layer, bias_row)
    kept = -(-(n_feat + 1) // SUB) * SUB

    state = None
    scale = 2.0 / runs_total
    grp = lax.axis_index("grp").astype(jnp.int32)[None]
    for c in range(chunks):
        snaps = diffuse(c, chunks, start_field, edges, ids_wide, run_rows_here, ends, grp, n_grp)
        targets = [snaps[0]]
        for offset in range(1, n_grp):
            pairs = [(i, i ^ offset) for i in range(n_grp)]
            targets.append(lax.ppermute(snaps[offset], "grp", pairs))
        before = state
        state = learn(
            c, chunks, cols, grp, guess, targets, output_layer, bias_row,
            gain_t, project, hidden_t, before, kept, scale,
        )
    misfit, bias_next, partial, slope = state
    output_next, strips = before[3], rows // n_grp
    for part in range(UPDATES):
        first, past = part * strips // UPDATES, (part + 1) * strips // UPDATES
        output_next = update(
            first, past - first, chunks, cols, hidden_t, slope, output_layer, output_next
        )
    total = sum_over_devices(partial.reshape(-1, LANES)).reshape(partial.shape)
    input_next = finish(total, input_layer)
    return misfit, output_next, bias_next.reshape(-1), input_next


def solution(mesh):
    in_specs = (
        P("grp", "tile", None),
        P("tile", None),
        P(),
        P(),
        P(),
        P(),
        P(None, ("grp", "tile")),
        P(("grp", "tile")),
    )
    out_specs = (P(None, ("grp", "tile")), P(None, ("grp", "tile")), P(("grp", "tile")), P())

    return jax.shard_map(
        on_device, mesh=mesh, in_specs=in_specs, out_specs=out_specs, check_vma=False
    )
```

```python
import functools

import jax
import jax.numpy as jnp
from jax import lax
from jax.experimental import pallas as pl
from jax.experimental.pallas import tpu as pltpu
from jax.sharding import PartitionSpec as P


STEPS = 4
LEVELS = 8
LANES = 128
SUB = 8
BLOCK = 256
CHUNKS = 2
UPDATES = 2
F32 = jnp.float32
BF16 = jnp.bfloat16
SPACE = pl.BlockSpec(memory_space=pltpu.VMEM)
ANY = pl.BlockSpec(memory_space=pl.ANY)
SCALARS = pl.BlockSpec(memory_space=pltpu.SMEM)


def in_vmem(x):
    return pltpu.with_memory_space_constraint(x, pltpu.VMEM)


def cost(flops, nbytes, transcendentals=0):
    return pl.CostEstimate(
        flops=int(flops), bytes_accessed=int(nbytes), transcendentals=int(transcendentals)
    )


def spans(cols, chunks):
    width = cols // chunks
    out = []
    for c in range(chunks):
        low = max(c * width - SUB, 0)
        high = min((c + 1) * width + SUB, cols)
        sent = 0 if c == 0 else c * width + SUB
        out.append((low, high, sent))
    return out


def pack_kernel(parts, field_ref, ids_ref, *outs):
    rows, cols = ids_ref.shape
    for j in range(cols // LANES):

        @pl.when(pl.program_id(0) == j)
        def _(j=j):
            for side in range(2):
                for r in range(STEPS):
                    row = r if side == 0 else rows - STEPS + r
                    tile = jnp.transpose(field_ref[:, row, :])
                    for c, (_, high, sent) in enumerate(parts):
                        first, last = max(sent, j * LANES), min(high, (j + 1) * LANES)
                        if first < last:
                            at = r * (high - sent) + first - sent
                            outs[2 * c + side][at : at + last - first, :] = tile[
                                first - j * LANES : last - j * LANES, :
                            ]
                    at = STEPS * (parts[0][1] - parts[0][2]) + r * (cols // LANES) + j
                    outs[side][at : at + 1, :] = ids_ref[
                        row : row + 1, j * LANES : (j + 1) * LANES
                    ].astype(F32)


def pack_edges(start_field, ids, parts):
    runs, rows, cols = start_field.shape
    shapes = []
    for c, (_, high, sent) in enumerate(parts):
        extra = STEPS * cols // LANES if c == 0 else 0
        shapes += [jax.ShapeDtypeStruct((STEPS * (high - sent) + extra, runs), F32)] * 2
    return pl.pallas_call(
        functools.partial(pack_kernel, parts),
        grid=(cols // LANES,),
        in_specs=[
            pl.BlockSpec((runs, rows, LANES), lambda j: (0, 0, j)),
            pl.BlockSpec((rows, cols), lambda j: (0, 0)),
        ],
        out_specs=[pl.BlockSpec(x.shape, lambda j: (0, 0)) for x in shapes],
        out_shape=shapes,
        cost_estimate=cost(0, 6 * runs * rows * cols),
        name="pack_edges",
    )(start_field, ids)


def diffuse_kernel(chunk, chunks, ends_ref, grp_ref, field_ref, ids_ref, runs_ref, *refs):
    edges, outs = refs[: 2 + 2 * (chunk > 0)], refs[2 + 2 * (chunk > 0) : -11]
    raw_ref, u0_ref, u1_ref, d_ref, a_ref, b_ref, fx_ref, v_ref, wide_ref, made_ref, sem = refs[-11:]
    rows, cols = ids_ref.shape
    total = rows + 2 * STEPS
    parts = spans(cols, chunks)
    low, high, sent = parts[chunk]
    width = high - low
    own = cols // chunks
    tile0, tile1 = low // LANES, -(-high // LANES)
    copy = pltpu.make_async_copy(field_ref.at[:, :, tile0 * LANES : tile1 * LANES], raw_ref, sem.at[0])
    copy.start()
    brought = STEPS * (parts[0][1] - parts[0][2])
    for j in range(tile0, tile1):
        at = slice(j * LANES, (j + 1) * LANES)
        for side in range(2):
            for r in range(STEPS):
                line = brought + r * (cols // LANES) + j
                wide_ref[side * (total - STEPS) + r, :, at] = edges[side - 2][line : line + 1, :]
        for r in range(rows):
            wide_ref[STEPS + r, :, at] = ids_ref[r : r + 1, at].astype(F32)

    level, pick, steep = runs_ref[0:LEVELS], runs_ref[LEVELS : LEVELS + 1], runs_ref[LEVELS + 1 : LEVELS + 2]
    table = 0.03 * jnp.exp(level * jnp.log(F32(1.35)))
    both = jnp.concatenate([table * (0.5 * steep), table * (0.5 * (1.0 - steep))], axis=1)
    pieces = []
    for _ in range(3):
        piece = both.astype(BF16).astype(F32)
        pieces.append(piece)
        both = both - piece
    pieces.append(jnp.zeros_like(both))
    tables = jnp.concatenate(pieces, axis=0).astype(BF16)
    klass = (lax.broadcasted_iota(jnp.int32, (4 * LEVELS, LANES), 0) % LEVELS).astype(F32)
    pick8 = jnp.broadcast_to(pick, (SUB, LANES))
    has_top, has_bottom = ends_ref[0], ends_ref[1]
    zeros = jnp.zeros((SUB, LANES), F32)

    def inside(r):
        return jnp.where(r < STEPS, has_top, jnp.where(r >= total - STEPS, has_bottom, 1.0))

    def coefficients(r, carry):
        valid = inside(r)
        ids = wide_ref[r]
        for j in range(tile0, tile1):
            here = jnp.broadcast_to(ids[:, j * LANES : (j + 1) * LANES], klass.shape)
            onehot = jnp.where(here == klass, valid, 0.0)
            ab = lax.dot_general(
                onehot.astype(BF16), tables, (((0,), (0,)), ((), ())), preferred_element_type=F32
            )
            first, last = max(low, j * LANES), min(high, (j + 1) * LANES)
            at, of = slice(first - low, last - low), slice(first - j * LANES, last - j * LANES)
            a_ref[r, at, :] = ab[of, :LANES]
            b_ref[r, at, :] = ab[of, LANES:]
        for ref in (u0_ref, u1_ref, d_ref):
            ref[r, 0:SUB, :] = zeros
            ref[r, SUB + width : 2 * SUB + width, :] = zeros
        return carry

    lax.fori_loop(0, total, coefficients, 0, unroll=4)

    for side in range(2):
        here = edges[side]
        for r in range(STEPS):
            row = r if side == 0 else total - STEPS + r
            n = high - sent
            at = SUB + sent - low
            u0_ref[row, at : at + n, :] = here[r * n : (r + 1) * n, :]
            if chunk:
                prior = edges[2 + side]
                n0 = parts[chunk - 1][1] - parts[chunk - 1][2]
                m = sent - low
                u0_ref[row, SUB : SUB + m, :] = prior[(r + 1) * n0 - m : (r + 1) * n0, :]
    copy.wait()
    for i in range(rows):
        for j in range(tile0, tile1):
            tile = jnp.transpose(raw_ref[:, i, (j - tile0) * LANES : (j - tile0 + 1) * LANES])
            first, last = max(low, j * LANES), min(high, (j + 1) * LANES)
            at = SUB + first - low
            u0_ref[STEPS + i, at : at + last - first, :] = tile[first - j * LANES : last - j * LANES, :]

    blocks = range(width // SUB)
    for step in range(1, STEPS + 1):
        src, dst = (u0_ref, u1_ref) if step % 2 else (u1_ref, u0_ref)

        def conduct(r, k, u, src=src):
            at = slice(k * SUB, (k + 1) * SUB)
            d = a_ref[r, at, :] + b_ref[r, at, :] * (1.0 / (1.0 + u * u))
            d_ref[r, SUB + k * SUB : 2 * SUB + k * SUB, :] = d
            return d

        top = step - 1
        for k in blocks:
            at = slice(SUB + k * SUB, 2 * SUB + k * SUB)
            u, un = src[top, at, :], src[top + 1, at, :]
            d, dn = conduct(top, k, u), conduct(top + 1, k, un)
            v_ref[k * SUB : (k + 1) * SUB, :] = (d + dn) * (un - u)

        def advance(r, carry, src=src, dst=dst, step=step, conduct=conduct):
            active = pick8 >= jnp.where(inside(r) > 0.0, F32(step), F32(2 * STEPS))
            for k in range(-1, width // SUB):
                p = SUB + k * SUB
                u, d = src[r, p : p + SUB, :], d_ref[r, p : p + SUB, :]
                flux = (d + d_ref[r, p + 1 : p + 1 + SUB, :]) * (src[r, p + 1 : p + 1 + SUB, :] - u)
                fx_ref[p : p + SUB, :] = flux
                if k < 0:
                    continue
                at = slice(k * SUB, (k + 1) * SUB)
                un = src[r + 1, p : p + SUB, :]
                dn = conduct(r + 1, k, un)
                down = (d + dn) * (un - u)
                across = flux - fx_ref[p - 1 : p - 1 + SUB, :]
                new = u + across + (down - v_ref[at, :])
                v_ref[at, :] = down
                dst[r, p : p + SUB, :] = jnp.where(active, new, u)
            return carry

        lax.fori_loop(step, total - step, advance, 0)

    result = u0_ref if STEPS % 2 == 0 else u1_ref
    per_block = rows // len(outs)
    done = []
    for offset in list(range(1, len(outs))) + [0]:
        row = STEPS + (grp_ref[0] ^ offset) * per_block
        for i in range(per_block):
            for j in range(own // LANES):
                p = SUB + chunk * own + j * LANES - low
                at = i * own + j * LANES
                made_ref[offset, :, at : at + LANES] = jnp.transpose(result[row + i, p : p + LANES, :])
        done.append(pltpu.make_async_copy(made_ref.at[offset], outs[offset], sem.at[1 + offset]))
        done[-1].start()
    for sent_out in done:
        sent_out.wait()


def diffuse(chunk, chunks, start_field, edges, ids, run_rows, ends, grp, blocks):
    runs, rows, cols = start_field.shape
    total = rows + 2 * STEPS
    low, high, _ = spans(cols, chunks)[chunk]
    width = high - low
    tiles = -(-high // LANES) - low // LANES
    own = cols // chunks
    edges = list(edges[chunk]) + (list(edges[chunk - 1]) if chunk else [])
    state = pltpu.VMEM((total, width + 2 * SUB, runs), F32)
    return pl.pallas_call(
        functools.partial(diffuse_kernel, chunk, chunks),
        in_specs=[SCALARS, SCALARS, ANY, SPACE, SPACE] + [SPACE] * len(edges),
        out_specs=[ANY] * blocks,
        out_shape=[jax.ShapeDtypeStruct((runs, rows * own // blocks), F32)] * blocks,
        scratch_shapes=[
            pltpu.VMEM((runs, rows, tiles * LANES), F32),
            state,
            state,
            state,
            pltpu.VMEM((total, width, runs), F32),
            pltpu.VMEM((total, width, runs), F32),
            pltpu.VMEM((width + 2 * SUB, runs), F32),
            pltpu.VMEM((width, runs), F32),
            pltpu.VMEM((total, 1, cols), F32),
            pltpu.VMEM((blocks, runs, rows * own // blocks), F32),
            pltpu.SemaphoreType.DMA((blocks + 1,)),
        ],
        cost_estimate=cost(100 * runs * total * width, 12 * runs * total * width),
        name="diffuse",
    )(ends, grp, start_field, ids, run_rows, *edges)


PITCH = 80


def hidden_kernel(
    runs_ref, layer_ref, hidden_ref, hidden_t_ref, gain_t_ref, project_ref, f_ref, ft_ref, rest_ref, stack_ref
):
    depth, runs = ft_ref.shape
    n_feat, block = layer_ref.shape
    n_exact = n_feat - 1
    steep = runs_ref[LEVELS + 1 : LEVELS + 2]
    rest = steep - steep.astype(BF16).astype(F32)

    @pl.when(pl.program_id(0) == 0)
    def _():
        held = runs_ref[...]
        row = lax.broadcasted_iota(jnp.int32, (depth, held.shape[0]), 0)
        col = lax.broadcasted_iota(jnp.int32, (depth, held.shape[0]), 1)

        def place(row):
            return jnp.where(row < 3 * PITCH, row % PITCH, PITCH)

        n_level = LEVELS * LEVELS
        at = place(row)
        source = jnp.where(
            at < n_level,
            at // LEVELS,
            jnp.where(at < n_exact, LEVELS, jnp.where(at == n_exact, LEVELS + 1, -1)),
        )
        spread = jnp.where(col == source, 1.0, 0.0).astype(BF16)
        value = jnp.dot(spread, held.astype(BF16), preferred_element_type=F32)
        at = place(lax.broadcasted_iota(jnp.int32, (depth, runs), 0))
        wanted = jnp.where(at < n_level, at % LEVELS, at - n_level + 1).astype(F32)
        feats = jnp.where(at < n_exact, jnp.where(value == wanted, 1.0, 0.0), value)
        ft_ref[...] = feats.astype(BF16)
        f_ref[...] = jnp.transpose(feats).astype(BF16)
        line = lax.broadcasted_iota(jnp.int32, (LANES, runs), 0)
        wide_rest = jnp.broadcast_to(rest, (LANES, runs))
        project = jnp.where(
            line < n_feat, feats[:LANES], jnp.where(line == n_feat, wide_rest, 0.0)
        )
        project_ref[...] = jnp.transpose(project).astype(BF16)
        rest_ref[...] = jnp.transpose(wide_rest)
        stack_ref[...] = jnp.zeros(stack_ref.shape, F32)

    layer = layer_ref[...]
    left = layer
    for piece in range(3):
        part = left.astype(BF16).astype(F32)
        stack_ref[piece * PITCH : piece * PITCH + n_feat, :] = part
        left = left - part
    stack = stack_ref[...]
    column = jnp.concatenate([rest_ref[...]] * (block // LANES), axis=1)
    pre = jnp.dot(f_ref[...], stack.astype(BF16), preferred_element_type=F32)
    pre = pre + column * layer[n_exact:n_feat, :]
    hidden_ref[...] = (pre * jax.nn.sigmoid(pre)).astype(BF16)
    stack_t = jnp.transpose(stack)
    last = sum(stack_t[:, p * PITCH + n_exact : p * PITCH + n_feat] for p in range(3))
    pre = jnp.dot(stack_t.astype(BF16), ft_ref[...], preferred_element_type=F32)
    pre = pre + last * rest
    logistic = jax.nn.sigmoid(pre)
    hidden_t_ref[...] = (pre * logistic).astype(BF16)
    gain_t_ref[...] = logistic * (1.0 + pre * (1.0 - logistic))


def hidden_units(run_rows, layer, block=512):
    held, runs = run_rows.shape
    n_feat, hid = layer.shape
    depth = -(-3 * PITCH // LANES) * LANES
    return pl.pallas_call(
        hidden_kernel,
        grid=(hid // block,),
        in_specs=[
            pl.BlockSpec((held, runs), lambda i: (0, 0)),
            pl.BlockSpec((n_feat, block), lambda i: (0, i)),
        ],
        out_specs=[
            pl.BlockSpec((runs, block), lambda i: (0, i)),
            pl.BlockSpec((block, runs), lambda i: (i, 0)),
            pl.BlockSpec((block, runs), lambda i: (i, 0)),
            pl.BlockSpec((runs, LANES), lambda i: (0, 0)),
        ],
        out_shape=[
            jax.ShapeDtypeStruct((runs, hid), BF16),
            jax.ShapeDtypeStruct((hid, runs), BF16),
            jax.ShapeDtypeStruct((hid, runs), F32),
            jax.ShapeDtypeStruct((runs, LANES), BF16),
        ],
        scratch_shapes=[
            pltpu.VMEM((runs, depth), BF16),
            pltpu.VMEM((depth, runs), BF16),
            pltpu.VMEM((runs, LANES), F32),
            pltpu.VMEM((depth, block), F32),
        ],
        cost_estimate=cost(4 * runs * hid * depth, 10 * runs * hid, 4 * runs * hid),
        name="hidden_units",
    )(run_rows, layer)


def predict_kernel(hidden_ref, weight_ref, bias_ref, out_ref):
    out_ref[...] = (
        jnp.dot(hidden_ref[...], weight_ref[...], preferred_element_type=F32) + bias_ref[...]
    )


def predict(hidden, weight, bias, block=512):
    runs, hid = hidden.shape
    cells = weight.shape[1]
    return pl.pallas_call(
        predict_kernel,
        grid=(cells // block,),
        in_specs=[
            pl.BlockSpec((runs, hid), lambda i: (0, 0)),
            pl.BlockSpec((hid, block), lambda i: (0, i)),
            pl.BlockSpec((1, block), lambda i: (0, i)),
        ],
        out_specs=pl.BlockSpec((runs, block), lambda i: (0, i)),
        out_shape=jax.ShapeDtypeStruct((runs, cells), F32),
        cost_estimate=cost(2 * runs * hid * cells, 2 * hid * cells + 4 * runs * cells),
        name="predict",
    )(hidden, weight, bias)


def learn_kernel(last, has_before, scale, sources, *refs):
    grp_ref, guess_ref = refs[:2]
    targets, refs = refs[2 : 2 + sources], refs[2 + sources :]
    weight_ref, bias_ref, gain_any, feats_ref = refs[:4]
    refs = refs[4:]
    if not last:
        hidden_t_ref, refs = refs[0], refs[1:]
    if has_before:
        acc_in_any, refs = refs[2], refs[3 + (not last) :]
    misfit_ref, bias_out_ref, acc_ref, extra_ref = refs[:4]
    back_ref, gain_ref, sem, acc_in_ref = refs[4:8]
    slope_ref = extra_ref if last else refs[8]
    step, steps = pl.program_id(0), pl.num_programs(0)
    load = pltpu.make_async_copy(gain_any, gain_ref, sem.at[0])
    if has_before:
        load_acc = pltpu.make_async_copy(acc_in_any, acc_in_ref, sem.at[1])

    @pl.when(step == 0)
    def _():
        load.start()
        if has_before:
            load_acc.start()
        back_ref[...] = jnp.zeros(back_ref.shape, F32)

    per_source, own = targets[0].shape
    total = jnp.zeros((1, own), F32)
    for offset, target_ref in enumerate(targets):
        at = pl.ds(pl.multiple_of((grp_ref[0] ^ offset) * per_source, per_source), per_source)
        if offset:
            target = target_ref[:, pl.ds(pl.multiple_of(step * own, own), own)]
        else:
            target = target_ref[...]
        error = guess_ref[at, :] - target
        misfit_ref[at, :] = error.astype(BF16)
        slope = (error * scale).astype(BF16)
        slope_ref[at, :] = slope
        total = total + jnp.sum(slope.astype(F32), axis=0, keepdims=True)
    bias_out_ref[...] = bias_ref[...] - 0.5 * total
    slope = slope_ref[...]
    for h in range(0, weight_ref.shape[0], BLOCK):
        at = slice(h, h + BLOCK)
        weight = weight_ref[at, :]
        back_ref[at, :] += lax.dot_general(
            weight, slope, (((1,), (1,)), ((), ())), preferred_element_type=F32
        )
        if not last:
            grad = jnp.dot(hidden_t_ref[at, :], slope, preferred_element_type=F32)
            extra_ref[at, :] = (weight.astype(F32) - 0.5 * grad).astype(BF16)

    @pl.when(step == steps - 1)
    def _():
        load.wait()
        if has_before:
            load_acc.wait()
        feats = feats_ref[...]
        for h in range(0, back_ref.shape[0], BLOCK):
            at = slice(h, h + BLOCK)
            full = back_ref[at, :] * gain_ref[at, :]
            high = full.astype(BF16)
            low = (full - high.astype(F32)).astype(BF16)
            acc = jnp.dot(high, feats, preferred_element_type=F32)
            acc = acc + jnp.dot(low, feats, preferred_element_type=F32)
            if has_before:
                acc = acc + acc_in_ref[at, :]
            if last:
                for t in range(0, BLOCK, LANES):
                    turned = jnp.transpose(acc[t : t + LANES, :])
                    acc_ref[(h + t) // LANES] = turned[: acc_ref.shape[1], :]
            else:
                acc_ref[at, :] = acc


def learn(chunk, chunks, cols, grp, guess, targets, weight, bias, gain_t, feats, hidden_t, before, kept, scale):
    hid, cells = weight.shape
    sources = len(targets)
    per_source, mine = targets[0].shape
    runs = sources * per_source
    own = cols // chunks
    last, has_before = chunk == chunks - 1, before is not None
    strip = lambda i: (0, i * chunks + chunk)
    in_specs = [SCALARS, pl.BlockSpec((runs, own), strip)]
    in_specs += [pl.BlockSpec((per_source, own), lambda i: (0, i))] + [SPACE] * (sources - 1)
    in_specs += [pl.BlockSpec((hid, own), strip), pl.BlockSpec((1, own), strip), ANY, SPACE]
    args = [grp, guess, *targets, weight, bias, gain_t, feats]
    if not last:
        in_specs.append(SPACE)
        args.append(hidden_t)
    aliases = {}
    if has_before:
        aliases = {len(args): 0, len(args) + 1: 1}
        in_specs += [ANY, ANY, ANY]
        args += list(before[:3])
        if not last:
            aliases[len(args)] = 3
            in_specs.append(ANY)
            args.append(before[3])
    acc_shape = (hid // LANES, kept, LANES) if last else (hid, LANES)
    extra = (runs, own, runs) if last else (hid, own, hid)
    scratch = [
        pltpu.VMEM((hid, runs), F32),
        pltpu.VMEM((hid, runs), F32),
        pltpu.SemaphoreType.DMA((2,)),
        pltpu.VMEM((hid, LANES), F32),
    ]
    if not last:
        scratch.append(pltpu.VMEM((runs, own), BF16))
    products = 1 if last else 2
    return pl.pallas_call(
        functools.partial(learn_kernel, last, has_before, scale, sources),
        grid=(mine // own,),
        in_specs=in_specs,
        out_specs=[
            pl.BlockSpec((runs, own), strip),
            pl.BlockSpec((1, own), strip),
            pl.BlockSpec(acc_shape, lambda i: (0,) * len(acc_shape)),
            pl.BlockSpec((extra[0], own), (lambda i: (0, i)) if last else strip),
        ],
        out_shape=[
            jax.ShapeDtypeStruct((runs, cells), BF16),
            jax.ShapeDtypeStruct((1, cells), F32),
            jax.ShapeDtypeStruct(acc_shape, F32),
            jax.ShapeDtypeStruct((runs, mine) if last else (hid, cells), BF16),
        ],
        scratch_shapes=scratch,
        input_output_aliases=aliases,
        cost_estimate=cost(
            2 * runs * hid * (products * mine + 2 * LANES), 2 * hid * mine * products + 12 * runs * mine
        ),
        name="learn",
    )(*args)


def update_kernel(hidden_t_ref, slope_ref, weight_ref, _, out_ref):
    slope = slope_ref[...]
    for h in range(0, weight_ref.shape[0], BLOCK):
        at = slice(h, h + BLOCK)
        grad = jnp.dot(hidden_t_ref[at, :], slope, preferred_element_type=F32)
        out_ref[at, :] = (weight_ref[at, :].astype(F32) - 0.5 * grad).astype(BF16)


def update(first, count, chunks, cols, hidden_t, slope, weight, so_far):
    hid, cells = weight.shape
    runs, _ = slope.shape
    own = cols // chunks
    strip = lambda i: (0, (first + i) * chunks + chunks - 1)
    return pl.pallas_call(
        update_kernel,
        grid=(count,),
        in_specs=[
            pl.BlockSpec((hid, runs), lambda i: (0, 0)),
            pl.BlockSpec((runs, own), lambda i: (0, first + i)),
            pl.BlockSpec((hid, own), strip),
            ANY,
        ],
        out_specs=pl.BlockSpec((hid, own), strip),
        out_shape=jax.ShapeDtypeStruct((hid, cells), BF16),
        input_output_aliases={3: 0},
        cost_estimate=cost(2 * runs * hid * own * count, (4 * hid + 4 * runs) * own * count),
        name="update",
    )(hidden_t, slope, weight, so_far)


def finish_kernel(total_ref, layer_ref, out_ref):
    n_feat = layer_ref.shape[0]
    line = lax.broadcasted_iota(jnp.int32, (n_feat, LANES), 0)
    for t in range(total_ref.shape[0]):
        at = slice(t * LANES, (t + 1) * LANES)
        rest = jnp.broadcast_to(total_ref[t, n_feat : n_feat + 1, :], (n_feat, LANES))
        grad = total_ref[t, :n_feat, :] + jnp.where(line == n_feat - 1, rest, 0.0)
        out_ref[:, at] = layer_ref[:, at] - 2.0 * grad


def finish(total, layer):
    return pl.pallas_call(
        finish_kernel,
        in_specs=[SPACE, SPACE],
        out_specs=SPACE,
        out_shape=jax.ShapeDtypeStruct(layer.shape, F32),
        cost_estimate=cost(3 * layer.size, 12 * layer.size),
        name="finish",
    )(total, layer)


def bits_of(size):
    return [1 << b for b in range(size.bit_length() - 1)]


def halve(x, axis, bit):
    size = lax.axis_size(axis)
    upper = (lax.axis_index(axis) & bit) != 0
    half = x.shape[0] // 2
    kept = lax.dynamic_slice_in_dim(x, jnp.where(upper, half, 0), half, 0)
    sent = lax.dynamic_slice_in_dim(x, jnp.where(upper, 0, half), half, 0)
    return kept + lax.ppermute(sent, axis, [(i, i ^ bit) for i in range(size)])


def rejoin(x, axis, bit):
    size = lax.axis_size(axis)
    upper = (lax.axis_index(axis) & bit) != 0
    other = lax.ppermute(x, axis, [(i, i ^ bit) for i in range(size)])
    return jnp.where(
        upper, jnp.concatenate([other, x], axis=0), jnp.concatenate([x, other], axis=0)
    )


def sum_over_devices(x):
    grp, tile = lax.axis_size("grp"), lax.axis_size("tile")
    for bit in bits_of(grp):
        x = halve(x, "grp", bit)
    for bit in bits_of(tile):
        x = x + lax.ppermute(x, "tile", [(i, i ^ bit) for i in range(tile)])
    for bit in bits_of(grp)[::-1]:
        x = rejoin(x, "grp", bit)
    return x


def on_device(
    start_field, class_ids, run_levels, steepness, step_pick, input_layer, output_layer, output_bias
):
    local_runs, rows, cols = start_field.shape
    n_grp, n_tile = lax.axis_size("grp"), lax.axis_size("tile")
    tile = lax.axis_index("tile")
    first_run = lax.axis_index("grp") * local_runs
    chunks = CHUNKS
    parts = spans(cols, chunks)
    runs_total, classes = run_levels.shape
    n_feat, _ = input_layer.shape

    up = [(i, i + 1) for i in range(n_tile - 1)]
    down = [(j, i) for i, j in up]
    packed = pack_edges(start_field, class_ids, parts)
    edges = []
    for c in range(chunks):
        top, bottom = packed[2 * c], packed[2 * c + 1]
        above = lax.ppermute(bottom, "tile", up)
        below = lax.ppermute(top, "tile", down)
        edges.append((in_vmem(above), in_vmem(below)))

    run_rows = jnp.concatenate(
        [
            run_levels.T.astype(F32),
            step_pick[None, :].astype(F32),
            steepness[None, :],
            jnp.zeros((2 * LEVELS - classes - 2, runs_total), F32),
        ],
        axis=0,
    )
    run_rows_here = lax.dynamic_slice_in_dim(run_rows, first_run, local_runs, 1)
    ends = jnp.stack([(tile > 0).astype(F32), (tile < n_tile - 1).astype(F32)])
    hidden, hidden_t, gain_t, project = hidden_units(run_rows, input_layer)
    bias_row = output_bias[None, :]
    guess = predict(hidden, output_layer, bias_row)
    kept = -(-(n_feat + 1) // SUB) * SUB

    state = None
    scale = 2.0 / runs_total
    grp = lax.axis_index("grp").astype(jnp.int32)[None]
    for c in range(chunks):
        snaps = diffuse(c, chunks, start_field, edges, class_ids, run_rows_here, ends, grp, n_grp)
        targets = [snaps[0]]
        for offset in range(1, n_grp):
            pairs = [(i, i ^ offset) for i in range(n_grp)]
            targets.append(in_vmem(lax.ppermute(snaps[offset], "grp", pairs)))
        before = state
        state = learn(
            c, chunks, cols, grp, guess, targets, output_layer, bias_row,
            gain_t, project, hidden_t, before, kept, scale,
        )
    misfit, bias_next, partial, slope = state
    output_next, strips = before[3], rows // n_grp
    for part in range(UPDATES):
        first, past = part * strips // UPDATES, (part + 1) * strips // UPDATES
        output_next = update(
            first, past - first, chunks, cols, hidden_t, slope, output_layer, output_next
        )
    total = sum_over_devices(partial.reshape(-1, LANES)).reshape(partial.shape)
    input_next = finish(total, input_layer)
    return misfit, output_next, bias_next.reshape(-1), input_next


def solution(mesh):
    in_specs = (
        P("grp", "tile", None),
        P("tile", None),
        P(),
        P(),
        P(),
        P(),
        P(None, ("grp", "tile")),
        P(("grp", "tile")),
    )
    out_specs = (P(None, ("grp", "tile")), P(None, ("grp", "tile")), P(("grp", "tile")), P())

    return jax.shard_map(on_device, mesh=mesh, in_specs=in_specs, out_specs=out_specs, check_vma=False)
```

```python
import functools

import jax
import jax.numpy as jnp
from jax import lax
from jax.experimental import pallas as pl
from jax.experimental.pallas import tpu as pltpu
from jax.sharding import PartitionSpec as P


STEPS = 4
LEVELS = 8
LANES = 128
SUB = 8
BLOCK = 256
CHUNKS = 2
UPDATES = 2
F32 = jnp.float32
BF16 = jnp.bfloat16
SPACE = pl.BlockSpec(memory_space=pltpu.VMEM)
ANY = pl.BlockSpec(memory_space=pl.ANY)
SCALARS = pl.BlockSpec(memory_space=pltpu.SMEM)


def in_vmem(x):
    return pltpu.with_memory_space_constraint(x, pltpu.VMEM)


def cost(flops, nbytes, transcendentals=0):
    return pl.CostEstimate(
        flops=int(flops), bytes_accessed=int(nbytes), transcendentals=int(transcendentals)
    )


def spans(cols, chunks):
    width = cols // chunks
    out = []
    for c in range(chunks):
        low = max(c * width - SUB, 0)
        high = min((c + 1) * width + SUB, cols)
        sent = 0 if c == 0 else c * width + SUB
        out.append((low, high, sent))
    return out


def pack_kernel(chunk, part, field_ref, ids_ref, *outs):
    rows, cols = ids_ref.shape
    _, high, sent = part
    for j in range(sent // LANES, -(-high // LANES)):

        @pl.when(pl.program_id(0) == j - sent // LANES)
        def _(j=j):
            first, last = max(sent, j * LANES), min(high, (j + 1) * LANES)
            for side in range(2):
                for r in range(STEPS):
                    row = r if side == 0 else rows - STEPS + r
                    tile = jnp.transpose(field_ref[:, row, :])
                    at = r * (high - sent) + first - sent
                    outs[side][at : at + last - first, :] = tile[
                        first - j * LANES : last - j * LANES, :
                    ]

    @pl.when(pl.program_id(0) == 0)
    def _():
        if chunk == 0:
            for side in range(2):
                for r in range(STEPS):
                    row = r if side == 0 else rows - STEPS + r
                    for j in range(cols // LANES):
                        at = STEPS * (high - sent) + r * (cols // LANES) + j
                        outs[side][at : at + 1, :] = ids_ref[
                            row : row + 1, j * LANES : (j + 1) * LANES
                        ].astype(F32)


def pack_edges(chunk, start_field, ids, parts):
    runs, rows, cols = start_field.shape
    _, high, sent = parts[chunk]
    extra = STEPS * cols // LANES if chunk == 0 else 0
    shapes = [jax.ShapeDtypeStruct((STEPS * (high - sent) + extra, runs), F32)] * 2
    tile0, tile1 = sent // LANES, -(-high // LANES)
    return pl.pallas_call(
        functools.partial(pack_kernel, chunk, parts[chunk]),
        grid=(tile1 - tile0,),
        in_specs=[
            pl.BlockSpec((runs, rows, LANES), lambda j: (0, 0, tile0 + j)),
            pl.BlockSpec((rows, cols), lambda j: (0, 0)),
        ],
        out_specs=[pl.BlockSpec(x.shape, lambda j: (0, 0)) for x in shapes],
        out_shape=shapes,
        cost_estimate=cost(0, 6 * runs * rows * (high - sent)),
        name="pack_edges",
    )(start_field, ids)


def diffuse_kernel(chunk, chunks, ends_ref, grp_ref, field_ref, ids_ref, runs_ref, *refs):
    edges, outs = refs[: 2 + 2 * (chunk > 0)], refs[2 + 2 * (chunk > 0) : -11]
    raw_ref, u0_ref, u1_ref, d_ref, a_ref, b_ref, fx_ref, v_ref, wide_ref, made_ref, sem = refs[-11:]
    rows, cols = ids_ref.shape
    total = rows + 2 * STEPS
    parts = spans(cols, chunks)
    low, high, sent = parts[chunk]
    width = high - low
    own = cols // chunks
    tile0, tile1 = low // LANES, -(-high // LANES)
    copy = pltpu.make_async_copy(field_ref.at[:, :, tile0 * LANES : tile1 * LANES], raw_ref, sem.at[0])
    copy.start()
    brought = STEPS * (parts[0][1] - parts[0][2])
    for j in range(tile0, tile1):
        at = slice(j * LANES, (j + 1) * LANES)
        for side in range(2):
            for r in range(STEPS):
                line = brought + r * (cols // LANES) + j
                wide_ref[side * (total - STEPS) + r, :, at] = edges[side - 2][line : line + 1, :]
        for r in range(rows):
            wide_ref[STEPS + r, :, at] = ids_ref[r : r + 1, at].astype(F32)

    level, pick, steep = runs_ref[0:LEVELS], runs_ref[LEVELS : LEVELS + 1], runs_ref[LEVELS + 1 : LEVELS + 2]
    table = 0.03 * jnp.exp(level * jnp.log(F32(1.35)))
    both = jnp.concatenate([table * (0.5 * steep), table * (0.5 * (1.0 - steep))], axis=1)
    pieces = []
    for _ in range(3):
        piece = both.astype(BF16).astype(F32)
        pieces.append(piece)
        both = both - piece
    pieces.append(jnp.zeros_like(both))
    tables = jnp.concatenate(pieces, axis=0).astype(BF16)
    klass = (lax.broadcasted_iota(jnp.int32, (4 * LEVELS, LANES), 0) % LEVELS).astype(F32)
    pick8 = jnp.broadcast_to(pick, (SUB, LANES))
    has_top, has_bottom = ends_ref[0], ends_ref[1]
    zeros = jnp.zeros((SUB, LANES), F32)

    def inside(r):
        return jnp.where(r < STEPS, has_top, jnp.where(r >= total - STEPS, has_bottom, 1.0))

    def coefficients(r, carry):
        valid = inside(r)
        ids = wide_ref[r]
        for j in range(tile0, tile1):
            here = jnp.broadcast_to(ids[:, j * LANES : (j + 1) * LANES], klass.shape)
            onehot = jnp.where(here == klass, valid, 0.0)
            ab = lax.dot_general(
                onehot.astype(BF16), tables, (((0,), (0,)), ((), ())), preferred_element_type=F32
            )
            first, last = max(low, j * LANES), min(high, (j + 1) * LANES)
            at, of = slice(first - low, last - low), slice(first - j * LANES, last - j * LANES)
            a_ref[r, at, :] = ab[of, :LANES]
            b_ref[r, at, :] = ab[of, LANES:]
        for ref in (u0_ref, u1_ref, d_ref):
            ref[r, 0:SUB, :] = zeros
            ref[r, SUB + width : 2 * SUB + width, :] = zeros
        return carry

    lax.fori_loop(0, total, coefficients, 0, unroll=4)

    for side in range(2):
        here = edges[side]
        for r in range(STEPS):
            row = r if side == 0 else total - STEPS + r
            n = high - sent
            at = SUB + sent - low
            u0_ref[row, at : at + n, :] = here[r * n : (r + 1) * n, :]
            if chunk:
                prior = edges[2 + side]
                n0 = parts[chunk - 1][1] - parts[chunk - 1][2]
                m = sent - low
                u0_ref[row, SUB : SUB + m, :] = prior[(r + 1) * n0 - m : (r + 1) * n0, :]
    copy.wait()
    for i in range(rows):
        for j in range(tile0, tile1):
            tile = jnp.transpose(raw_ref[:, i, (j - tile0) * LANES : (j - tile0 + 1) * LANES])
            first, last = max(low, j * LANES), min(high, (j + 1) * LANES)
            at = SUB + first - low
            u0_ref[STEPS + i, at : at + last - first, :] = tile[first - j * LANES : last - j * LANES, :]

    blocks = range(width // SUB)
    for step in range(1, STEPS + 1):
        src, dst = (u0_ref, u1_ref) if step % 2 else (u1_ref, u0_ref)

        def conduct(r, k, u, src=src):
            at = slice(k * SUB, (k + 1) * SUB)
            d = a_ref[r, at, :] + b_ref[r, at, :] * (1.0 / (1.0 + u * u))
            d_ref[r, SUB + k * SUB : 2 * SUB + k * SUB, :] = d
            return d

        top = step - 1
        for k in blocks:
            at = slice(SUB + k * SUB, 2 * SUB + k * SUB)
            u, un = src[top, at, :], src[top + 1, at, :]
            d, dn = conduct(top, k, u), conduct(top + 1, k, un)
            v_ref[k * SUB : (k + 1) * SUB, :] = (d + dn) * (un - u)

        def advance(r, carry, src=src, dst=dst, step=step, conduct=conduct):
            active = pick8 >= jnp.where(inside(r) > 0.0, F32(step), F32(2 * STEPS))
            for k in range(-1, width // SUB):
                p = SUB + k * SUB
                u, d = src[r, p : p + SUB, :], d_ref[r, p : p + SUB, :]
                flux = (d + d_ref[r, p + 1 : p + 1 + SUB, :]) * (src[r, p + 1 : p + 1 + SUB, :] - u)
                fx_ref[p : p + SUB, :] = flux
                if k < 0:
                    continue
                at = slice(k * SUB, (k + 1) * SUB)
                un = src[r + 1, p : p + SUB, :]
                dn = conduct(r + 1, k, un)
                down = (d + dn) * (un - u)
                across = flux - fx_ref[p - 1 : p - 1 + SUB, :]
                new = u + across + (down - v_ref[at, :])
                v_ref[at, :] = down
                dst[r, p : p + SUB, :] = jnp.where(active, new, u)
            return carry

        lax.fori_loop(step, total - step, advance, 0)

    result = u0_ref if STEPS % 2 == 0 else u1_ref
    per_block = rows // len(outs)
    done = []
    for offset in list(range(1, len(outs))) + [0]:
        row = STEPS + (grp_ref[0] ^ offset) * per_block
        for i in range(per_block):
            for j in range(own // LANES):
                p = SUB + chunk * own + j * LANES - low
                at = i * own + j * LANES
                made_ref[offset, :, at : at + LANES] = jnp.transpose(result[row + i, p : p + LANES, :])
        done.append(pltpu.make_async_copy(made_ref.at[offset], outs[offset], sem.at[1 + offset]))
        done[-1].start()
    for sent_out in done:
        sent_out.wait()


def diffuse(chunk, chunks, start_field, edges, ids, run_rows, ends, grp, blocks):
    runs, rows, cols = start_field.shape
    total = rows + 2 * STEPS
    low, high, _ = spans(cols, chunks)[chunk]
    width = high - low
    tiles = -(-high // LANES) - low // LANES
    own = cols // chunks
    edges = list(edges[chunk]) + (list(edges[chunk - 1]) if chunk else [])
    state = pltpu.VMEM((total, width + 2 * SUB, runs), F32)
    return pl.pallas_call(
        functools.partial(diffuse_kernel, chunk, chunks),
        in_specs=[SCALARS, SCALARS, ANY, SPACE, SPACE] + [SPACE] * len(edges),
        out_specs=[ANY] * blocks,
        out_shape=[jax.ShapeDtypeStruct((runs, rows * own // blocks), F32)] * blocks,
        scratch_shapes=[
            pltpu.VMEM((runs, rows, tiles * LANES), F32),
            state,
            state,
            state,
            pltpu.VMEM((total, width, runs), F32),
            pltpu.VMEM((total, width, runs), F32),
            pltpu.VMEM((width + 2 * SUB, runs), F32),
            pltpu.VMEM((width, runs), F32),
            pltpu.VMEM((total, 1, cols), F32),
            pltpu.VMEM((blocks, runs, rows * own // blocks), F32),
            pltpu.SemaphoreType.DMA((blocks + 1,)),
        ],
        cost_estimate=cost(100 * runs * total * width, 12 * runs * total * width),
        name="diffuse",
    )(ends, grp, start_field, ids, run_rows, *edges)


PITCH = 80


def hidden_kernel(
    runs_ref, layer_ref, hidden_ref, hidden_t_ref, gain_t_ref, project_ref, f_ref, ft_ref, rest_ref, stack_ref
):
    depth, runs = ft_ref.shape
    n_feat, block = layer_ref.shape
    n_exact = n_feat - 1
    steep = runs_ref[LEVELS + 1 : LEVELS + 2]
    rest = steep - steep.astype(BF16).astype(F32)

    @pl.when(pl.program_id(0) == 0)
    def _():
        held = runs_ref[...]
        row = lax.broadcasted_iota(jnp.int32, (depth, held.shape[0]), 0)
        col = lax.broadcasted_iota(jnp.int32, (depth, held.shape[0]), 1)

        def place(row):
            return jnp.where(row < 3 * PITCH, row % PITCH, PITCH)

        n_level = LEVELS * LEVELS
        at = place(row)
        source = jnp.where(
            at < n_level,
            at // LEVELS,
            jnp.where(at < n_exact, LEVELS, jnp.where(at == n_exact, LEVELS + 1, -1)),
        )
        spread = jnp.where(col == source, 1.0, 0.0).astype(BF16)
        value = jnp.dot(spread, held.astype(BF16), preferred_element_type=F32)
        at = place(lax.broadcasted_iota(jnp.int32, (depth, runs), 0))
        wanted = jnp.where(at < n_level, at % LEVELS, at - n_level + 1).astype(F32)
        feats = jnp.where(at < n_exact, jnp.where(value == wanted, 1.0, 0.0), value)
        ft_ref[...] = feats.astype(BF16)
        f_ref[...] = jnp.transpose(feats).astype(BF16)
        line = lax.broadcasted_iota(jnp.int32, (LANES, runs), 0)
        wide_rest = jnp.broadcast_to(rest, (LANES, runs))
        project = jnp.where(
            line < n_feat, feats[:LANES], jnp.where(line == n_feat, wide_rest, 0.0)
        )
        project_ref[...] = jnp.transpose(project).astype(BF16)
        rest_ref[...] = jnp.transpose(wide_rest)
        stack_ref[...] = jnp.zeros(stack_ref.shape, F32)

    layer = layer_ref[...]
    left = layer
    for piece in range(3):
        part = left.astype(BF16).astype(F32)
        stack_ref[piece * PITCH : piece * PITCH + n_feat, :] = part
        left = left - part
    stack = stack_ref[...]
    column = jnp.concatenate([rest_ref[...]] * (block // LANES), axis=1)
    pre = jnp.dot(f_ref[...], stack.astype(BF16), preferred_element_type=F32)
    pre = pre + column * layer[n_exact:n_feat, :]
    hidden_ref[...] = (pre * jax.nn.sigmoid(pre)).astype(BF16)
    stack_t = jnp.transpose(stack)
    last = sum(stack_t[:, p * PITCH + n_exact : p * PITCH + n_feat] for p in range(3))
    pre = jnp.dot(stack_t.astype(BF16), ft_ref[...], preferred_element_type=F32)
    pre = pre + last * rest
    logistic = jax.nn.sigmoid(pre)
    hidden_t_ref[...] = (pre * logistic).astype(BF16)
    gain_t_ref[...] = logistic * (1.0 + pre * (1.0 - logistic))


def hidden_units(run_rows, layer, block=512):
    held, runs = run_rows.shape
    n_feat, hid = layer.shape
    depth = -(-3 * PITCH // LANES) * LANES
    return pl.pallas_call(
        hidden_kernel,
        grid=(hid // block,),
        in_specs=[
            pl.BlockSpec((held, runs), lambda i: (0, 0)),
            pl.BlockSpec((n_feat, block), lambda i: (0, i)),
        ],
        out_specs=[
            pl.BlockSpec((runs, block), lambda i: (0, i)),
            pl.BlockSpec((block, runs), lambda i: (i, 0)),
            pl.BlockSpec((block, runs), lambda i: (i, 0)),
            pl.BlockSpec((runs, LANES), lambda i: (0, 0)),
        ],
        out_shape=[
            jax.ShapeDtypeStruct((runs, hid), BF16),
            jax.ShapeDtypeStruct((hid, runs), BF16),
            jax.ShapeDtypeStruct((hid, runs), F32),
            jax.ShapeDtypeStruct((runs, LANES), BF16),
        ],
        scratch_shapes=[
            pltpu.VMEM((runs, depth), BF16),
            pltpu.VMEM((depth, runs), BF16),
            pltpu.VMEM((runs, LANES), F32),
            pltpu.VMEM((depth, block), F32),
        ],
        cost_estimate=cost(4 * runs * hid * depth, 10 * runs * hid, 4 * runs * hid),
        name="hidden_units",
    )(run_rows, layer)


def predict_kernel(hidden_ref, weight_ref, bias_ref, out_ref):
    out_ref[...] = (
        jnp.dot(hidden_ref[...], weight_ref[...], preferred_element_type=F32) + bias_ref[...]
    )


def predict(hidden, weight, bias, block=512):
    runs, hid = hidden.shape
    cells = weight.shape[1]
    return pl.pallas_call(
        predict_kernel,
        grid=(cells // block,),
        in_specs=[
            pl.BlockSpec((runs, hid), lambda i: (0, 0)),
            pl.BlockSpec((hid, block), lambda i: (0, i)),
            pl.BlockSpec((1, block), lambda i: (0, i)),
        ],
        out_specs=pl.BlockSpec((runs, block), lambda i: (0, i)),
        out_shape=jax.ShapeDtypeStruct((runs, cells), F32),
        cost_estimate=cost(2 * runs * hid * cells, 2 * hid * cells + 4 * runs * cells),
        name="predict",
    )(hidden, weight, bias)


def learn_kernel(last, has_before, scale, sources, *refs):
    grp_ref, guess_ref = refs[:2]
    targets, refs = refs[2 : 2 + sources], refs[2 + sources :]
    weight_ref, bias_ref, gain_any, feats_ref = refs[:4]
    refs = refs[4:]
    if not last:
        hidden_t_ref, refs = refs[0], refs[1:]
    if has_before:
        acc_in_any, refs = refs[2], refs[3 + (not last) :]
    misfit_ref, bias_out_ref, acc_ref, extra_ref = refs[:4]
    back_ref, gain_ref, sem, acc_in_ref = refs[4:8]
    slope_ref = extra_ref if last else refs[8]
    step, steps = pl.program_id(0), pl.num_programs(0)
    load = pltpu.make_async_copy(gain_any, gain_ref, sem.at[0])
    if has_before:
        load_acc = pltpu.make_async_copy(acc_in_any, acc_in_ref, sem.at[1])

    @pl.when(step == 0)
    def _():
        load.start()
        if has_before:
            load_acc.start()
        back_ref[...] = jnp.zeros(back_ref.shape, F32)

    per_source, own = targets[0].shape
    total = jnp.zeros((1, own), F32)
    for offset, target_ref in enumerate(targets):
        at = pl.ds(pl.multiple_of((grp_ref[0] ^ offset) * per_source, per_source), per_source)
        if offset:
            target = target_ref[:, pl.ds(pl.multiple_of(step * own, own), own)]
        else:
            target = target_ref[...]
        error = guess_ref[at, :] - target
        misfit_ref[at, :] = error.astype(BF16)
        slope = (error * scale).astype(BF16)
        slope_ref[at, :] = slope
        total = total + jnp.sum(slope.astype(F32), axis=0, keepdims=True)
    bias_out_ref[...] = bias_ref[...] - 0.5 * total
    slope = slope_ref[...]
    for h in range(0, weight_ref.shape[0], BLOCK):
        at = slice(h, h + BLOCK)
        weight = weight_ref[at, :]
        back_ref[at, :] += lax.dot_general(
            weight, slope, (((1,), (1,)), ((), ())), preferred_element_type=F32
        )
        if not last:
            grad = jnp.dot(hidden_t_ref[at, :], slope, preferred_element_type=F32)
            extra_ref[at, :] = (weight.astype(F32) - 0.5 * grad).astype(BF16)

    @pl.when(step == steps - 1)
    def _():
        load.wait()
        if has_before:
            load_acc.wait()
        feats = feats_ref[...]
        for h in range(0, back_ref.shape[0], BLOCK):
            at = slice(h, h + BLOCK)
            full = back_ref[at, :] * gain_ref[at, :]
            high = full.astype(BF16)
            low = (full - high.astype(F32)).astype(BF16)
            acc = jnp.dot(high, feats, preferred_element_type=F32)
            acc = acc + jnp.dot(low, feats, preferred_element_type=F32)
            if has_before:
                acc = acc + acc_in_ref[at, :]
            if last:
                for t in range(0, BLOCK, LANES):
                    turned = jnp.transpose(acc[t : t + LANES, :])
                    acc_ref[(h + t) // LANES] = turned[: acc_ref.shape[1], :]
            else:
                acc_ref[at, :] = acc


def learn(chunk, chunks, cols, grp, guess, targets, weight, bias, gain_t, feats, hidden_t, before, kept, scale):
    hid, cells = weight.shape
    sources = len(targets)
    per_source, mine = targets[0].shape
    runs = sources * per_source
    own = cols // chunks
    last, has_before = chunk == chunks - 1, before is not None
    strip = lambda i: (0, i * chunks + chunk)
    in_specs = [SCALARS, pl.BlockSpec((runs, own), strip)]
    in_specs += [pl.BlockSpec((per_source, own), lambda i: (0, i))] + [SPACE] * (sources - 1)
    in_specs += [pl.BlockSpec((hid, own), strip), pl.BlockSpec((1, own), strip), ANY, SPACE]
    args = [grp, guess, *targets, weight, bias, gain_t, feats]
    if not last:
        in_specs.append(SPACE)
        args.append(hidden_t)
    aliases = {}
    if has_before:
        aliases = {len(args): 0, len(args) + 1: 1}
        in_specs += [ANY, ANY, ANY]
        args += list(before[:3])
        if not last:
            aliases[len(args)] = 3
            in_specs.append(ANY)
            args.append(before[3])
    acc_shape = (hid // LANES, kept, LANES) if last else (hid, LANES)
    extra = (runs, own, runs) if last else (hid, own, hid)
    scratch = [
        pltpu.VMEM((hid, runs), F32),
        pltpu.VMEM((hid, runs), F32),
        pltpu.SemaphoreType.DMA((2,)),
        pltpu.VMEM((hid, LANES), F32),
    ]
    if not last:
        scratch.append(pltpu.VMEM((runs, own), BF16))
    products = 1 if last else 2
    return pl.pallas_call(
        functools.partial(learn_kernel, last, has_before, scale, sources),
        grid=(mine // own,),
        in_specs=in_specs,
        out_specs=[
            pl.BlockSpec((runs, own), strip),
            pl.BlockSpec((1, own), strip),
            pl.BlockSpec(acc_shape, lambda i: (0,) * len(acc_shape)),
            pl.BlockSpec((extra[0], own), (lambda i: (0, i)) if last else strip),
        ],
        out_shape=[
            jax.ShapeDtypeStruct((runs, cells), BF16),
            jax.ShapeDtypeStruct((1, cells), F32),
            jax.ShapeDtypeStruct(acc_shape, F32),
            jax.ShapeDtypeStruct((runs, mine) if last else (hid, cells), BF16),
        ],
        scratch_shapes=scratch,
        input_output_aliases=aliases,
        cost_estimate=cost(
            2 * runs * hid * (products * mine + 2 * LANES), 2 * hid * mine * products + 12 * runs * mine
        ),
        name="learn",
    )(*args)


def update_kernel(hidden_t_ref, slope_ref, weight_ref, _, out_ref):
    slope = slope_ref[...]
    for h in range(0, weight_ref.shape[0], BLOCK):
        at = slice(h, h + BLOCK)
        grad = jnp.dot(hidden_t_ref[at, :], slope, preferred_element_type=F32)
        out_ref[at, :] = (weight_ref[at, :].astype(F32) - 0.5 * grad).astype(BF16)


def update(first, count, chunks, cols, hidden_t, slope, weight, so_far):
    hid, cells = weight.shape
    runs, _ = slope.shape
    own = cols // chunks
    strip = lambda i: (0, (first + i) * chunks + chunks - 1)
    return pl.pallas_call(
        update_kernel,
        grid=(count,),
        in_specs=[
            pl.BlockSpec((hid, runs), lambda i: (0, 0)),
            pl.BlockSpec((runs, own), lambda i: (0, first + i)),
            pl.BlockSpec((hid, own), strip),
            ANY,
        ],
        out_specs=pl.BlockSpec((hid, own), strip),
        out_shape=jax.ShapeDtypeStruct((hid, cells), BF16),
        input_output_aliases={3: 0},
        cost_estimate=cost(2 * runs * hid * own * count, (4 * hid + 4 * runs) * own * count),
        name="update",
    )(hidden_t, slope, weight, so_far)


def finish_kernel(total_ref, layer_ref, out_ref):
    n_feat = layer_ref.shape[0]
    line = lax.broadcasted_iota(jnp.int32, (n_feat, LANES), 0)
    for t in range(total_ref.shape[0]):
        at = slice(t * LANES, (t + 1) * LANES)
        rest = jnp.broadcast_to(total_ref[t, n_feat : n_feat + 1, :], (n_feat, LANES))
        grad = total_ref[t, :n_feat, :] + jnp.where(line == n_feat - 1, rest, 0.0)
        out_ref[:, at] = layer_ref[:, at] - 2.0 * grad


def finish(total, layer):
    return pl.pallas_call(
        finish_kernel,
        in_specs=[SPACE, SPACE],
        out_specs=SPACE,
        out_shape=jax.ShapeDtypeStruct(layer.shape, F32),
        cost_estimate=cost(3 * layer.size, 12 * layer.size),
        name="finish",
    )(total, layer)


def bits_of(size):
    return [1 << b for b in range(size.bit_length() - 1)]


def halve(x, axis, bit):
    size = lax.axis_size(axis)
    upper = (lax.axis_index(axis) & bit) != 0
    half = x.shape[0] // 2
    kept = lax.dynamic_slice_in_dim(x, jnp.where(upper, half, 0), half, 0)
    sent = lax.dynamic_slice_in_dim(x, jnp.where(upper, 0, half), half, 0)
    return kept + lax.ppermute(sent, axis, [(i, i ^ bit) for i in range(size)])


def rejoin(x, axis, bit):
    size = lax.axis_size(axis)
    upper = (lax.axis_index(axis) & bit) != 0
    other = lax.ppermute(x, axis, [(i, i ^ bit) for i in range(size)])
    return jnp.where(
        upper, jnp.concatenate([other, x], axis=0), jnp.concatenate([x, other], axis=0)
    )


def sum_over_devices(x):
    grp, tile = lax.axis_size("grp"), lax.axis_size("tile")
    for bit in bits_of(grp):
        x = halve(x, "grp", bit)
    for bit in bits_of(tile):
        x = x + lax.ppermute(x, "tile", [(i, i ^ bit) for i in range(tile)])
    for bit in bits_of(grp)[::-1]:
        x = rejoin(x, "grp", bit)
    return x


def on_device(
    start_field, class_ids, run_levels, steepness, step_pick, input_layer, output_layer, output_bias
):
    local_runs, rows, cols = start_field.shape
    n_grp, n_tile = lax.axis_size("grp"), lax.axis_size("tile")
    tile = lax.axis_index("tile")
    first_run = lax.axis_index("grp") * local_runs
    chunks = CHUNKS
    parts = spans(cols, chunks)
    runs_total, classes = run_levels.shape
    n_feat, _ = input_layer.shape

    up = [(i, i + 1) for i in range(n_tile - 1)]
    down = [(j, i) for i, j in up]
    edges = []
    for c in range(chunks):
        top, bottom = pack_edges(c, start_field, class_ids, parts)
        above = lax.ppermute(bottom, "tile", up)
        below = lax.ppermute(top, "tile", down)
        edges.append((in_vmem(above), in_vmem(below)))

    run_rows = jnp.concatenate(
        [
            run_levels.T.astype(F32),
            step_pick[None, :].astype(F32),
            steepness[None, :],
            jnp.zeros((2 * LEVELS - classes - 2, runs_total), F32),
        ],
        axis=0,
    )
    run_rows_here = lax.dynamic_slice_in_dim(run_rows, first_run, local_runs, 1)
    ends = jnp.stack([(tile > 0).astype(F32), (tile < n_tile - 1).astype(F32)])
    hidden, hidden_t, gain_t, project = hidden_units(run_rows, input_layer)
    bias_row = output_bias[None, :]
    guess = predict(hidden, output_layer, bias_row)
    kept = -(-(n_feat + 1) // SUB) * SUB

    state = None
    scale = 2.0 / runs_total
    grp = lax.axis_index("grp").astype(jnp.int32)[None]
    for c in range(chunks):
        snaps = diffuse(c, chunks, start_field, edges, class_ids, run_rows_here, ends, grp, n_grp)
        targets = [snaps[0]]
        for offset in range(1, n_grp):
            pairs = [(i, i ^ offset) for i in range(n_grp)]
            targets.append(in_vmem(lax.ppermute(snaps[offset], "grp", pairs)))
        before = state
        state = learn(
            c, chunks, cols, grp, guess, targets, output_layer, bias_row,
            gain_t, project, hidden_t, before, kept, scale,
        )
    misfit, bias_next, partial, slope = state
    output_next, strips = before[3], rows // n_grp
    for part in range(UPDATES):
        first, past = part * strips // UPDATES, (part + 1) * strips // UPDATES
        output_next = update(
            first, past - first, chunks, cols, hidden_t, slope, output_layer, output_next
        )
    total = sum_over_devices(partial.reshape(-1, LANES)).reshape(partial.shape)
    input_next = finish(in_vmem(total), in_vmem(input_layer))
    return misfit, output_next, bias_next.reshape(-1), input_next


def solution(mesh):
    in_specs = (
        P("grp", "tile", None),
        P("tile", None),
        P(),
        P(),
        P(),
        P(),
        P(None, ("grp", "tile")),
        P(("grp", "tile")),
    )
    out_specs = (P(None, ("grp", "tile")), P(None, ("grp", "tile")), P(("grp", "tile")), P())

    return jax.shard_map(on_device, mesh=mesh, in_specs=in_specs, out_specs=out_specs, check_vma=False)
```

```python
import functools

import jax
import jax.numpy as jnp
from jax import lax
from jax.experimental import pallas as pl
from jax.experimental.pallas import tpu as pltpu
from jax.sharding import PartitionSpec as P


STEPS = 4
LEVELS = 8
LANES = 128
SUB = 8
BLOCK = 256
CHUNKS = 2
UPDATES = 2
F32 = jnp.float32
BF16 = jnp.bfloat16
SPACE = pl.BlockSpec(memory_space=pltpu.VMEM)
ANY = pl.BlockSpec(memory_space=pl.ANY)
SCALARS = pl.BlockSpec(memory_space=pltpu.SMEM)


def in_vmem(x):
    return pltpu.with_memory_space_constraint(x, pltpu.VMEM)


def cost(flops, nbytes, transcendentals=0):
    return pl.CostEstimate(
        flops=int(flops), bytes_accessed=int(nbytes), transcendentals=int(transcendentals)
    )


def spans(cols, chunks):
    width = cols // chunks
    out = []
    for c in range(chunks):
        low = max(c * width - SUB, 0)
        high = min((c + 1) * width + SUB, cols)
        sent = 0 if c == 0 else c * width + SUB
        out.append((low, high, sent))
    return out


def pack_kernel(chunk, part, field_ref, ids_ref, *outs):
    rows, cols = ids_ref.shape
    _, high, sent = part
    for j in range(sent // LANES, -(-high // LANES)):

        @pl.when(pl.program_id(0) == j - sent // LANES)
        def _(j=j):
            first, last = max(sent, j * LANES), min(high, (j + 1) * LANES)
            for side in range(2):
                for r in range(STEPS):
                    row = r if side == 0 else rows - STEPS + r
                    tile = jnp.transpose(field_ref[:, row, :])
                    at = r * (high - sent) + first - sent
                    outs[side][at : at + last - first, :] = tile[
                        first - j * LANES : last - j * LANES, :
                    ]

    @pl.when(pl.program_id(0) == 0)
    def _():
        if chunk == 0:
            for side in range(2):
                for r in range(STEPS):
                    row = r if side == 0 else rows - STEPS + r
                    for j in range(cols // LANES):
                        at = STEPS * (high - sent) + r * (cols // LANES) + j
                        outs[side][at : at + 1, :] = ids_ref[
                            row : row + 1, j * LANES : (j + 1) * LANES
                        ].astype(F32)


def pack_edges(chunk, start_field, ids, parts):
    runs, rows, cols = start_field.shape
    _, high, sent = parts[chunk]
    extra = STEPS * cols // LANES if chunk == 0 else 0
    shapes = [jax.ShapeDtypeStruct((STEPS * (high - sent) + extra, runs), F32)] * 2
    tile0, tile1 = sent // LANES, -(-high // LANES)
    return pl.pallas_call(
        functools.partial(pack_kernel, chunk, parts[chunk]),
        grid=(tile1 - tile0,),
        in_specs=[
            pl.BlockSpec((runs, rows, LANES), lambda j: (0, 0, tile0 + j)),
            pl.BlockSpec((rows, cols), lambda j: (0, 0)),
        ],
        out_specs=[pl.BlockSpec(x.shape, lambda j: (0, 0)) for x in shapes],
        out_shape=shapes,
        cost_estimate=cost(0, 6 * runs * rows * (high - sent)),
        name="pack_edges",
    )(start_field, ids)


def diffuse_kernel(chunk, chunks, n_tile, tile_ref, grp_ref, field_ref, ids_ref, runs_ref, *refs):
    edges, outs = refs[: 2 + 2 * (chunk > 0)], refs[2 + 2 * (chunk > 0) : -11]
    raw_ref, u0_ref, u1_ref, d_ref, a_ref, b_ref, fx_ref, v_ref, wide_ref, made_ref, sem = refs[-11:]
    rows, cols = ids_ref.shape
    total = rows + 2 * STEPS
    parts = spans(cols, chunks)
    low, high, sent = parts[chunk]
    width = high - low
    own = cols // chunks
    tile0, tile1 = low // LANES, -(-high // LANES)
    copy = pltpu.make_async_copy(field_ref.at[:, :, tile0 * LANES : tile1 * LANES], raw_ref, sem.at[0])
    copy.start()
    brought = STEPS * (parts[0][1] - parts[0][2])
    for j in range(tile0, tile1):
        at = slice(j * LANES, (j + 1) * LANES)
        for side in range(2):
            for r in range(STEPS):
                line = brought + r * (cols // LANES) + j
                wide_ref[side * (total - STEPS) + r, :, at] = edges[side - 2][line : line + 1, :]
        for r in range(rows):
            wide_ref[STEPS + r, :, at] = ids_ref[r : r + 1, at].astype(F32)

    mine = pl.ds(pl.multiple_of(grp_ref[0] * LANES, LANES), LANES)
    level, pick, steep = (
        runs_ref[0:LEVELS, mine],
        runs_ref[LEVELS : LEVELS + 1, mine],
        runs_ref[LEVELS + 1 : LEVELS + 2, mine],
    )
    table = 0.03 * jnp.exp(level * jnp.log(F32(1.35)))
    both = jnp.concatenate([table * (0.5 * steep), table * (0.5 * (1.0 - steep))], axis=1)
    pieces = []
    for _ in range(3):
        piece = both.astype(BF16).astype(F32)
        pieces.append(piece)
        both = both - piece
    pieces.append(jnp.zeros_like(both))
    tables = jnp.concatenate(pieces, axis=0).astype(BF16)
    klass = (lax.broadcasted_iota(jnp.int32, (4 * LEVELS, LANES), 0) % LEVELS).astype(F32)
    pick8 = jnp.broadcast_to(pick, (SUB, LANES))
    has_top = jnp.where(tile_ref[0] > 0, F32(1.0), F32(0.0))
    has_bottom = jnp.where(tile_ref[0] < n_tile - 1, F32(1.0), F32(0.0))
    zeros = jnp.zeros((SUB, LANES), F32)

    def inside(r):
        return jnp.where(r < STEPS, has_top, jnp.where(r >= total - STEPS, has_bottom, 1.0))

    def coefficients(r, carry):
        valid = inside(r)
        ids = wide_ref[r]
        for j in range(tile0, tile1):
            here = jnp.broadcast_to(ids[:, j * LANES : (j + 1) * LANES], klass.shape)
            onehot = jnp.where(here == klass, valid, 0.0)
            ab = lax.dot_general(
                onehot.astype(BF16), tables, (((0,), (0,)), ((), ())), preferred_element_type=F32
            )
            first, last = max(low, j * LANES), min(high, (j + 1) * LANES)
            at, of = slice(first - low, last - low), slice(first - j * LANES, last - j * LANES)
            a_ref[r, at, :] = ab[of, :LANES]
            b_ref[r, at, :] = ab[of, LANES:]
        for ref in (u0_ref, u1_ref, d_ref):
            ref[r, 0:SUB, :] = zeros
            ref[r, SUB + width : 2 * SUB + width, :] = zeros
        return carry

    lax.fori_loop(0, total, coefficients, 0, unroll=4)

    for side in range(2):
        here = edges[side]
        for r in range(STEPS):
            row = r if side == 0 else total - STEPS + r
            n = high - sent
            at = SUB + sent - low
            u0_ref[row, at : at + n, :] = here[r * n : (r + 1) * n, :]
            if chunk:
                prior = edges[2 + side]
                n0 = parts[chunk - 1][1] - parts[chunk - 1][2]
                m = sent - low
                u0_ref[row, SUB : SUB + m, :] = prior[(r + 1) * n0 - m : (r + 1) * n0, :]
    copy.wait()
    for i in range(rows):
        for j in range(tile0, tile1):
            tile = jnp.transpose(raw_ref[:, i, (j - tile0) * LANES : (j - tile0 + 1) * LANES])
            first, last = max(low, j * LANES), min(high, (j + 1) * LANES)
            at = SUB + first - low
            u0_ref[STEPS + i, at : at + last - first, :] = tile[first - j * LANES : last - j * LANES, :]

    blocks = range(width // SUB)
    for step in range(1, STEPS + 1):
        src, dst = (u0_ref, u1_ref) if step % 2 else (u1_ref, u0_ref)

        def conduct(r, k, u, src=src):
            at = slice(k * SUB, (k + 1) * SUB)
            d = a_ref[r, at, :] + b_ref[r, at, :] * (1.0 / (1.0 + u * u))
            d_ref[r, SUB + k * SUB : 2 * SUB + k * SUB, :] = d
            return d

        top = step - 1
        for k in blocks:
            at = slice(SUB + k * SUB, 2 * SUB + k * SUB)
            u, un = src[top, at, :], src[top + 1, at, :]
            d, dn = conduct(top, k, u), conduct(top + 1, k, un)
            v_ref[k * SUB : (k + 1) * SUB, :] = (d + dn) * (un - u)

        def advance(r, carry, src=src, dst=dst, step=step, conduct=conduct):
            active = pick8 >= jnp.where(inside(r) > 0.0, F32(step), F32(2 * STEPS))
            for k in range(-1, width // SUB):
                p = SUB + k * SUB
                u, d = src[r, p : p + SUB, :], d_ref[r, p : p + SUB, :]
                flux = (d + d_ref[r, p + 1 : p + 1 + SUB, :]) * (src[r, p + 1 : p + 1 + SUB, :] - u)
                fx_ref[p : p + SUB, :] = flux
                if k < 0:
                    continue
                at = slice(k * SUB, (k + 1) * SUB)
                un = src[r + 1, p : p + SUB, :]
                dn = conduct(r + 1, k, un)
                down = (d + dn) * (un - u)
                across = flux - fx_ref[p - 1 : p - 1 + SUB, :]
                new = u + across + (down - v_ref[at, :])
                v_ref[at, :] = down
                dst[r, p : p + SUB, :] = jnp.where(active, new, u)
            return carry

        lax.fori_loop(step, total - step, advance, 0)

    result = u0_ref if STEPS % 2 == 0 else u1_ref
    per_block = rows // len(outs)
    done = []
    for offset in list(range(1, len(outs))) + [0]:
        row = STEPS + (grp_ref[0] ^ offset) * per_block
        for i in range(per_block):
            for j in range(own // LANES):
                p = SUB + chunk * own + j * LANES - low
                at = i * own + j * LANES
                made_ref[offset, :, at : at + LANES] = jnp.transpose(result[row + i, p : p + LANES, :])
        done.append(pltpu.make_async_copy(made_ref.at[offset], outs[offset], sem.at[1 + offset]))
        done[-1].start()
    for sent_out in done:
        sent_out.wait()


def diffuse(chunk, chunks, start_field, edges, ids, run_rows, tile, n_tile, grp, blocks):
    runs, rows, cols = start_field.shape
    total = rows + 2 * STEPS
    low, high, _ = spans(cols, chunks)[chunk]
    width = high - low
    tiles = -(-high // LANES) - low // LANES
    own = cols // chunks
    edges = list(edges[chunk]) + (list(edges[chunk - 1]) if chunk else [])
    state = pltpu.VMEM((total, width + 2 * SUB, runs), F32)
    return pl.pallas_call(
        functools.partial(diffuse_kernel, chunk, chunks, n_tile),
        in_specs=[SCALARS, SCALARS, ANY, SPACE, SPACE] + [SPACE] * len(edges),
        out_specs=[ANY] * blocks,
        out_shape=[jax.ShapeDtypeStruct((runs, rows * own // blocks), F32)] * blocks,
        scratch_shapes=[
            pltpu.VMEM((runs, rows, tiles * LANES), F32),
            state,
            state,
            state,
            pltpu.VMEM((total, width, runs), F32),
            pltpu.VMEM((total, width, runs), F32),
            pltpu.VMEM((width + 2 * SUB, runs), F32),
            pltpu.VMEM((width, runs), F32),
            pltpu.VMEM((total, 1, cols), F32),
            pltpu.VMEM((blocks, runs, rows * own // blocks), F32),
            pltpu.SemaphoreType.DMA((blocks + 1,)),
        ],
        cost_estimate=cost(100 * runs * total * width, 12 * runs * total * width),
        name="diffuse",
    )(tile, grp, start_field, ids, run_rows, *edges)


PITCH = 80


def hidden_kernel(
    runs_ref, layer_ref, hidden_ref, hidden_t_ref, gain_t_ref, project_ref, f_ref, ft_ref, rest_ref, stack_ref
):
    depth, runs = ft_ref.shape
    n_feat, block = layer_ref.shape
    n_exact = n_feat - 1
    steep = runs_ref[LEVELS + 1 : LEVELS + 2]
    rest = steep - steep.astype(BF16).astype(F32)

    @pl.when(pl.program_id(0) == 0)
    def _():
        held = runs_ref[...]
        row = lax.broadcasted_iota(jnp.int32, (depth, held.shape[0]), 0)
        col = lax.broadcasted_iota(jnp.int32, (depth, held.shape[0]), 1)

        def place(row):
            return jnp.where(row < 3 * PITCH, row % PITCH, PITCH)

        n_level = LEVELS * LEVELS
        at = place(row)
        source = jnp.where(
            at < n_level,
            at // LEVELS,
            jnp.where(at < n_exact, LEVELS, jnp.where(at == n_exact, LEVELS + 1, -1)),
        )
        spread = jnp.where(col == source, 1.0, 0.0).astype(BF16)
        value = jnp.dot(spread, held.astype(BF16), preferred_element_type=F32)
        at = place(lax.broadcasted_iota(jnp.int32, (depth, runs), 0))
        wanted = jnp.where(at < n_level, at % LEVELS, at - n_level + 1).astype(F32)
        feats = jnp.where(at < n_exact, jnp.where(value == wanted, 1.0, 0.0), value)
        ft_ref[...] = feats.astype(BF16)
        f_ref[...] = jnp.transpose(feats).astype(BF16)
        line = lax.broadcasted_iota(jnp.int32, (LANES, runs), 0)
        wide_rest = jnp.broadcast_to(rest, (LANES, runs))
        project = jnp.where(
            line < n_feat, feats[:LANES], jnp.where(line == n_feat, wide_rest, 0.0)
        )
        project_ref[...] = jnp.transpose(project).astype(BF16)
        rest_ref[...] = jnp.transpose(wide_rest)
        stack_ref[...] = jnp.zeros(stack_ref.shape, F32)

    layer = layer_ref[...]
    left = layer
    for piece in range(3):
        part = left.astype(BF16).astype(F32)
        stack_ref[piece * PITCH : piece * PITCH + n_feat, :] = part
        left = left - part
    stack = stack_ref[...]
    column = jnp.concatenate([rest_ref[...]] * (block // LANES), axis=1)
    pre = jnp.dot(f_ref[...], stack.astype(BF16), preferred_element_type=F32)
    pre = pre + column * layer[n_exact:n_feat, :]
    hidden_ref[...] = (pre * jax.nn.sigmoid(pre)).astype(BF16)
    stack_t = jnp.transpose(stack)
    last = sum(stack_t[:, p * PITCH + n_exact : p * PITCH + n_feat] for p in range(3))
    pre = jnp.dot(stack_t.astype(BF16), ft_ref[...], preferred_element_type=F32)
    pre = pre + last * rest
    logistic = jax.nn.sigmoid(pre)
    hidden_t_ref[...] = (pre * logistic).astype(BF16)
    gain_t_ref[...] = logistic * (1.0 + pre * (1.0 - logistic))


def hidden_units(run_rows, layer, block=512):
    held, runs = run_rows.shape
    n_feat, hid = layer.shape
    depth = -(-3 * PITCH // LANES) * LANES
    return pl.pallas_call(
        hidden_kernel,
        grid=(hid // block,),
        in_specs=[
            pl.BlockSpec((held, runs), lambda i: (0, 0)),
            pl.BlockSpec((n_feat, block), lambda i: (0, i)),
        ],
        out_specs=[
            pl.BlockSpec((runs, block), lambda i: (0, i)),
            pl.BlockSpec((block, runs), lambda i: (i, 0)),
            pl.BlockSpec((block, runs), lambda i: (i, 0)),
            pl.BlockSpec((runs, LANES), lambda i: (0, 0)),
        ],
        out_shape=[
            jax.ShapeDtypeStruct((runs, hid), BF16),
            jax.ShapeDtypeStruct((hid, runs), BF16),
            jax.ShapeDtypeStruct((hid, runs), F32),
            jax.ShapeDtypeStruct((runs, LANES), BF16),
        ],
        scratch_shapes=[
            pltpu.VMEM((runs, depth), BF16),
            pltpu.VMEM((depth, runs), BF16),
            pltpu.VMEM((runs, LANES), F32),
            pltpu.VMEM((depth, block), F32),
        ],
        cost_estimate=cost(4 * runs * hid * depth, 10 * runs * hid, 4 * runs * hid),
        name="hidden_units",
    )(run_rows, layer)


def predict_kernel(hidden_ref, weight_ref, bias_ref, out_ref):
    out_ref[...] = (
        jnp.dot(hidden_ref[...], weight_ref[...], preferred_element_type=F32) + bias_ref[...]
    )


def predict(chunk, chunks, cols, hidden, weight, bias):
    runs, hid = hidden.shape
    own = cols // chunks
    mine = weight.shape[1] // chunks
    strip = lambda i: (0, i * chunks + chunk)
    return pl.pallas_call(
        predict_kernel,
        grid=(mine // own,),
        in_specs=[
            pl.BlockSpec((runs, hid), lambda i: (0, 0)),
            pl.BlockSpec((hid, own), strip),
            pl.BlockSpec((1, own), strip),
        ],
        out_specs=pl.BlockSpec((runs, own), lambda i: (0, i)),
        out_shape=jax.ShapeDtypeStruct((runs, mine), F32),
        cost_estimate=cost(2 * runs * hid * mine, 2 * hid * mine + 4 * runs * mine),
        name="predict",
    )(hidden, weight, bias)


def learn_kernel(last, has_before, scale, sources, *refs):
    grp_ref, guess_ref = refs[:2]
    targets, refs = refs[2 : 2 + sources], refs[2 + sources :]
    weight_ref, bias_ref, gain_any, feats_ref = refs[:4]
    refs = refs[4:]
    if not last:
        hidden_t_ref, refs = refs[0], refs[1:]
    if has_before:
        acc_in_any, refs = refs[2], refs[3 + (not last) :]
    misfit_ref, bias_out_ref, acc_ref, extra_ref = refs[:4]
    if last:
        sent_ref, refs = refs[4], refs[1:]
    back_ref, gain_ref, sem, acc_in_ref = refs[4:8]
    slope_ref = extra_ref if last else refs[8]
    step, steps = pl.program_id(0), pl.num_programs(0)
    load = pltpu.make_async_copy(gain_any, gain_ref, sem.at[0])
    if has_before:
        load_acc = pltpu.make_async_copy(acc_in_any, acc_in_ref, sem.at[1])

    @pl.when(step == 0)
    def _():
        load.start()
        if has_before:
            load_acc.start()
        back_ref[...] = jnp.zeros(back_ref.shape, F32)

    per_source, own = targets[0].shape
    total = jnp.zeros((1, own), F32)
    for offset, target_ref in enumerate(targets):
        at = pl.ds(pl.multiple_of((grp_ref[0] ^ offset) * per_source, per_source), per_source)
        if offset:
            target = target_ref[:, pl.ds(pl.multiple_of(step * own, own), own)]
        else:
            target = target_ref[...]
        error = guess_ref[at, :] - target
        misfit_ref[at, :] = error.astype(BF16)
        slope = (error * scale).astype(BF16)
        slope_ref[at, :] = slope
        total = total + jnp.sum(slope.astype(F32), axis=0, keepdims=True)
    bias_out_ref[...] = bias_ref[...] - 0.5 * total
    slope = slope_ref[...]
    for h in range(0, weight_ref.shape[0], BLOCK):
        at = slice(h, h + BLOCK)
        weight = weight_ref[at, :]
        back_ref[at, :] += lax.dot_general(
            weight, slope, (((1,), (1,)), ((), ())), preferred_element_type=F32
        )
        if not last:
            grad = jnp.dot(hidden_t_ref[at, :], slope, preferred_element_type=F32)
            extra_ref[at, :] = (weight.astype(F32) - 0.5 * grad).astype(BF16)

    @pl.when(step == steps - 1)
    def _():
        load.wait()
        if has_before:
            load_acc.wait()
        feats = feats_ref[...]
        for h in range(0, back_ref.shape[0], BLOCK):
            at = slice(h, h + BLOCK)
            full = back_ref[at, :] * gain_ref[at, :]
            high = full.astype(BF16)
            low = (full - high.astype(F32)).astype(BF16)
            acc = jnp.dot(high, feats, preferred_element_type=F32)
            acc = acc + jnp.dot(low, feats, preferred_element_type=F32)
            if has_before:
                acc = acc + acc_in_ref[at, :]
            if last:
                for t in range(0, BLOCK, LANES):
                    turned = jnp.transpose(acc[t : t + LANES, :])[: acc_ref.shape[1], :]
                    half, place = divmod((h + t) // LANES, acc_ref.shape[0])

                    @pl.when((grp_ref[0] & 1) == half)
                    def _(turned=turned, place=place):
                        acc_ref[place] = turned

                    @pl.when((grp_ref[0] & 1) != half)
                    def _(turned=turned, place=place):
                        sent_ref[place] = turned
            else:
                acc_ref[at, :] = acc


def learn(chunk, chunks, cols, grp, guess, targets, weight, bias, gain_t, feats, hidden_t, before, kept, scale):
    hid, cells = weight.shape
    sources = len(targets)
    per_source, mine = targets[0].shape
    runs = sources * per_source
    own = cols // chunks
    last, has_before = chunk == chunks - 1, before is not None
    strip = lambda i: (0, i * chunks + chunk)
    in_specs = [SCALARS, pl.BlockSpec((runs, own), lambda i: (0, i))]
    in_specs += [pl.BlockSpec((per_source, own), lambda i: (0, i))] + [SPACE] * (sources - 1)
    in_specs += [pl.BlockSpec((hid, own), strip), pl.BlockSpec((1, own), strip), ANY, SPACE]
    args = [grp, guess, *targets, weight, bias, gain_t, feats]
    if not last:
        in_specs.append(SPACE)
        args.append(hidden_t)
    aliases = {}
    if has_before:
        aliases = {len(args): 0, len(args) + 1: 1}
        in_specs += [ANY, ANY, ANY]
        args += list(before[:3])
        if not last:
            aliases[len(args)] = 3
            in_specs.append(ANY)
            args.append(before[3])
    acc_shape = (hid // LANES // 2, kept, LANES) if last else (hid, LANES)
    acc_spec = pl.BlockSpec(acc_shape, lambda i: (0,) * len(acc_shape))
    more = 1 if last else 0
    extra = (runs, own, runs) if last else (hid, own, hid)
    scratch = [
        pltpu.VMEM((hid, runs), F32),
        pltpu.VMEM((hid, runs), F32),
        pltpu.SemaphoreType.DMA((2,)),
        pltpu.VMEM((hid, LANES), F32),
    ]
    if not last:
        scratch.append(pltpu.VMEM((runs, own), BF16))
    products = 1 if last else 2
    return pl.pallas_call(
        functools.partial(learn_kernel, last, has_before, scale, sources),
        grid=(mine // own,),
        in_specs=in_specs,
        out_specs=[
            pl.BlockSpec((runs, own), strip),
            pl.BlockSpec((1, own), strip),
            acc_spec,
            pl.BlockSpec((extra[0], own), (lambda i: (0, i)) if last else strip),
        ]
        + [acc_spec] * more,
        out_shape=[
            jax.ShapeDtypeStruct((runs, cells), BF16),
            jax.ShapeDtypeStruct((1, cells), F32),
            jax.ShapeDtypeStruct(acc_shape, F32),
            jax.ShapeDtypeStruct((runs, mine) if last else (hid, cells), BF16),
        ]
        + [jax.ShapeDtypeStruct(acc_shape, F32)] * more,
        scratch_shapes=scratch,
        input_output_aliases=aliases,
        cost_estimate=cost(
            2 * runs * hid * (products * mine + 2 * LANES), 2 * hid * mine * products + 12 * runs * mine
        ),
        name="learn",
    )(*args)


def update_kernel(hidden_t_ref, slope_ref, weight_ref, _, out_ref):
    slope = slope_ref[...]
    for h in range(0, weight_ref.shape[0], BLOCK):
        at = slice(h, h + BLOCK)
        grad = jnp.dot(hidden_t_ref[at, :], slope, preferred_element_type=F32)
        out_ref[at, :] = (weight_ref[at, :].astype(F32) - 0.5 * grad).astype(BF16)


def update(first, count, chunks, cols, hidden_t, slope, weight, so_far):
    hid, cells = weight.shape
    runs, _ = slope.shape
    own = cols // chunks
    strip = lambda i: (0, (first + i) * chunks + chunks - 1)
    return pl.pallas_call(
        update_kernel,
        grid=(count,),
        in_specs=[
            pl.BlockSpec((hid, runs), lambda i: (0, 0)),
            pl.BlockSpec((runs, own), lambda i: (0, first + i)),
            pl.BlockSpec((hid, own), strip),
            ANY,
        ],
        out_specs=pl.BlockSpec((hid, own), strip),
        out_shape=jax.ShapeDtypeStruct((hid, cells), BF16),
        input_output_aliases={3: 0},
        cost_estimate=cost(2 * runs * hid * own * count, (4 * hid + 4 * runs) * own * count),
        name="update",
    )(hidden_t, slope, weight, so_far)


def finish_kernel(total_ref, layer_ref, out_ref):
    n_feat = layer_ref.shape[0]
    line = lax.broadcasted_iota(jnp.int32, (n_feat, LANES), 0)
    for t in range(total_ref.shape[0]):
        at = slice(t * LANES, (t + 1) * LANES)
        rest = jnp.broadcast_to(total_ref[t, n_feat : n_feat + 1, :], (n_feat, LANES))
        grad = total_ref[t, :n_feat, :] + jnp.where(line == n_feat - 1, rest, 0.0)
        out_ref[:, at] = layer_ref[:, at] - 2.0 * grad


def finish(total, layer):
    return pl.pallas_call(
        finish_kernel,
        in_specs=[SPACE, SPACE],
        out_specs=SPACE,
        out_shape=jax.ShapeDtypeStruct(layer.shape, F32),
        cost_estimate=cost(3 * layer.size, 12 * layer.size),
        name="finish",
    )(total, layer)


def bits_of(size):
    return [1 << b for b in range(size.bit_length() - 1)]


def halve(x, axis, bit):
    size = lax.axis_size(axis)
    upper = (lax.axis_index(axis) & bit) != 0
    half = x.shape[0] // 2
    kept = lax.dynamic_slice_in_dim(x, jnp.where(upper, half, 0), half, 0)
    sent = lax.dynamic_slice_in_dim(x, jnp.where(upper, 0, half), half, 0)
    return kept + lax.ppermute(sent, axis, [(i, i ^ bit) for i in range(size)])


def rejoin(x, axis, bit):
    size = lax.axis_size(axis)
    upper = (lax.axis_index(axis) & bit) != 0
    other = lax.ppermute(x, axis, [(i, i ^ bit) for i in range(size)])
    return jnp.where(
        upper, jnp.concatenate([other, x], axis=0), jnp.concatenate([x, other], axis=0)
    )


def sum_over_devices(x, sent):
    grp, tile = lax.axis_size("grp"), lax.axis_size("tile")
    x = x + lax.ppermute(sent, "grp", [(i, i ^ 1) for i in range(grp)])
    for bit in bits_of(grp)[1:]:
        x = halve(x, "grp", bit)
    for bit in bits_of(tile):
        x = x + lax.ppermute(x, "tile", [(i, i ^ bit) for i in range(tile)])
    for bit in bits_of(grp)[::-1]:
        x = rejoin(x, "grp", bit)
    return x


def on_device(
    start_field, class_ids, run_levels, steepness, step_pick, input_layer, output_layer, output_bias
):
    _, rows, cols = start_field.shape
    n_grp, n_tile = lax.axis_size("grp"), lax.axis_size("tile")
    tile = lax.axis_index("tile").astype(jnp.int32)[None]
    grp = lax.axis_index("grp").astype(jnp.int32)[None]
    chunks = CHUNKS
    parts = spans(cols, chunks)
    runs_total, classes = run_levels.shape
    n_feat, hid = input_layer.shape

    up = [(i, i + 1) for i in range(n_tile - 1)]
    down = [(j, i) for i, j in up]
    edges = []
    for c in range(chunks):
        top, bottom = pack_edges(c, start_field, class_ids, parts)
        above = lax.ppermute(bottom, "tile", up)
        below = lax.ppermute(top, "tile", down)
        edges.append((in_vmem(above), in_vmem(below)))

    run_rows = jnp.concatenate(
        [
            run_levels.T.astype(F32),
            step_pick[None, :].astype(F32),
            steepness[None, :],
            jnp.zeros((2 * LEVELS - classes - 2, runs_total), F32),
        ],
        axis=0,
    )
    hidden, hidden_t, gain_t, project = hidden_units(run_rows, input_layer)
    bias_row = output_bias[None, :]
    guesses = []
    for c in range(chunks):
        guesses.append(predict(c, chunks, cols, hidden, output_layer, bias_row))
    kept = -(-(n_feat + 1) // SUB) * SUB

    state = None
    scale = 2.0 / runs_total
    for c in range(chunks):
        snaps = diffuse(c, chunks, start_field, edges, class_ids, run_rows, tile, n_tile, grp, n_grp)
        targets = [snaps[0]]
        for offset in range(1, n_grp):
            pairs = [(i, i ^ offset) for i in range(n_grp)]
            targets.append(in_vmem(lax.ppermute(snaps[offset], "grp", pairs)))
        before = state
        state = learn(
            c, chunks, cols, grp, guesses[c], targets, output_layer, bias_row,
            gain_t, project, hidden_t, before, kept, scale,
        )
    misfit, bias_next, partial, slope, sent = state
    output_next, strips = before[3], rows // n_grp
    for part in range(UPDATES):
        first, past = part * strips // UPDATES, (part + 1) * strips // UPDATES
        output_next = update(
            first, past - first, chunks, cols, hidden_t, slope, output_layer, output_next
        )
    total = sum_over_devices(partial.reshape(-1, LANES), sent.reshape(-1, LANES))
    total = total.reshape(hid // LANES, kept, LANES)
    input_next = finish(in_vmem(total), in_vmem(input_layer))
    return misfit, output_next, bias_next.reshape(-1), input_next


def solution(mesh):
    in_specs = (
        P("grp", "tile", None),
        P("tile", None),
        P(),
        P(),
        P(),
        P(),
        P(None, ("grp", "tile")),
        P(("grp", "tile")),
    )
    out_specs = (P(None, ("grp", "tile")), P(None, ("grp", "tile")), P(("grp", "tile")), P())

    return jax.shard_map(on_device, mesh=mesh, in_specs=in_specs, out_specs=out_specs, check_vma=False)
```

```python
import functools

import jax
import jax.numpy as jnp
from jax import lax
from jax.experimental import pallas as pl
from jax.experimental.pallas import tpu as pltpu
from jax.sharding import PartitionSpec as P


STEPS = 4
LEVELS = 8
LANES = 128
SUB = 8
BLOCK = 256
CHUNKS = 2
UPDATES = 2
F32 = jnp.float32
BF16 = jnp.bfloat16
SPACE = pl.BlockSpec(memory_space=pltpu.VMEM)
ANY = pl.BlockSpec(memory_space=pl.ANY)
SCALARS = pl.BlockSpec(memory_space=pltpu.SMEM)


def in_vmem(x):
    return pltpu.with_memory_space_constraint(x, pltpu.VMEM)


def cost(flops, nbytes, transcendentals=0):
    return pl.CostEstimate(
        flops=int(flops), bytes_accessed=int(nbytes), transcendentals=int(transcendentals)
    )


def spans(cols, chunks):
    width = cols // chunks
    out = []
    for c in range(chunks):
        low = max(c * width - SUB, 0)
        high = min((c + 1) * width + SUB, cols)
        sent = 0 if c == 0 else c * width + SUB
        out.append((low, high, sent))
    return out


def pack_kernel(chunk, part, field_ref, ids_ref, *outs):
    rows, cols = ids_ref.shape
    _, high, sent = part
    for j in range(sent // LANES, -(-high // LANES)):

        @pl.when(pl.program_id(0) == j - sent // LANES)
        def _(j=j):
            first, last = max(sent, j * LANES), min(high, (j + 1) * LANES)
            for side in range(2):
                for r in range(STEPS):
                    row = r if side == 0 else rows - STEPS + r
                    tile = jnp.transpose(field_ref[:, row, :])
                    at = r * (high - sent) + first - sent
                    outs[side][at : at + last - first, :] = tile[
                        first - j * LANES : last - j * LANES, :
                    ]

    @pl.when(pl.program_id(0) == 0)
    def _():
        if chunk == 0:
            for side in range(2):
                for r in range(STEPS):
                    row = r if side == 0 else rows - STEPS + r
                    for j in range(cols // LANES):
                        at = STEPS * (high - sent) + r * (cols // LANES) + j
                        outs[side][at : at + 1, :] = ids_ref[
                            row : row + 1, j * LANES : (j + 1) * LANES
                        ].astype(F32)


def pack_edges(chunk, start_field, ids, parts):
    runs, rows, cols = start_field.shape
    _, high, sent = parts[chunk]
    extra = STEPS * cols // LANES if chunk == 0 else 0
    shapes = [jax.ShapeDtypeStruct((STEPS * (high - sent) + extra, runs), F32)] * 2
    tile0, tile1 = sent // LANES, -(-high // LANES)
    return pl.pallas_call(
        functools.partial(pack_kernel, chunk, parts[chunk]),
        grid=(tile1 - tile0,),
        in_specs=[
            pl.BlockSpec((runs, rows, LANES), lambda j: (0, 0, tile0 + j)),
            pl.BlockSpec((rows, cols), lambda j: (0, 0)),
        ],
        out_specs=[pl.BlockSpec(x.shape, lambda j: (0, 0)) for x in shapes],
        out_shape=shapes,
        cost_estimate=cost(0, 6 * runs * rows * (high - sent)),
        name="pack_edges",
    )(start_field, ids)


def diffuse_kernel(chunk, chunks, n_tile, tile_ref, grp_ref, field_ref, ids_ref, runs_ref, *refs):
    edges, outs = refs[: 2 + 2 * (chunk > 0)], refs[2 + 2 * (chunk > 0) : -11]
    raw_ref, u0_ref, u1_ref, d_ref, a_ref, b_ref, fx_ref, v_ref, wide_ref, made_ref, sem = refs[-11:]
    rows, cols = ids_ref.shape
    total = rows + 2 * STEPS
    parts = spans(cols, chunks)
    low, high, sent = parts[chunk]
    width = high - low
    own = cols // chunks
    tile0, tile1 = low // LANES, -(-high // LANES)
    copy = pltpu.make_async_copy(field_ref.at[:, :, tile0 * LANES : tile1 * LANES], raw_ref, sem.at[0])
    copy.start()
    brought = STEPS * (parts[0][1] - parts[0][2])
    for j in range(tile0, tile1):
        at = slice(j * LANES, (j + 1) * LANES)
        for side in range(2):
            for r in range(STEPS):
                line = brought + r * (cols // LANES) + j
                wide_ref[side * (total - STEPS) + r, :, at] = edges[side - 2][line : line + 1, :]
        for r in range(rows):
            wide_ref[STEPS + r, :, at] = ids_ref[r : r + 1, at].astype(F32)

    mine = pl.ds(pl.multiple_of(grp_ref[0] * LANES, LANES), LANES)
    level, pick, steep = (
        runs_ref[0:LEVELS, mine],
        runs_ref[LEVELS : LEVELS + 1, mine],
        runs_ref[LEVELS + 1 : LEVELS + 2, mine],
    )
    table = 0.03 * jnp.exp(level * jnp.log(F32(1.35)))
    both = jnp.concatenate([table * (0.5 * steep), table * (0.5 * (1.0 - steep))], axis=1)
    pieces = []
    for _ in range(3):
        piece = both.astype(BF16).astype(F32)
        pieces.append(piece)
        both = both - piece
    pieces.append(jnp.zeros_like(both))
    tables = jnp.concatenate(pieces, axis=0).astype(BF16)
    klass = (lax.broadcasted_iota(jnp.int32, (4 * LEVELS, LANES), 0) % LEVELS).astype(F32)
    pick8 = jnp.broadcast_to(pick, (SUB, LANES))
    has_top = jnp.where(tile_ref[0] > 0, F32(1.0), F32(0.0))
    has_bottom = jnp.where(tile_ref[0] < n_tile - 1, F32(1.0), F32(0.0))
    zeros = jnp.zeros((SUB, LANES), F32)

    def inside(r):
        return jnp.where(r < STEPS, has_top, jnp.where(r >= total - STEPS, has_bottom, 1.0))

    def coefficients(r, carry):
        valid = inside(r)
        ids = wide_ref[r]
        for j in range(tile0, tile1):
            here = jnp.broadcast_to(ids[:, j * LANES : (j + 1) * LANES], klass.shape)
            onehot = jnp.where(here == klass, valid, 0.0)
            ab = lax.dot_general(
                onehot.astype(BF16), tables, (((0,), (0,)), ((), ())), preferred_element_type=F32
            )
            first, last = max(low, j * LANES), min(high, (j + 1) * LANES)
            at, of = slice(first - low, last - low), slice(first - j * LANES, last - j * LANES)
            a_ref[r, at, :] = ab[of, :LANES]
            b_ref[r, at, :] = ab[of, LANES:]
        for ref in (u0_ref, u1_ref, d_ref):
            ref[r, 0:SUB, :] = zeros
            ref[r, SUB + width : 2 * SUB + width, :] = zeros
        return carry

    lax.fori_loop(0, total, coefficients, 0, unroll=4)

    for side in range(2):
        here = edges[side]
        for r in range(STEPS):
            row = r if side == 0 else total - STEPS + r
            n = high - sent
            at = SUB + sent - low
            u0_ref[row, at : at + n, :] = here[r * n : (r + 1) * n, :]
            if chunk:
                prior = edges[2 + side]
                n0 = parts[chunk - 1][1] - parts[chunk - 1][2]
                m = sent - low
                u0_ref[row, SUB : SUB + m, :] = prior[(r + 1) * n0 - m : (r + 1) * n0, :]
    copy.wait()
    for i in range(rows):
        for j in range(tile0, tile1):
            tile = jnp.transpose(raw_ref[:, i, (j - tile0) * LANES : (j - tile0 + 1) * LANES])
            first, last = max(low, j * LANES), min(high, (j + 1) * LANES)
            at = SUB + first - low
            u0_ref[STEPS + i, at : at + last - first, :] = tile[first - j * LANES : last - j * LANES, :]

    blocks = range(width // SUB)
    for step in range(1, STEPS + 1):
        src, dst = (u0_ref, u1_ref) if step % 2 else (u1_ref, u0_ref)

        def conduct(r, k, u, src=src):
            at = slice(k * SUB, (k + 1) * SUB)
            d = a_ref[r, at, :] + b_ref[r, at, :] * (1.0 / (1.0 + u * u))
            d_ref[r, SUB + k * SUB : 2 * SUB + k * SUB, :] = d
            return d

        top = step - 1
        for k in blocks:
            at = slice(SUB + k * SUB, 2 * SUB + k * SUB)
            u, un = src[top, at, :], src[top + 1, at, :]
            d, dn = conduct(top, k, u), conduct(top + 1, k, un)
            v_ref[k * SUB : (k + 1) * SUB, :] = (d + dn) * (un - u)

        def advance(r, carry, src=src, dst=dst, step=step, conduct=conduct):
            active = pick8 >= jnp.where(inside(r) > 0.0, F32(step), F32(2 * STEPS))
            for k in range(-1, width // SUB):
                p = SUB + k * SUB
                u, d = src[r, p : p + SUB, :], d_ref[r, p : p + SUB, :]
                flux = (d + d_ref[r, p + 1 : p + 1 + SUB, :]) * (src[r, p + 1 : p + 1 + SUB, :] - u)
                fx_ref[p : p + SUB, :] = flux
                if k < 0:
                    continue
                at = slice(k * SUB, (k + 1) * SUB)
                un = src[r + 1, p : p + SUB, :]
                dn = conduct(r + 1, k, un)
                down = (d + dn) * (un - u)
                across = flux - fx_ref[p - 1 : p - 1 + SUB, :]
                new = u + across + (down - v_ref[at, :])
                v_ref[at, :] = down
                dst[r, p : p + SUB, :] = jnp.where(active, new, u)
            return carry

        lax.fori_loop(step, total - step, advance, 0)

    result = u0_ref if STEPS % 2 == 0 else u1_ref
    per_block = rows // len(outs)
    done = []
    for offset in list(range(1, len(outs))) + [0]:
        row = STEPS + (grp_ref[0] ^ offset) * per_block
        for i in range(per_block):
            for j in range(own // LANES):
                p = SUB + chunk * own + j * LANES - low
                at = i * own + j * LANES
                made_ref[offset, :, at : at + LANES] = jnp.transpose(result[row + i, p : p + LANES, :])
        done.append(pltpu.make_async_copy(made_ref.at[offset], outs[offset], sem.at[1 + offset]))
        done[-1].start()
    for sent_out in done:
        sent_out.wait()


def diffuse(chunk, chunks, start_field, edges, ids, run_rows, tile, n_tile, grp, blocks):
    runs, rows, cols = start_field.shape
    total = rows + 2 * STEPS
    low, high, _ = spans(cols, chunks)[chunk]
    width = high - low
    tiles = -(-high // LANES) - low // LANES
    own = cols // chunks
    edges = list(edges[chunk]) + (list(edges[chunk - 1]) if chunk else [])
    state = pltpu.VMEM((total, width + 2 * SUB, runs), F32)
    return pl.pallas_call(
        functools.partial(diffuse_kernel, chunk, chunks, n_tile),
        in_specs=[SCALARS, SCALARS, ANY, SPACE, SPACE] + [SPACE] * len(edges),
        out_specs=[ANY] * blocks,
        out_shape=[jax.ShapeDtypeStruct((runs, rows * own // blocks), F32)] * blocks,
        scratch_shapes=[
            pltpu.VMEM((runs, rows, tiles * LANES), F32),
            state,
            state,
            state,
            pltpu.VMEM((total, width, runs), F32),
            pltpu.VMEM((total, width, runs), F32),
            pltpu.VMEM((width + 2 * SUB, runs), F32),
            pltpu.VMEM((width, runs), F32),
            pltpu.VMEM((total, 1, cols), F32),
            pltpu.VMEM((blocks, runs, rows * own // blocks), F32),
            pltpu.SemaphoreType.DMA((blocks + 1,)),
        ],
        cost_estimate=cost(100 * runs * total * width, 12 * runs * total * width),
        name="diffuse",
    )(tile, grp, start_field, ids, run_rows, *edges)


PITCH = 80


def hidden_kernel(
    runs_ref, layer_ref, hidden_ref, hidden_t_ref, gain_t_ref, project_ref, f_ref, ft_ref, rest_ref, stack_ref
):
    depth, runs = ft_ref.shape
    n_feat, block = layer_ref.shape
    n_exact = n_feat - 1
    steep = runs_ref[LEVELS + 1 : LEVELS + 2]
    rest = steep - steep.astype(BF16).astype(F32)

    @pl.when(pl.program_id(0) == 0)
    def _():
        held = runs_ref[...]
        row = lax.broadcasted_iota(jnp.int32, (depth, held.shape[0]), 0)
        col = lax.broadcasted_iota(jnp.int32, (depth, held.shape[0]), 1)

        def place(row):
            return jnp.where(row < 3 * PITCH, row % PITCH, PITCH)

        n_level = LEVELS * LEVELS
        at = place(row)
        source = jnp.where(
            at < n_level,
            at // LEVELS,
            jnp.where(at < n_exact, LEVELS, jnp.where(at == n_exact, LEVELS + 1, -1)),
        )
        spread = jnp.where(col == source, 1.0, 0.0).astype(BF16)
        value = jnp.dot(spread, held.astype(BF16), preferred_element_type=F32)
        at = place(lax.broadcasted_iota(jnp.int32, (depth, runs), 0))
        wanted = jnp.where(at < n_level, at % LEVELS, at - n_level + 1).astype(F32)
        feats = jnp.where(at < n_exact, jnp.where(value == wanted, 1.0, 0.0), value)
        ft_ref[...] = feats.astype(BF16)
        f_ref[...] = jnp.transpose(feats).astype(BF16)
        line = lax.broadcasted_iota(jnp.int32, (LANES, runs), 0)
        wide_rest = jnp.broadcast_to(rest, (LANES, runs))
        project = jnp.where(
            line < n_feat, feats[:LANES], jnp.where(line == n_feat, wide_rest, 0.0)
        )
        project_ref[...] = jnp.transpose(project).astype(BF16)
        rest_ref[...] = jnp.transpose(wide_rest)
        stack_ref[...] = jnp.zeros(stack_ref.shape, F32)

    layer = layer_ref[...]
    left = layer
    for piece in range(3):
        part = left.astype(BF16).astype(F32)
        stack_ref[piece * PITCH : piece * PITCH + n_feat, :] = part
        left = left - part
    stack = stack_ref[...]
    column = jnp.concatenate([rest_ref[...]] * (block // LANES), axis=1)
    pre = jnp.dot(f_ref[...], stack.astype(BF16), preferred_element_type=F32)
    pre = pre + column * layer[n_exact:n_feat, :]
    hidden_ref[...] = (pre * jax.nn.sigmoid(pre)).astype(BF16)
    stack_t = jnp.transpose(stack)
    last = sum(stack_t[:, p * PITCH + n_exact : p * PITCH + n_feat] for p in range(3))
    pre = jnp.dot(stack_t.astype(BF16), ft_ref[...], preferred_element_type=F32)
    pre = pre + last * rest
    logistic = jax.nn.sigmoid(pre)
    hidden_t_ref[...] = (pre * logistic).astype(BF16)
    gain_t_ref[...] = logistic * (1.0 + pre * (1.0 - logistic))


def hidden_units(run_rows, layer, block=512):
    held, runs = run_rows.shape
    n_feat, hid = layer.shape
    depth = -(-3 * PITCH // LANES) * LANES
    return pl.pallas_call(
        hidden_kernel,
        grid=(hid // block,),
        in_specs=[
            pl.BlockSpec((held, runs), lambda i: (0, 0)),
            pl.BlockSpec((n_feat, block), lambda i: (0, i)),
        ],
        out_specs=[
            pl.BlockSpec((runs, block), lambda i: (0, i)),
            pl.BlockSpec((block, runs), lambda i: (i, 0)),
            pl.BlockSpec((block, runs), lambda i: (i, 0)),
            pl.BlockSpec((runs, LANES), lambda i: (0, 0)),
        ],
        out_shape=[
            jax.ShapeDtypeStruct((runs, hid), BF16),
            jax.ShapeDtypeStruct((hid, runs), BF16),
            jax.ShapeDtypeStruct((hid, runs), F32),
            jax.ShapeDtypeStruct((runs, LANES), BF16),
        ],
        scratch_shapes=[
            pltpu.VMEM((runs, depth), BF16),
            pltpu.VMEM((depth, runs), BF16),
            pltpu.VMEM((runs, LANES), F32),
            pltpu.VMEM((depth, block), F32),
        ],
        cost_estimate=cost(4 * runs * hid * depth, 10 * runs * hid, 4 * runs * hid),
        name="hidden_units",
    )(run_rows, layer)


def predict_kernel(hidden_ref, weight_ref, bias_ref, out_ref):
    out_ref[...] = (
        jnp.dot(hidden_ref[...], weight_ref[...], preferred_element_type=F32) + bias_ref[...]
    )


def predict(hidden, weight, bias, block=512):
    runs, hid = hidden.shape
    cells = weight.shape[1]
    return pl.pallas_call(
        predict_kernel,
        grid=(cells // block,),
        in_specs=[
            pl.BlockSpec((runs, hid), lambda i: (0, 0)),
            pl.BlockSpec((hid, block), lambda i: (0, i)),
            pl.BlockSpec((1, block), lambda i: (0, i)),
        ],
        out_specs=pl.BlockSpec((runs, block), lambda i: (0, i)),
        out_shape=jax.ShapeDtypeStruct((runs, cells), F32),
        cost_estimate=cost(2 * runs * hid * cells, 2 * hid * cells + 4 * runs * cells),
        name="predict",
    )(hidden, weight, bias)


def learn_kernel(last, has_before, scale, sources, *refs):
    grp_ref, guess_ref = refs[:2]
    targets, refs = refs[2 : 2 + sources], refs[2 + sources :]
    weight_ref, bias_ref, gain_any, feats_ref = refs[:4]
    refs = refs[4:]
    if not last:
        hidden_t_ref, refs = refs[0], refs[1:]
    if has_before:
        acc_in_any, refs = refs[2], refs[3 + (not last) :]
    misfit_ref, bias_out_ref, acc_ref, extra_ref = refs[:4]
    back_ref, gain_ref, sem, acc_in_ref = refs[4:8]
    slope_ref = extra_ref if last else refs[8]
    step, steps = pl.program_id(0), pl.num_programs(0)
    load = pltpu.make_async_copy(gain_any, gain_ref, sem.at[0])
    if has_before:
        load_acc = pltpu.make_async_copy(acc_in_any, acc_in_ref, sem.at[1])

    @pl.when(step == 0)
    def _():
        load.start()
        if has_before:
            load_acc.start()
        back_ref[...] = jnp.zeros(back_ref.shape, F32)

    per_source, own = targets[0].shape
    total = jnp.zeros((1, own), F32)
    for offset, target_ref in enumerate(targets):
        at = pl.ds(pl.multiple_of((grp_ref[0] ^ offset) * per_source, per_source), per_source)
        if offset:
            target = target_ref[:, pl.ds(pl.multiple_of(step * own, own), own)]
        else:
            target = target_ref[...]
        error = guess_ref[at, :] - target
        misfit_ref[at, :] = error.astype(BF16)
        slope = (error * scale).astype(BF16)
        slope_ref[at, :] = slope
        total = total + jnp.sum(slope.astype(F32), axis=0, keepdims=True)
    bias_out_ref[...] = bias_ref[...] - 0.5 * total
    slope = slope_ref[...]
    for h in range(0, weight_ref.shape[0], BLOCK):
        at = slice(h, h + BLOCK)
        weight = weight_ref[at, :]
        back_ref[at, :] += lax.dot_general(
            weight, slope, (((1,), (1,)), ((), ())), preferred_element_type=F32
        )
        if not last:
            grad = jnp.dot(hidden_t_ref[at, :], slope, preferred_element_type=F32)
            extra_ref[at, :] = (weight.astype(F32) - 0.5 * grad).astype(BF16)

    @pl.when(step == steps - 1)
    def _():
        load.wait()
        if has_before:
            load_acc.wait()
        feats = feats_ref[...]
        for h in range(0, back_ref.shape[0], BLOCK):
            at = slice(h, h + BLOCK)
            full = back_ref[at, :] * gain_ref[at, :]
            high = full.astype(BF16)
            low = (full - high.astype(F32)).astype(BF16)
            acc = jnp.dot(high, feats, preferred_element_type=F32)
            acc = acc + jnp.dot(low, feats, preferred_element_type=F32)
            if has_before:
                acc = acc + acc_in_ref[at, :]
            if last:
                for t in range(0, BLOCK, LANES):
                    turned = jnp.transpose(acc[t : t + LANES, :])
                    acc_ref[(h + t) // LANES] = turned[: acc_ref.shape[1], :]
            else:
                acc_ref[at, :] = acc


def learn(chunk, chunks, cols, grp, guess, targets, weight, bias, gain_t, feats, hidden_t, before, kept, scale):
    hid, cells = weight.shape
    sources = len(targets)
    per_source, mine = targets[0].shape
    runs = sources * per_source
    own = cols // chunks
    last, has_before = chunk == chunks - 1, before is not None
    strip = lambda i: (0, i * chunks + chunk)
    in_specs = [SCALARS, pl.BlockSpec((runs, own), strip)]
    in_specs += [pl.BlockSpec((per_source, own), lambda i: (0, i))] + [SPACE] * (sources - 1)
    in_specs += [pl.BlockSpec((hid, own), strip), pl.BlockSpec((1, own), strip), ANY, SPACE]
    args = [grp, guess, *targets, weight, bias, gain_t, feats]
    if not last:
        in_specs.append(SPACE)
        args.append(hidden_t)
    aliases = {}
    if has_before:
        aliases = {len(args): 0, len(args) + 1: 1}
        in_specs += [ANY, ANY, ANY]
        args += list(before[:3])
        if not last:
            aliases[len(args)] = 3
            in_specs.append(ANY)
            args.append(before[3])
    acc_shape = (hid // LANES, kept, LANES) if last else (hid, LANES)
    extra = (runs, own, runs) if last else (hid, own, hid)
    scratch = [
        pltpu.VMEM((hid, runs), F32),
        pltpu.VMEM((hid, runs), F32),
        pltpu.SemaphoreType.DMA((2,)),
        pltpu.VMEM((hid, LANES), F32),
    ]
    if not last:
        scratch.append(pltpu.VMEM((runs, own), BF16))
    products = 1 if last else 2
    return pl.pallas_call(
        functools.partial(learn_kernel, last, has_before, scale, sources),
        grid=(mine // own,),
        in_specs=in_specs,
        out_specs=[
            pl.BlockSpec((runs, own), strip),
            pl.BlockSpec((1, own), strip),
            pl.BlockSpec(acc_shape, lambda i: (0,) * len(acc_shape)),
            pl.BlockSpec((extra[0], own), (lambda i: (0, i)) if last else strip),
        ],
        out_shape=[
            jax.ShapeDtypeStruct((runs, cells), BF16),
            jax.ShapeDtypeStruct((1, cells), F32),
            jax.ShapeDtypeStruct(acc_shape, F32),
            jax.ShapeDtypeStruct((runs, mine) if last else (hid, cells), BF16),
        ],
        scratch_shapes=scratch,
        input_output_aliases=aliases,
        cost_estimate=cost(
            2 * runs * hid * (products * mine + 2 * LANES), 2 * hid * mine * products + 12 * runs * mine
        ),
        name="learn",
    )(*args)


def update_kernel(hidden_t_ref, slope_ref, weight_ref, _, out_ref):
    slope = slope_ref[...]
    for h in range(0, weight_ref.shape[0], BLOCK):
        at = slice(h, h + BLOCK)
        grad = jnp.dot(hidden_t_ref[at, :], slope, preferred_element_type=F32)
        out_ref[at, :] = (weight_ref[at, :].astype(F32) - 0.5 * grad).astype(BF16)


def update(first, count, chunks, cols, hidden_t, slope, weight, so_far):
    hid, cells = weight.shape
    runs, _ = slope.shape
    own = cols // chunks
    strip = lambda i: (0, (first + i) * chunks + chunks - 1)
    return pl.pallas_call(
        update_kernel,
        grid=(count,),
        in_specs=[
            pl.BlockSpec((hid, runs), lambda i: (0, 0)),
            pl.BlockSpec((runs, own), lambda i: (0, first + i)),
            pl.BlockSpec((hid, own), strip),
            ANY,
        ],
        out_specs=pl.BlockSpec((hid, own), strip),
        out_shape=jax.ShapeDtypeStruct((hid, cells), BF16),
        input_output_aliases={3: 0},
        cost_estimate=cost(2 * runs * hid * own * count, (4 * hid + 4 * runs) * own * count),
        name="update",
    )(hidden_t, slope, weight, so_far)


def finish_kernel(total_ref, layer_ref, out_ref):
    n_feat = layer_ref.shape[0]
    line = lax.broadcasted_iota(jnp.int32, (n_feat, LANES), 0)
    for t in range(total_ref.shape[0]):
        at = slice(t * LANES, (t + 1) * LANES)
        rest = jnp.broadcast_to(total_ref[t, n_feat : n_feat + 1, :], (n_feat, LANES))
        grad = total_ref[t, :n_feat, :] + jnp.where(line == n_feat - 1, rest, 0.0)
        out_ref[:, at] = layer_ref[:, at] - 2.0 * grad


def finish(total, layer):
    return pl.pallas_call(
        finish_kernel,
        in_specs=[SPACE, SPACE],
        out_specs=SPACE,
        out_shape=jax.ShapeDtypeStruct(layer.shape, F32),
        cost_estimate=cost(3 * layer.size, 12 * layer.size),
        name="finish",
    )(total, layer)


def bits_of(size):
    return [1 << b for b in range(size.bit_length() - 1)]


def halve(x, axis, bit):
    size = lax.axis_size(axis)
    upper = (lax.axis_index(axis) & bit) != 0
    half = x.shape[0] // 2
    kept = lax.dynamic_slice_in_dim(x, jnp.where(upper, half, 0), half, 0)
    sent = lax.dynamic_slice_in_dim(x, jnp.where(upper, 0, half), half, 0)
    return kept + lax.ppermute(sent, axis, [(i, i ^ bit) for i in range(size)])


def rejoin(x, axis, bit):
    size = lax.axis_size(axis)
    upper = (lax.axis_index(axis) & bit) != 0
    other = lax.ppermute(x, axis, [(i, i ^ bit) for i in range(size)])
    return jnp.where(
        upper, jnp.concatenate([other, x], axis=0), jnp.concatenate([x, other], axis=0)
    )


def sum_over_devices(x):
    grp, tile = lax.axis_size("grp"), lax.axis_size("tile")
    for bit in bits_of(grp):
        x = halve(x, "grp", bit)
    for bit in bits_of(tile):
        x = x + lax.ppermute(x, "tile", [(i, i ^ bit) for i in range(tile)])
    for bit in bits_of(grp)[::-1]:
        x = rejoin(x, "grp", bit)
    return x


def on_device(
    start_field, class_ids, run_levels, steepness, step_pick, input_layer, output_layer, output_bias
):
    _, rows, cols = start_field.shape
    n_grp, n_tile = lax.axis_size("grp"), lax.axis_size("tile")
    tile = lax.axis_index("tile").astype(jnp.int32)[None]
    grp = lax.axis_index("grp").astype(jnp.int32)[None]
    chunks = CHUNKS
    parts = spans(cols, chunks)
    runs_total, classes = run_levels.shape
    n_feat, _ = input_layer.shape

    up = [(i, i + 1) for i in range(n_tile - 1)]
    down = [(j, i) for i, j in up]
    edges = []
    for c in range(chunks):
        top, bottom = pack_edges(c, start_field, class_ids, parts)
        above = lax.ppermute(bottom, "tile", up)
        below = lax.ppermute(top, "tile", down)
        edges.append((in_vmem(above), in_vmem(below)))

    run_rows = jnp.concatenate(
        [
            run_levels.T.astype(F32),
            step_pick[None, :].astype(F32),
            steepness[None, :],
            jnp.zeros((2 * LEVELS - classes - 2, runs_total), F32),
        ],
        axis=0,
    )
    hidden, hidden_t, gain_t, project = hidden_units(run_rows, input_layer)
    bias_row = output_bias[None, :]
    guess = predict(hidden, output_layer, bias_row)
    kept = -(-(n_feat + 1) // SUB) * SUB

    state = None
    scale = 2.0 / runs_total
    for c in range(chunks):
        snaps = diffuse(c, chunks, start_field, edges, class_ids, run_rows, tile, n_tile, grp, n_grp)
        targets = [snaps[0]]
        for offset in range(1, n_grp):
            pairs = [(i, i ^ offset) for i in range(n_grp)]
            targets.append(in_vmem(lax.ppermute(snaps[offset], "grp", pairs)))
        before = state
        state = learn(
            c, chunks, cols, grp, guess, targets, output_layer, bias_row,
            gain_t, project, hidden_t, before, kept, scale,
        )
    misfit, bias_next, partial, slope = state
    output_next, strips = before[3], rows // n_grp
    for part in range(UPDATES):
        first, past = part * strips // UPDATES, (part + 1) * strips // UPDATES
        output_next = update(
            first, past - first, chunks, cols, hidden_t, slope, output_layer, output_next
        )
    total = sum_over_devices(partial.reshape(-1, LANES)).reshape(partial.shape)
    input_next = finish(in_vmem(total), in_vmem(input_layer))
    return misfit, output_next, bias_next.reshape(-1), input_next


def solution(mesh):
    in_specs = (
        P("grp", "tile", None),
        P("tile", None),
        P(),
        P(),
        P(),
        P(),
        P(None, ("grp", "tile")),
        P(("grp", "tile")),
    )
    out_specs = (P(None, ("grp", "tile")), P(None, ("grp", "tile")), P(("grp", "tile")), P())

    return jax.shard_map(on_device, mesh=mesh, in_specs=in_specs, out_specs=out_specs, check_vma=False)
```
